256 devices in a mesh: seq: 64 (over z_lo, x, y), round: 4 (over z_hi, core).
Axes of the slice: x: 4, y: 4, z: 8 (z_hi: 2, z_lo: 4; z = z_hi * 4 + z_lo), core: 2. Of those that a mesh axis runs over, the one named last changes fastest.
Arguments:
- tokens_x: bfloat16 [131072, 1024], P('seq'), may hold values from -208 to 208
- w_qk: bfloat16 [1024, 128], replicated, may hold values from -0.25 to 0.25
- w_v: bfloat16 [1024, 128], replicated, may hold values from -0.1875 to 0.1875
- w_out: bfloat16 [128, 1024], replicated, may hold values from -2 to 2
- send_slot: int32 [8, 131072], P('round', 'seq'), may hold values from 0 to 4095, as said below
- recv_row: int32 [8, 131072], P('round', 'seq'), may hold values from 0 to 4095, as said below
- look_back: int32 [8, 512], P('round', 'seq'), may hold values from 0 to 511, as said below
Outputs:
- mixed: bfloat16 [131072, 1024], P(('seq', 'round'))
The draws below stay inside these ranges and needn't reach their ends.
Inputs may be any that keep to these rules, and one draw needn't show every extreme that they name: `send_slot`: in each round each device of seq gives its 2048 tokens distinct slots; slot // 64 names the receiving device of seq, and a device sends at most 64 tokens to one device, reaching it for some pair in every round; every device of seq receives exactly 2048 tokens a round, in slots 0 to count - 1 of each source. recv_row // 64 is the source device and recv_row % 64 its slot; in each round every received row of a device of seq is taken by exactly one of its sorted positions. look_back[r, c] is c - 1 or c - 2, modulo 512.
All inputs are finite; a program needn't handle non-finite values.
Results may differ from the reference program's by a relative error of at most 0.014.
The reference program's roundings to bfloat16 on the way count: a program that leaves them out, or rounds other values in their place, can miss the bound.
Values may be sent and summed in bfloat16 or wider, within the bound.
No kernel may reach another device: no remote copies, remote signals or barrier semaphores. Data moves between devices by JAX's collectives and lax.ppermute only.
A program may use at most 64 MiB of HBM per device.

```python
import jax
import jax.numpy as jnp
from jax import lax

MODEL_DIM = 1024
HEAD_DIM = 128
BLOCK_LEN = 256
TOK_DEV = 2048
ROUNDS = 8
SEQ_LEN = 131072
CAPACITY = 64
BLOCKS = 512
N_SEQ = 64


def bucket_plan(key):
    base = jax.random.fold_in(key, 11)

    def one_round(round_id):
        round_key = jax.random.fold_in(base, round_id)
        key_order, key_fill, key_dest, key_local, key_recv = jax.random.split(round_key, 5)
        offsets = jax.random.permutation(key_order, N_SEQ)
        fills = jax.random.randint(key_fill, (N_SEQ // 2,), 0, CAPACITY + 1).astype(jnp.int32).at[0].set(CAPACITY)
        per_offset = jnp.zeros((N_SEQ,), jnp.int32).at[offsets[0::2]].set(fills).at[offsets[1::2]].set(CAPACITY - fills)
        ends = jnp.cumsum(per_offset).astype(jnp.int32)
        positions = jnp.arange(TOK_DEV, dtype=jnp.int32)
        offset_of = jnp.searchsorted(ends, positions, side='right').astype(jnp.int32)
        within = positions - (ends[offset_of] - per_offset[offset_of])
        dest_map = jax.random.permutation(key_dest, N_SEQ).astype(jnp.int32)
        sources = jnp.arange(N_SEQ, dtype=jnp.int32)
        destination = dest_map[(sources[:, None] + offset_of[None, :]) % N_SEQ]
        slot_ids = destination * CAPACITY + within[None, :]
        local = jax.vmap(lambda source_id: jax.random.permutation(jax.random.fold_in(key_local, source_id), TOK_DEV))(sources).astype(jnp.int32)
        token_ids = sources[:, None] * TOK_DEV + local
        sent = jnp.zeros((SEQ_LEN,), jnp.int32).at[token_ids.reshape(-1)].set(slot_ids.reshape(-1))
        pair_dest = dest_map[(sources[:, None] + sources[None, :]) % N_SEQ]
        counts = jnp.zeros((N_SEQ, N_SEQ), jnp.int32).at[jnp.broadcast_to(sources[:, None], (N_SEQ, N_SEQ)), pair_dest].set(jnp.broadcast_to(per_offset[None, :], (N_SEQ, N_SEQ)))
        buffer_ids = jnp.arange(N_SEQ * CAPACITY, dtype=jnp.int32)
        live = (buffer_ids % CAPACITY)[None, :] < counts.T[:, buffer_ids // CAPACITY]
        ranked = jnp.argsort(jnp.where(live, 0, 1), axis=1, stable=True)[:, :TOK_DEV].astype(jnp.int32)
        mixing = jax.vmap(lambda dest_id: jax.random.permutation(jax.random.fold_in(key_recv, dest_id), TOK_DEV))(sources).astype(jnp.int32)
        incoming_rows = jnp.take_along_axis(ranked, mixing, axis=1).reshape(-1)
        return (sent, incoming_rows)
    return jax.vmap(one_round)(jnp.arange(ROUNDS, dtype=jnp.int32))


def draw_send_slot(key, part):
    return bucket_plan(key)[0].astype(jnp.int32)


def draw_recv_row(key, part):
    return bucket_plan(key)[1].astype(jnp.int32)


def draw_look_back(key, part):
    steps_back = jax.random.randint(jax.random.fold_in(key, 5), (ROUNDS, BLOCKS), 1, 3).astype(jnp.int32)
    return ((jnp.arange(BLOCKS, dtype=jnp.int32)[None, :] - steps_back) % BLOCKS).astype(jnp.int32)


def draw_tokens_x(key, part):
    key_base = jax.random.fold_in(jax.random.fold_in(key, 3), 0)
    base = jax.random.normal(key_base, (SEQ_LEN, MODEL_DIM), jnp.float32)
    return jnp.clip(base, -6.0, 6.0).astype(jnp.bfloat16)


def normal_values(key, extent, spread, most, kind=jnp.bfloat16):
    array = spread * jax.random.normal(key, extent, jnp.float32)
    return jnp.clip(array, min=-most, max=most).astype(kind)


def setup_inputs(seed: int = 0) -> dict:
    splits = jax.random.split(jax.random.key(seed), 8)
    return {
        "tokens_x": draw_tokens_x(jax.random.fold_in(splits[7], 71), 0),
        "w_qk": normal_values(splits[1], (MODEL_DIM, HEAD_DIM), (MODEL_DIM // 2) ** -0.5, 0.25),
        "w_v": normal_values(splits[2], (MODEL_DIM, HEAD_DIM), MODEL_DIM ** -0.5, 0.1875),
        "w_out": normal_values(splits[3], (HEAD_DIM, MODEL_DIM), (HEAD_DIM // 16) ** -0.5, 2.0),
        "send_slot": draw_send_slot(jax.random.fold_in(splits[7], 71), 0),
        "recv_row": draw_recv_row(jax.random.fold_in(splits[7], 71), 0),
        "look_back": draw_look_back(jax.random.fold_in(splits[7], 71), 0),
    }


masked_score = -1000000000.0

def sorted_order(slots, taken):
    owner = jnp.arange(SEQ_LEN, dtype=jnp.int32) // TOK_DEV
    table = jnp.zeros((N_SEQ, N_SEQ * CAPACITY), jnp.int32).at[owner, slots].set(jnp.arange(SEQ_LEN, dtype=jnp.int32))
    return table[taken // CAPACITY, owner * CAPACITY + taken % CAPACITY]

def attend_blocks(inputs):
    query_rows_in, every_key_row, every_value_row = inputs
    logit_scores = jnp.einsum('jxw,jpw->jxp', query_rows_in.astype(jnp.float32), every_key_row.astype(jnp.float32))
    itself = jnp.arange(BLOCK_LEN)[:, None] == jnp.arange(2 * BLOCK_LEN)[None, :]
    logit_scores = jnp.where(itself, masked_score, logit_scores)
    top = lax.optimization_barrier(jnp.max(logit_scores, axis=-1))
    expon = jnp.exp(logit_scores - top[..., None])
    total = lax.optimization_barrier(jnp.sum(expon, axis=-1))
    softmax_weights = expon.astype(jnp.bfloat16).astype(jnp.float32)
    weighted_value_sum = jnp.einsum('lxt,lto->lxo', softmax_weights, every_value_row.astype(jnp.float32))
    return ((weighted_value_sum / total[..., None]).astype(jnp.bfloat16), top + jnp.log(total))

def reference(tokens_x, w_qk, w_v, w_out, send_slot, recv_row, look_back):
    floats_x = tokens_x.astype(jnp.float32)
    qk = jnp.dot(floats_x, w_qk.astype(jnp.float32), precision=lax.Precision.HIGHEST, preferred_element_type=jnp.float32).astype(jnp.bfloat16)
    values = jnp.dot(floats_x, w_v.astype(jnp.float32), precision=lax.Precision.HIGHEST, preferred_element_type=jnp.float32).astype(jnp.bfloat16)
    qk_float = qk.astype(jnp.float32)
    keys = (qk_float * lax.rsqrt(lax.optimization_barrier(jnp.sum(qk_float * qk_float, axis=-1, keepdims=True)) + 1e-06)).astype(jnp.bfloat16)

    def one_round(carry, inputs):
        slots, taken, looks = inputs
        order = sorted_order(slots, taken)
        query_blocks = qk[order].reshape(BLOCKS, BLOCK_LEN, HEAD_DIM)
        key_blocks = keys[order].reshape(BLOCKS, BLOCK_LEN, HEAD_DIM)
        value_blocks = values[order].reshape(BLOCKS, BLOCK_LEN, HEAD_DIM)
        joined_key_rows = jnp.concatenate([key_blocks, key_blocks[looks]], axis=1)
        value_join = jnp.concatenate([value_blocks, value_blocks[looks]], axis=1)
        groups = BLOCKS // 8
        result, log_total = lax.map(attend_blocks, (query_blocks.reshape(groups, 8, BLOCK_LEN, HEAD_DIM), joined_key_rows.reshape(groups, 8, 2 * BLOCK_LEN, HEAD_DIM), value_join.reshape(groups, 8, 2 * BLOCK_LEN, HEAD_DIM)))
        part = jnp.zeros((SEQ_LEN, HEAD_DIM), jnp.bfloat16).at[order].set(result.reshape(SEQ_LEN, HEAD_DIM))
        lse = jnp.zeros((SEQ_LEN,), jnp.float32).at[order].set(log_total.reshape(SEQ_LEN))
        top_old, total_old, summed_old = carry
        top_new = jnp.maximum(top_old, lse)
        scale_old = jnp.exp(top_old - top_new)
        scale_new = jnp.exp(lse - top_new)
        total_new = total_old * scale_old + scale_new
        summed_new = summed_old * scale_old[:, None] + part.astype(jnp.float32) * scale_new[:, None]
        return ((top_new, total_new, summed_new), None)
    start = (jnp.full((SEQ_LEN,), -jnp.inf, jnp.float32), jnp.zeros((SEQ_LEN,), jnp.float32), jnp.zeros((SEQ_LEN, HEAD_DIM), jnp.float32))
    final, unused = lax.scan(one_round, start, (send_slot, recv_row, look_back))
    blended = (final[2] / final[1][:, None]).astype(jnp.bfloat16)
    return jnp.dot(blended.astype(jnp.float32), w_out.astype(jnp.float32), precision=lax.Precision.HIGHEST, preferred_element_type=jnp.float32).astype(jnp.bfloat16)
```

```python
import functools

import jax
import jax.numpy as jnp
from jax import lax
from jax.experimental import pallas as pl
from jax.experimental.pallas import tpu as pltpu
from jax.sharding import Mesh
from jax.sharding import PartitionSpec as P

BLOCK = 256
MASKED = -1000000000.0
SEQ = ("zl", "x", "y")
ROUND = ("zh", "c")
BF = jnp.bfloat16
F32 = jnp.float32
VMEM_BYTES = 48 * 1024 * 1024


def params(n=1):
    return pltpu.CompilerParams(
        dimension_semantics=("arbitrary",) * n, vmem_limit_bytes=VMEM_BYTES
    )


def whole(shape):
    return pl.BlockSpec(shape, lambda *_: (0,) * len(shape))


def one_hot(a, b):
    return jnp.where(a == b, 1.0, 0.0).astype(BF)


def column(row):
    return jnp.transpose(jnp.broadcast_to(row, (8, row.shape[1])))[:, :1]


def project_kernel(x_ref, wqk_ref, wv_ref, out_ref, w_ref):
    @pl.when(pl.program_id(0) == 0)
    def _():
        w_ref[:, :128] = wqk_ref[...]
        w_ref[:, 128:] = wv_ref[...]

    out_ref[...] = jnp.dot(x_ref[...], w_ref[...], preferred_element_type=F32).astype(BF)


def project(x, w_qk, w_v):
    rows, model = x.shape
    step = 512
    return pl.pallas_call(
        project_kernel,
        grid=(rows // step,),
        in_specs=[
            pl.BlockSpec((step, model), lambda i: (i, 0)),
            whole(w_qk.shape),
            whole(w_v.shape),
        ],
        out_specs=pl.BlockSpec((step, 256), lambda i: (i, 0)),
        out_shape=jax.ShapeDtypeStruct((rows, 256), BF),
        scratch_shapes=[pltpu.VMEM((model, 256), BF)],
        compiler_params=params(),
        name="project",
    )(x, w_qk, w_v)


def scatter_kernel(idx_ref, rows_ref, out_ref):
    n = out_ref.shape[0] * out_ref.shape[1]
    base = pl.program_id(0) * n
    place = lax.broadcasted_iota(jnp.int32, (n, rows_ref.shape[0]), 0)
    hot = one_hot(idx_ref[...] - base, place)
    got = jnp.dot(hot, rows_ref[...], preferred_element_type=F32).astype(BF)
    out_ref[...] = got.reshape(out_ref.shape)


def scatter_rows(idx, rows, peers, cap):
    per = 8
    return pl.pallas_call(
        scatter_kernel,
        grid=(peers // per,),
        in_specs=[whole(idx.shape), whole(rows.shape)],
        out_specs=pl.BlockSpec((per, cap, 256), lambda i: (i, 0, 0)),
        out_shape=jax.ShapeDtypeStruct((peers, cap, 256), BF),
        compiler_params=params(),
        name="scatter_rows",
    )(idx, rows)


def sort_kernel(idx_ref, rows_ref, q_ref, kv_ref):
    n = rows_ref.shape[0]
    col = column(idx_ref[0])
    place = lax.broadcasted_iota(jnp.int32, (BLOCK, n), 1)
    got = jnp.dot(one_hot(col, place), rows_ref[...], preferred_element_type=F32)
    qk = got[:, :128]
    keys = qk * lax.rsqrt(jnp.sum(qk * qk, axis=-1, keepdims=True) + 1e-06)
    q_ref[...] = qk.astype(BF)
    kv_ref[:, :128] = keys.astype(BF)
    kv_ref[:, 128:] = got[:, 128:].astype(BF)


def sort_rows(idx, rows):
    count = idx.shape[-1]
    blocks = count // BLOCK
    return pl.pallas_call(
        sort_kernel,
        grid=(blocks,),
        in_specs=[pl.BlockSpec((1, 1, BLOCK), lambda i: (i, 0, 0)), whole(rows.shape)],
        out_specs=[
            pl.BlockSpec((BLOCK, 128), lambda i: (i, 0)),
            pl.BlockSpec((BLOCK, 256), lambda i: (i, 0)),
        ],
        out_shape=[
            jax.ShapeDtypeStruct((count, 128), BF),
            jax.ShapeDtypeStruct((count, 256), BF),
        ],
        compiler_params=params(),
        name="sort_rows",
    )(idx.reshape(blocks, 1, BLOCK), rows)


def three_terms(v):
    hi = v.astype(BF).astype(F32)
    mid = (v - hi).astype(BF).astype(F32)
    lo = v - hi - mid
    return hi, mid, lo


def term_lanes(v, rows):
    hi, mid, lo = three_terms(v)
    group = lax.broadcasted_iota(jnp.int32, (rows, 128), 1) // 32
    return jnp.where(
        group == 0, hi, jnp.where(group == 1, mid, jnp.where(group == 2, lo, 1.0))
    ).astype(BF)


def attend_kernel(dist_ref, q_ref, kv_ref, halo_ref, out_ref, ext_ref):
    c = pl.program_id(0)

    @pl.when(c == 0)
    def _():
        ext_ref[: 2 * BLOCK] = halo_ref[...]
        ext_ref[2 * BLOCK :] = kv_ref[...]

    own = ext_ref[pl.ds(pl.multiple_of((c + 2) * BLOCK, BLOCK), BLOCK), :]
    behind = ext_ref[pl.ds(pl.multiple_of((c + 2 - dist_ref[c]) * BLOCK, BLOCK), BLOCK), :]
    q = q_ref[...]
    nt = (((1,), (1,)), ((), ()))
    s1 = lax.dot_general(q, own[:, :128], nt, preferred_element_type=F32)
    s2 = lax.dot_general(q, behind[:, :128], nt, preferred_element_type=F32)
    r = lax.broadcasted_iota(jnp.int32, (BLOCK, BLOCK), 0)
    k = lax.broadcasted_iota(jnp.int32, (BLOCK, BLOCK), 1)
    s1 = jnp.where(r == k, MASKED, s1)
    top = jnp.maximum(
        jnp.max(s1, axis=-1, keepdims=True), jnp.max(s2, axis=-1, keepdims=True)
    )
    e1 = jnp.exp(s1 - top)
    e2 = jnp.exp(s2 - top)
    total = jnp.sum(e1, axis=-1, keepdims=True) + jnp.sum(e2, axis=-1, keepdims=True)
    o = jnp.dot(e1.astype(BF), own[:, 128:], preferred_element_type=F32) + jnp.dot(
        e2.astype(BF), behind[:, 128:], preferred_element_type=F32
    )
    out_ref[:, :128] = (o / total).astype(BF)
    out_ref[:, 128:] = term_lanes(top + jnp.log(total), BLOCK)


def attend(dist, q, kv, halo):
    count = q.shape[0]
    return pl.pallas_call(
        attend_kernel,
        grid_spec=pltpu.PrefetchScalarGridSpec(
            num_scalar_prefetch=1,
            grid=(count // BLOCK,),
            in_specs=[
                pl.BlockSpec((BLOCK, 128), lambda i, d: (i, 0)),
                whole(kv.shape),
                whole(halo.shape),
            ],
            out_specs=pl.BlockSpec((BLOCK, 256), lambda i, d: (i, 0)),
            scratch_shapes=[pltpu.VMEM((count + 2 * BLOCK, 256), BF)],
        ),
        out_shape=jax.ShapeDtypeStruct((count, 256), BF),
        compiler_params=params(),
        name="attend",
    )(dist, q, kv, halo)


def back_kernel(idx_ref, res_ref, out_ref):
    per, ext, _ = out_ref.shape
    cap = ext - 8
    n = per * cap
    base = pl.program_id(0) * n
    place = lax.broadcasted_iota(jnp.int32, (n, res_ref.shape[0]), 0)
    hot = one_hot(idx_ref[...] - base, place)
    got = jnp.dot(hot, res_ref[...], preferred_element_type=F32)
    out_ref[:, :cap, :] = got[:, :128].astype(BF).reshape(per, cap, 128)
    terms = got[:, 128:].reshape(per * cap // 32, 32, 128)
    slot = lax.broadcasted_iota(jnp.int32, terms.shape, 1)
    lane = lax.broadcasted_iota(jnp.int32, terms.shape, 2) % 32
    line = jnp.sum(jnp.where(slot == lane, terms, 0.0), axis=1, keepdims=True)
    line = line.reshape(per, cap // 32, 1, 128)
    row = lax.broadcasted_iota(jnp.int32, (per, 8, 128), 1)
    tail = jnp.zeros((per, 8, 128), F32)
    for part in range(cap // 32):
        tail = jnp.where(row == part, line[:, part], tail)
    out_ref[:, cap:, :] = tail.astype(BF)


def back_rows(idx, res, peers, cap):
    per = 8
    return pl.pallas_call(
        back_kernel,
        grid=(peers // per,),
        in_specs=[whole(idx.shape), whole(res.shape)],
        out_specs=pl.BlockSpec((per, cap + 8, 128), lambda i: (i, 0, 0)),
        out_shape=jax.ShapeDtypeStruct((peers, cap + 8, 128), BF),
        compiler_params=params(),
        name="back_rows",
    )(idx, res)


def home_kernel(idx_ref, *refs):
    (*home_refs, out_ref, x_ref) = refs
    peers, ext, _ = home_refs[0].shape
    cap = ext - 8
    n = peers * cap

    @pl.when(pl.program_id(0) == 0)
    def _():
        lane = lax.broadcasted_iota(jnp.int32, (128, 128), 0) // 32
        pick = one_hot(lane, lax.broadcasted_iota(jnp.int32, (128, 128), 1))
        for i, ref in enumerate(home_refs):
            x_ref[i, :, :128] = ref[:, :cap, :].reshape(n, 128)
            tail = ref[:, cap:, :].astype(F32)
            shape = (peers, 32, 128)
            slot = lax.broadcasted_iota(jnp.int32, shape, 1)
            at = lax.broadcasted_iota(jnp.int32, shape, 2) % 32
            spread = [
                jnp.where(slot == at, tail[:, part : part + 1], 0.0)
                for part in range(cap // 32)
            ]
            spread = jnp.concatenate(spread, axis=1).reshape(n, 128).astype(BF)
            x_ref[i, :, 128:] = jnp.dot(spread, pick, preferred_element_type=F32).astype(BF)

    step = out_ref.shape[1]
    place = lax.broadcasted_iota(jnp.int32, (step, n), 1)
    parts, logs = [], []
    for i in range(len(home_refs)):
        hot = one_hot(column(idx_ref[0, i : i + 1]), place)
        got = jnp.dot(hot, x_ref[i], preferred_element_type=F32)
        parts.append(got[:, :128])
        logs.append(got[:, 128:129] + got[:, 129:130] + got[:, 130:131])
    top = functools.reduce(jnp.maximum, logs)
    scales = [jnp.exp(v - top) for v in logs]
    total = sum(scales)
    summed = sum(s * p for s, p in zip(scales, parts))
    out_ref[0, :, :128] = summed
    lane = lax.broadcasted_iota(jnp.int32, (step, 128), 1)
    out_ref[0, :, 128:] = jnp.where(lane < 64, top, total)


def home_rows(idx, homes):
    rounds, count = idx.shape
    step = BLOCK
    steps = count // step
    quarters = 4
    per = steps // quarters
    peers, ext, _ = homes[0].shape
    n = peers * (ext - 8)
    return pl.pallas_call(
        home_kernel,
        grid=(steps,),
        in_specs=[pl.BlockSpec((1, rounds, step), lambda i: (i, 0, 0))]
        + [whole(h.shape) for h in homes],
        out_specs=pl.BlockSpec((1, step, 256), lambda i: (i // per, i % per, 0)),
        out_shape=jax.ShapeDtypeStruct((quarters, count // quarters, 256), F32),
        scratch_shapes=[pltpu.VMEM((rounds, n, 256), BF)],
        compiler_params=params(),
        name="home_rows",
    )(idx.reshape(rounds, steps, step).transpose(1, 0, 2), *homes)


def finish_kernel(m_ref, w_ref, out_ref):
    tops = [m_ref[i, :, 128:129] for i in range(4)]
    totals = [m_ref[i, :, 192:193] for i in range(4)]
    top = functools.reduce(jnp.maximum, tops)
    scales = [jnp.exp(t - top) for t in tops]
    total = sum(s * t for s, t in zip(scales, totals))
    summed = sum(s * m_ref[i, :, :128] for i, s in enumerate(scales))
    blended = (summed / total).astype(BF)
    out_ref[...] = jnp.dot(blended, w_ref[...], preferred_element_type=F32).astype(BF)


def finish(merged, w_out):
    parts, rows, wide = merged.shape
    step = 256
    return pl.pallas_call(
        finish_kernel,
        grid=(rows // step,),
        in_specs=[pl.BlockSpec((parts, step, wide), lambda i: (0, i, 0)), whole(w_out.shape)],
        out_specs=pl.BlockSpec((step, w_out.shape[1]), lambda i: (i, 0)),
        out_shape=jax.ShapeDtypeStruct((rows, w_out.shape[1]), BF),
        compiler_params=params(),
        name="finish",
    )(merged, w_out)


def body(x, w_qk, w_v, w_out, slots, taken, looks):
    rounds, count = slots.shape
    peers = lax.axis_size(SEQ)
    cap = 2 * count // peers
    blocks = count // BLOCK
    packed = project(x, w_qk, w_v)
    mine = lax.axis_index(SEQ) * blocks + jnp.arange(blocks, dtype=jnp.int32)
    dist = (mine[None, :] - looks) % (peers * blocks)
    ring = [(i, (i + 1) % peers) for i in range(peers)]
    arrived = []
    for i in range(rounds):
        out = scatter_rows(slots[i : i + 1], packed, peers, cap)
        arrived.append(lax.all_to_all(out, SEQ, 0, 0, tiled=True))
    homes = []
    for i in range(rounds):
        q, kv = sort_rows(taken[i], arrived[i].reshape(peers * cap, 256))
        halo = lax.ppermute(kv[count - 2 * BLOCK :], SEQ, ring)
        res = attend(dist[i], q, kv, halo)
        back = back_rows(taken[i : i + 1], res, peers, cap)
        homes.append(lax.all_to_all(back, SEQ, 0, 0, tiled=True))
    state = home_rows(slots, homes)
    merged = lax.all_to_all(state, ROUND, 0, 0, tiled=True)
    return finish(merged, w_out)


def solution(mesh):
    fine = Mesh(mesh.devices.reshape(4, 4, 4, 2, 2), SEQ + ROUND)
    in_specs = (P(SEQ, None), P(), P(), P()) + (P(ROUND, SEQ),) * 3
    return jax.shard_map(
        body, mesh=fine, in_specs=in_specs, out_specs=P(SEQ + ROUND, None), check_vma=False
    )
```

```python
import functools

import jax
import jax.numpy as jnp
from jax import lax
from jax.experimental import pallas as pl
from jax.experimental.pallas import tpu as pltpu
from jax.sharding import Mesh
from jax.sharding import PartitionSpec as P

BLOCK = 256
SHIFTS = (0, 1, -1, 2, -2)
MASKED = -1000000000.0
SEQ = ("zl", "x", "y")
PLANE = ("x", "y")
ROUND = ("zh", "c")
BF = jnp.bfloat16
F32 = jnp.float32
VMEM_BYTES = 48 * 1024 * 1024


def params(n=1):
    return pltpu.CompilerParams(
        dimension_semantics=("arbitrary",) * n, vmem_limit_bytes=VMEM_BYTES
    )


def whole(shape):
    return pl.BlockSpec(shape, lambda *_: (0,) * len(shape))


def one_hot(a, b):
    return jnp.where(a == b, 1.0, 0.0).astype(BF)


def column(row):
    return jnp.transpose(jnp.broadcast_to(row, (8, row.shape[1])))[:, :1]


def project_kernel(x_ref, wqk_ref, wv_ref, out_ref, w_ref):
    @pl.when(pl.program_id(0) == 0)
    def _():
        w_ref[:, :128] = wqk_ref[...]
        w_ref[:, 128:] = wv_ref[...]

    out_ref[...] = jnp.dot(x_ref[...], w_ref[...], preferred_element_type=F32).astype(BF)


def project(x, w_qk, w_v):
    rows, model = x.shape
    step = 512
    return pl.pallas_call(
        project_kernel,
        grid=(rows // step,),
        in_specs=[
            pl.BlockSpec((step, model), lambda i: (i, 0)),
            whole(w_qk.shape),
            whole(w_v.shape),
        ],
        out_specs=pl.BlockSpec((step, 256), lambda i: (i, 0)),
        out_shape=jax.ShapeDtypeStruct((rows, 256), BF),
        scratch_shapes=[pltpu.VMEM((model, 256), BF)],
        compiler_params=params(),
        name="project",
    )(x, w_qk, w_v)


def ring(value, shift):
    def at(z):
        return (z % 4) * 2 + z // 4

    route = [(at(z), at((z + shift) % 8)) for z in range(8)]
    return lax.ppermute(value, ("zl", "zh"), route)


def ring_all(pieces, sign):
    return [pieces[0]] + [ring(p, sign * k) for p, k in zip(pieces[1:], SHIFTS[1:])]


def ring_first(split, sign):
    a, b, c, d, e = ring_all(split, sign)
    joint = jnp.stack([a, b, c, jnp.concatenate([d, e])], axis=1)
    return lax.all_to_all(joint, PLANE, 0, 0, tiled=True)


def plane_first(joint, sign):
    joint = lax.all_to_all(joint, PLANE, 0, 0, tiled=True)
    split = [joint[:, 0], joint[:, 1], joint[:, 2], joint[:8, 3], joint[8:, 3]]
    return ring_all(split, sign)


def emit_specs(split, width, lanes):
    if not split:
        return (
            [pl.BlockSpec((8, 1, width, lanes), lambda i: (i % 2, i // 2, 0, 0))],
            [jax.ShapeDtypeStruct((16, 4, width, lanes), BF)],
        )

    def spec(first):
        return pl.BlockSpec((8, width, lanes), lambda i: (jnp.clip(i - first, 0, 1), 0, 0))

    big = jax.ShapeDtypeStruct((16, width, lanes), BF)
    small = jax.ShapeDtypeStruct((8, width, lanes), BF)
    return [spec(0), spec(2), spec(4)] + [whole(small.shape)] * 2, [big] * 3 + [small] * 2


def emit(refs, store):
    if len(refs) == 1:
        store(refs[0].at[:, 0])
        return
    step = pl.program_id(0)
    for ref, (first, last) in zip(refs, ((0, 1), (2, 3), (4, 5), (6, 6), (7, 7))):

        @pl.when((step >= first) & (step <= last))
        def _(ref=ref):
            store(ref)


def scatter_kernel(width, idx_ref, rows_ref, *out_refs):
    n = 8 * width
    step = pl.program_id(0)
    line = idx_ref[pl.ds(jnp.where(step == 7, 4, step // 2), 1), :]
    place = lax.broadcasted_iota(jnp.int32, (n, rows_ref.shape[0]), 0)
    hot = one_hot(line - (step % 2) * n, place)
    got = jnp.dot(hot, rows_ref[...], preferred_element_type=F32).astype(BF)

    def store(ref):
        ref[...] = got.reshape(8, width, 256)

    emit(out_refs, store)


def scatter_rows(idx, rows, width, split):
    specs, shapes = emit_specs(split, width, 256)
    return pl.pallas_call(
        functools.partial(scatter_kernel, width),
        grid=(8,),
        in_specs=[whole(idx.shape), whole(rows.shape)],
        out_specs=specs,
        out_shape=shapes,
        compiler_params=params(),
        name="scatter_rows",
    )(idx, rows)


def sort_kernel(idx_ref, *refs):
    (*row_refs, q_ref, kv_ref) = refs
    col = column(idx_ref[0])
    got, base = 0.0, 0
    for ref in row_refs:
        rows = ref[...].reshape(-1, 256)
        n = rows.shape[0]
        place = lax.broadcasted_iota(jnp.int32, (BLOCK, n), 1) + base
        got += jnp.dot(one_hot(col, place), rows, preferred_element_type=F32)
        base += n
    qk = got[:, :128]
    keys = qk * lax.rsqrt(jnp.sum(qk * qk, axis=-1, keepdims=True) + 1e-06)
    q_ref[...] = qk.astype(BF)
    kv_ref[:, :128] = keys.astype(BF)
    kv_ref[:, 128:] = got[:, 128:].astype(BF)


def sort_rows(idx, rows):
    count = idx.shape[-1]
    blocks = count // BLOCK
    return pl.pallas_call(
        sort_kernel,
        grid=(blocks,),
        in_specs=[pl.BlockSpec((1, 1, BLOCK), lambda i: (i, 0, 0))]
        + [whole(r.shape) for r in rows],
        out_specs=[
            pl.BlockSpec((BLOCK, 128), lambda i: (i, 0)),
            pl.BlockSpec((BLOCK, 256), lambda i: (i, 0)),
        ],
        out_shape=[
            jax.ShapeDtypeStruct((count, 128), BF),
            jax.ShapeDtypeStruct((count, 256), BF),
        ],
        compiler_params=params(),
        name="sort_rows",
    )(idx.reshape(blocks, 1, BLOCK), *rows)


def terms_to_lines(terms, groups):
    terms = terms.reshape(groups, 32, 128)
    slot = lax.broadcasted_iota(jnp.int32, terms.shape, 1)
    lane = lax.broadcasted_iota(jnp.int32, terms.shape, 2) % 32
    return jnp.sum(jnp.where(slot == lane, terms, 0.0), axis=1, keepdims=True)


def lines_to_terms(line):
    n = line.shape[0]
    shape = (n, 32, 128)
    slot = lax.broadcasted_iota(jnp.int32, shape, 1)
    lane = lax.broadcasted_iota(jnp.int32, shape, 2) % 32
    spread = jnp.where(slot == lane, line, 0.0).reshape(n * 32, 128).astype(BF)
    group = lax.broadcasted_iota(jnp.int32, (128, 128), 0) // 32
    pick = one_hot(group, lax.broadcasted_iota(jnp.int32, (128, 128), 1))
    return jnp.dot(spread, pick, preferred_element_type=F32)


def three_terms(v):
    hi = v.astype(BF).astype(F32)
    mid = (v - hi).astype(BF).astype(F32)
    lo = v - hi - mid
    return hi, mid, lo


def term_lanes(v, rows):
    hi, mid, lo = three_terms(v)
    group = lax.broadcasted_iota(jnp.int32, (rows, 128), 1) // 32
    return jnp.where(
        group == 0, hi, jnp.where(group == 1, mid, jnp.where(group == 2, lo, 1.0))
    ).astype(BF)


def attend_block(q, own, behind, out_ref):
    nt = (((1,), (1,)), ((), ()))
    s1 = lax.dot_general(q, own[:, :128], nt, preferred_element_type=F32)
    s2 = lax.dot_general(q, behind[:, :128], nt, preferred_element_type=F32)
    r = lax.broadcasted_iota(jnp.int32, (BLOCK, BLOCK), 0)
    k = lax.broadcasted_iota(jnp.int32, (BLOCK, BLOCK), 1)
    s1 = jnp.where(r == k, MASKED, s1)
    top = jnp.maximum(
        jnp.max(s1, axis=-1, keepdims=True), jnp.max(s2, axis=-1, keepdims=True)
    )
    e1 = jnp.exp(s1 - top)
    e2 = jnp.exp(s2 - top)
    total = jnp.sum(e1, axis=-1, keepdims=True) + jnp.sum(e2, axis=-1, keepdims=True)
    o = jnp.dot(e1.astype(BF), own[:, 128:], preferred_element_type=F32) + jnp.dot(
        e2.astype(BF), behind[:, 128:], preferred_element_type=F32
    )
    out_ref[:, :128] = (o / total).astype(BF)
    out_ref[:, 128:] = term_lanes(top + jnp.log(total), BLOCK)


def inner_kernel(dist_ref, q_ref, kv_ref, out_ref):
    c = pl.program_id(0) + 2
    own = kv_ref[pl.ds(pl.multiple_of(c * BLOCK, BLOCK), BLOCK), :]
    behind = kv_ref[pl.ds(pl.multiple_of((c - dist_ref[c]) * BLOCK, BLOCK), BLOCK), :]
    attend_block(q_ref[...], own, behind, out_ref)


def edge_kernel(dist_ref, q_ref, kv_ref, halo_ref, out_ref):
    c = pl.program_id(0)
    own = kv_ref[pl.ds(pl.multiple_of(c * BLOCK, BLOCK), BLOCK), :]
    at = c + 2 - dist_ref[c]
    before = halo_ref[pl.ds(pl.multiple_of(jnp.minimum(at, 1) * BLOCK, BLOCK), BLOCK), :]
    behind = jnp.where(at < 2, before, kv_ref[:BLOCK, :])
    attend_block(q_ref[...], own, behind, out_ref)


def attend_inner(dist, q, kv):
    blocks = q.shape[0] // BLOCK - 2
    return pl.pallas_call(
        inner_kernel,
        grid_spec=pltpu.PrefetchScalarGridSpec(
            num_scalar_prefetch=1,
            grid=(blocks,),
            in_specs=[pl.BlockSpec((BLOCK, 128), lambda i, d: (i + 2, 0)), whole(kv.shape)],
            out_specs=pl.BlockSpec((BLOCK, 256), lambda i, d: (i, 0)),
        ),
        out_shape=jax.ShapeDtypeStruct((blocks * BLOCK, 256), BF),
        compiler_params=params(),
        name="attend_inner",
    )(dist, q, kv)


def attend_edge(dist, q, kv, halo):
    return pl.pallas_call(
        edge_kernel,
        grid_spec=pltpu.PrefetchScalarGridSpec(
            num_scalar_prefetch=1,
            grid=(2,),
            in_specs=[
                pl.BlockSpec((BLOCK, 128), lambda i, d: (i, 0)),
                whole((2 * BLOCK, 256)),
                whole(halo.shape),
            ],
            out_specs=pl.BlockSpec((BLOCK, 256), lambda i, d: (i, 0)),
        ),
        out_shape=jax.ShapeDtypeStruct((2 * BLOCK, 256), BF),
        compiler_params=params(),
        name="attend_edge",
    )(dist, q, kv, halo)


def back_kernel(width, idx_ref, *refs):
    edge_ref, inner_ref, *out_refs = refs
    n = 8 * width
    base = pl.program_id(0) * n
    idx = idx_ref[...] - base
    got = 0.0
    first = 0
    for ref in (edge_ref, inner_ref):
        count = ref.shape[0]
        place = lax.broadcasted_iota(jnp.int32, (n, count), 0)
        hot = one_hot(idx[:, first : first + count], place)
        got += jnp.dot(hot, ref[...], preferred_element_type=F32)
        first += count
    lines = terms_to_lines(got[:, 128:], n // 32).reshape(8, width // 32, 1, 128)
    row = lax.broadcasted_iota(jnp.int32, (8, 8, 128), 1)
    tail = jnp.zeros((8, 8, 128), F32)
    for part in range(width // 32):
        tail = jnp.where(row == part, lines[:, part], tail)

    def store(ref):
        ref[:, :width, :] = got[:, :128].astype(BF).reshape(8, width, 128)
        ref[:, width:, :] = tail.astype(BF)

    emit(out_refs, store)


def back_rows(idx, edge, inner, width, split):
    specs, shapes = emit_specs(split, width + 8, 128)
    return pl.pallas_call(
        functools.partial(back_kernel, width),
        grid=(8,),
        in_specs=[whole(idx.shape), whole(edge.shape), whole(inner.shape)],
        out_specs=specs,
        out_shape=shapes,
        compiler_params=params(),
        name="back_rows",
    )(idx, edge, inner)


ABSENT = -1e30


def home_kernel(width, splits, own_ref, idx_ref, *refs):
    (*home_refs, out_ref, x_ref) = refs
    jobs = len(splits)
    big, small = 16 * width, 8 * width
    sizes = (big, big, big, small, small)

    @pl.when(pl.program_id(0) == 0)
    def _():
        at = 0
        for job in range(jobs):
            if splits[job]:
                blocks = [home_refs[at + g] for g in range(5)]
                at += 5
            else:
                ref = home_refs[at]
                blocks = [ref.at[:, g] for g in range(3)] + [ref.at[:8, 3], ref.at[8:, 3]]
                at += 1
            row = 0
            for size, block in zip(sizes, blocks):
                x_ref[job, row : row + size, :128] = block[:, :width, :].reshape(size, 128)
                tail = block[:, width:, :].astype(F32)
                lines = jnp.concatenate(
                    [tail[:, p : p + 1][:, None] for p in range(width // 32)], axis=1
                ).reshape(size // 32, 1, 128)
                x_ref[job, row : row + size, 128:] = lines_to_terms(lines).astype(BF)
                row += size

    step = out_ref.shape[1] - out_ref.shape[1] // 33
    cols = jnp.transpose(idx_ref[0])
    states = {}
    for job in range(jobs):
        row = 0
        for g, size in enumerate(sizes):
            c = job * 5 + g
            first = small if g == 4 else 0
            place = lax.broadcasted_iota(jnp.int32, (step, size), 1) + first
            hot = one_hot(cols[:, c : c + 1], place)
            got = jnp.dot(hot, x_ref[job, row : row + size], preferred_element_type=F32)
            row += size
            key = ROUND_OF[job]
            if g == 0:
                states[key, 0] = states.get((key, 0), 0.0) + got
            else:
                mine = own_ref[c] == 1
                states[key, 0] = states[key, 0] + jnp.where(mine, got, 0.0)
                states[key, 1] = states.get((key, 1), 0.0) + jnp.where(mine, 0.0, got)
    states = list(states.values())
    here = [s[:, 131:132] > 0.5 for s in states]
    logs = [
        jnp.where(h, s[:, 128:129] + s[:, 129:130] + s[:, 130:131], ABSENT)
        for h, s in zip(here, states)
    ]
    top = functools.reduce(jnp.maximum, logs)
    scales = [jnp.where(h, jnp.exp(v - top), 0.0) for h, v in zip(here, logs)]
    total = sum(scales)
    some = total > 0.0
    summed = sum(s * p[:, :128] for s, p in zip(scales, states))
    safe = jnp.where(some, total, 1.0)
    log = jnp.where(some, top + jnp.log(safe), ABSENT)
    out_ref[0, :step, :] = (summed / safe).astype(BF)
    terms = term_lanes(log, step).astype(F32)
    out_ref[0, step:, :] = terms_to_lines(terms, step // 32).reshape(step // 32, 128).astype(BF)


def home_rows(own, idx, homes, width, splits):
    columns, count = idx.shape
    quarters = 4
    step = count // quarters
    flat = [h for home in homes for h in home]
    return pl.pallas_call(
        functools.partial(home_kernel, width, splits),
        grid_spec=pltpu.PrefetchScalarGridSpec(
            num_scalar_prefetch=1,
            grid=(quarters,),
            in_specs=[pl.BlockSpec((1, columns, step), lambda i, o: (i, 0, 0))]
            + [whole(h.shape) for h in flat],
            out_specs=pl.BlockSpec((1, step + step // 32, 128), lambda i, o: (i, 0, 0)),
            scratch_shapes=[pltpu.VMEM((len(homes), 64 * width, 256), BF)],
        ),
        out_shape=jax.ShapeDtypeStruct((quarters, step + step // 32, 128), BF),
        compiler_params=params(),
        name="home_rows",
    )(own, idx.reshape(columns, quarters, step).transpose(1, 0, 2), *flat)


def finish_kernel(m_ref, w_ref, out_ref):
    rows = out_ref.shape[0]
    logs = []
    for i in range(4):
        line = m_ref[i, rows:, :].astype(F32).reshape(rows // 32, 1, 128)
        terms = lines_to_terms(line)
        logs.append(terms[:, 0:1] + terms[:, 1:2] + terms[:, 2:3])
    top = functools.reduce(jnp.maximum, logs)
    scales = [jnp.exp(v - top) for v in logs]
    total = sum(scales)
    summed = sum(s * m_ref[i, :rows, :].astype(F32) for i, s in enumerate(scales))
    blended = (summed / total).astype(BF)
    out_ref[...] = jnp.dot(blended, w_ref[...], preferred_element_type=F32).astype(BF)


def finish(merged, w_out):
    parts, rows, _ = merged.shape
    rows -= rows // 33
    return pl.pallas_call(
        finish_kernel,
        in_specs=[whole(merged.shape), whole(w_out.shape)],
        out_specs=whole((rows, w_out.shape[1])),
        grid=(1,),
        out_shape=jax.ShapeDtypeStruct((rows, w_out.shape[1]), BF),
        compiler_params=params(),
        name="finish",
    )(merged, w_out)


def send_places(own_slots, other_slots, low, width, by_target):
    zl, zh = lax.axis_index("zl"), lax.axis_index("zh")
    late = lax.axis_index(PLANE) >= 8
    places, mine = [], []
    for g, shift in enumerate(SHIFTS):
        if by_target or g < 3:
            k = shift
        else:
            k = jnp.where(late, -2, 2)
        own = ((zh * 4 + zl + k + 8) & 7) // 4 == zh
        slot = jnp.where(own, own_slots, other_slots)
        place = (slot >> 6) & 15
        at = slot & 63
        hit = ((slot >> 10) == ((zl + k + 8) & 3)) & (at >= low) & (at < low + width)
        if g == 3:
            hit &= place < 8
        if g == 4:
            hit &= place >= 8
        places.append(jnp.where(hit, place * width + at - low, -1))
        mine.append(own)
    return jnp.stack(places), jnp.stack(mine).astype(jnp.int32)


def take_places(taken, low, width):
    zl = lax.axis_index("zl")
    away = (zl - (taken >> 10)) & 3
    group = jnp.where(away < 2, away, 5 - away)
    source = (taken >> 6) & 15
    at = taken & 63
    hit = (at >= low) & (at < low + width)
    by_group = jnp.where(hit, (group * 16 + source) * width + at - low, -1)
    by_source = jnp.where(hit, (source * 4 + group) * width + at - low, -1)
    return by_group, by_source


WIDTH = 64
JOBS = ((0, 0, True), (1, 0, False))
ROUND_OF = tuple(job[0] for job in JOBS)


def body(x, w_qk, w_v, w_out, slots, taken, looks):
    rounds, count = slots.shape
    peers = lax.axis_size(SEQ)
    blocks = count // BLOCK
    others = lax.ppermute(slots, "zh", [(0, 1), (1, 0)])
    packed = project(x, w_qk, w_v)
    mine = lax.axis_index(SEQ) * blocks + jnp.arange(blocks, dtype=jnp.int32)
    dist = (mine[None, :] - looks) % (peers * blocks)
    next_device = [(i, (i + 1) % peers) for i in range(peers)]
    sent, own, arrived = [], [], []
    for i, low, z_first in JOBS:
        places, flags = send_places(slots[i], others[i], low, WIDTH, z_first)
        sent.append(places)
        own.append(flags)
        out = scatter_rows(places, packed, WIDTH, z_first)
        if z_first:
            arrived.append([ring_first(out, 1)])
        else:
            arrived.append(plane_first(out[0], 1))
    homes = [None] * len(JOBS)
    for i in range(rounds):
        rows, spots, base = [], 0, 0
        back_spots = {}
        for job, (which, low, z_first) in enumerate(JOBS):
            if which != i:
                continue
            by_group, by_source = take_places(taken[i], low, WIDTH)
            back_spots[job] = by_group
            spot = by_source if z_first else by_group
            spots = jnp.where(spot >= 0, spot + base, spots)
            base += 64 * WIDTH
            rows += arrived[job]
        q, kv = sort_rows(spots, rows)
        halo = lax.ppermute(kv[count - 2 * BLOCK :], SEQ, next_device)
        inner = attend_inner(dist[i], q, kv)
        edge = attend_edge(dist[i], q, kv, halo)
        for job, spot in back_spots.items():
            z_first = JOBS[job][2]
            back = back_rows(spot[None], edge, inner, WIDTH, not z_first)
            if z_first:
                homes[job] = plane_first(back[0], -1)
            else:
                homes[job] = [ring_first(back, -1)]
    splits = tuple(z_first for _, _, z_first in JOBS)
    state = home_rows(jnp.concatenate(own), jnp.concatenate(sent), homes, WIDTH, splits)
    merged = lax.all_to_all(state, ROUND, 0, 0, tiled=True)
    return finish(merged, w_out)


def solution(mesh):
    fine = Mesh(mesh.devices.reshape(4, 4, 4, 2, 2), SEQ + ROUND)
    in_specs = (P(SEQ, None), P(), P(), P()) + (P(ROUND, SEQ),) * 3
    return jax.shard_map(
        body, mesh=fine, in_specs=in_specs, out_specs=P(SEQ + ROUND, None), check_vma=False
    )
```

```python
import functools

import jax
import jax.numpy as jnp
from jax import lax
from jax.experimental import pallas as pl
from jax.experimental.pallas import tpu as pltpu
from jax.sharding import Mesh
from jax.sharding import PartitionSpec as P

BLOCK = 256
SHIFTS = (0, 1, -1, 2, -2)
MASKED = -1000000000.0
SEQ = ("zl", "x", "y")
PLANE = ("x", "y")
ROUND = ("zh", "c")
BF = jnp.bfloat16
F32 = jnp.float32
VMEM_BYTES = 48 * 1024 * 1024


def params(n=1):
    return pltpu.CompilerParams(
        dimension_semantics=("arbitrary",) * n, vmem_limit_bytes=VMEM_BYTES
    )


def whole(shape):
    return pl.BlockSpec(shape, lambda *_: (0,) * len(shape))


def one_hot(a, b):
    return jnp.where(a == b, 1.0, 0.0).astype(BF)


def column(row):
    return jnp.transpose(jnp.broadcast_to(row, (8, row.shape[1])))[:, :1]


def project_kernel(x_ref, wqk_ref, wv_ref, out_ref, w_ref):
    @pl.when(pl.program_id(0) == 0)
    def _():
        w_ref[:, :128] = wqk_ref[...]
        w_ref[:, 128:] = wv_ref[...]

    out_ref[...] = jnp.dot(x_ref[...], w_ref[...], preferred_element_type=F32).astype(BF)


def project(x, w_qk, w_v):
    rows, model = x.shape
    step = 512
    return pl.pallas_call(
        project_kernel,
        grid=(rows // step,),
        in_specs=[
            pl.BlockSpec((step, model), lambda i: (i, 0)),
            whole(w_qk.shape),
            whole(w_v.shape),
        ],
        out_specs=pl.BlockSpec((step, 256), lambda i: (i, 0)),
        out_shape=jax.ShapeDtypeStruct((rows, 256), BF),
        scratch_shapes=[pltpu.VMEM((model, 256), BF)],
        compiler_params=params(),
        name="project",
    )(x, w_qk, w_v)


def ring(value, shift):
    def at(z):
        return (z % 4) * 2 + z // 4

    route = [(at(z), at((z + shift) % 8)) for z in range(8)]
    return lax.ppermute(value, ("zl", "zh"), route)


def ring_all(pieces, sign):
    return [pieces[0]] + [ring(p, sign * k) for p, k in zip(pieces[1:], SHIFTS[1:])]


def join(split):
    a, b, c, d, e = split
    return jnp.stack([a, b, c, jnp.concatenate([d, e])], axis=1)


def part(joint):
    return [joint[:, 0], joint[:, 1], joint[:, 2], joint[:8, 3], joint[8:, 3]]


def plane(joint):
    return lax.all_to_all(joint, PLANE, 0, 0, tiled=True)


together = lax.optimization_barrier


def emit_specs(split, width, lanes):
    if not split:
        return (
            [pl.BlockSpec((16, 1, width, lanes), lambda i: (0, i, 0, 0))],
            [jax.ShapeDtypeStruct((16, 4, width, lanes), BF)],
        )
    shapes = [(16, width, lanes)] * 3 + [(8, width, lanes)] * 2
    return [whole(v) for v in shapes], [jax.ShapeDtypeStruct(v, BF) for v in shapes]


def emit(refs, store):
    if len(refs) == 1:
        for half in range(2):
            store(refs[0].at[8 * half : 8 * half + 8, 0], half)
        return
    for group in range(4):

        @pl.when(pl.program_id(0) == group)
        def _(group=group):
            for half in range(2):
                if group < 3:
                    store(refs[group].at[8 * half : 8 * half + 8], half)
                else:
                    store(refs[3 + half], half)


def scatter_kernel(width, idx_ref, rows_ref, *out_refs):
    n = 8 * width
    group = pl.program_id(0)
    place = lax.broadcasted_iota(jnp.int32, (n, rows_ref.shape[0]), 0)
    halves = []
    for half in range(2):
        line = idx_ref[pl.ds(jnp.where(group == 3, 3 + half, group), 1), :]
        hot = one_hot(line - half * n, place)
        got = jnp.dot(hot, rows_ref[...], preferred_element_type=F32).astype(BF)
        halves.append(got.reshape(8, width, 256))

    def store(ref, half):
        ref[...] = halves[half]

    emit(out_refs, store)


def scatter_rows(idx, rows, width, split):
    specs, shapes = emit_specs(split, width, 256)
    return pl.pallas_call(
        functools.partial(scatter_kernel, width),
        grid=(4,),
        in_specs=[whole(idx.shape), whole(rows.shape)],
        out_specs=specs,
        out_shape=shapes,
        compiler_params=params(),
        name="scatter_rows",
    )(idx, rows)


def sort_kernel(idx_ref, *refs):
    (*row_refs, q_ref, kv_ref) = refs
    col = column(idx_ref[0])
    got, base = 0.0, 0
    for ref in row_refs:
        rows = ref[...].reshape(-1, 256)
        n = rows.shape[0]
        place = lax.broadcasted_iota(jnp.int32, (q_ref.shape[0], n), 1) + base
        got += jnp.dot(one_hot(col, place), rows, preferred_element_type=F32)
        base += n
    qk = got[:, :128]
    keys = qk * lax.rsqrt(jnp.sum(qk * qk, axis=-1, keepdims=True) + 1e-06)
    q_ref[...] = qk.astype(BF)
    kv_ref[:, :128] = keys.astype(BF)
    kv_ref[:, 128:] = got[:, 128:].astype(BF)


def sort_rows(idx, rows, step):
    count = idx.shape[-1]
    blocks = count // step
    return pl.pallas_call(
        sort_kernel,
        grid=(blocks,),
        in_specs=[pl.BlockSpec((1, 1, step), lambda i: (i, 0, 0))]
        + [whole(r.shape) for r in rows],
        out_specs=[
            pl.BlockSpec((step, 128), lambda i: (i, 0)),
            pl.BlockSpec((step, 256), lambda i: (i, 0)),
        ],
        out_shape=[
            jax.ShapeDtypeStruct((count, 128), BF),
            jax.ShapeDtypeStruct((count, 256), BF),
        ],
        compiler_params=params(),
        name="sort_rows",
    )(idx.reshape(blocks, 1, step), *rows)


def terms_to_lines(terms, groups):
    terms = terms.reshape(groups, 32, 128)
    slot = lax.broadcasted_iota(jnp.int32, terms.shape, 1)
    lane = lax.broadcasted_iota(jnp.int32, terms.shape, 2) % 32
    return jnp.sum(jnp.where(slot == lane, terms, 0.0), axis=1, keepdims=True)


def lines_to_terms(line):
    n = line.shape[0]
    shape = (n, 32, 128)
    slot = lax.broadcasted_iota(jnp.int32, shape, 1)
    lane = lax.broadcasted_iota(jnp.int32, shape, 2) % 32
    spread = jnp.where(slot == lane, line, 0.0).reshape(n * 32, 128).astype(BF)
    group = lax.broadcasted_iota(jnp.int32, (128, 128), 0) // 32
    pick = one_hot(group, lax.broadcasted_iota(jnp.int32, (128, 128), 1))
    return jnp.dot(spread, pick, preferred_element_type=F32)


def three_terms(v):
    hi = v.astype(BF).astype(F32)
    mid = (v - hi).astype(BF).astype(F32)
    lo = v - hi - mid
    return hi, mid, lo


def term_lanes(v, rows):
    hi, mid, lo = three_terms(v)
    group = lax.broadcasted_iota(jnp.int32, (rows, 128), 1) // 32
    return jnp.where(
        group == 0, hi, jnp.where(group == 1, mid, jnp.where(group == 2, lo, 1.0))
    ).astype(BF)


def attend_block(q, own, behind, out_ref):
    nt = (((1,), (1,)), ((), ()))
    s1 = lax.dot_general(q, own[:, :128], nt, preferred_element_type=F32)
    s2 = lax.dot_general(q, behind[:, :128], nt, preferred_element_type=F32)
    r = lax.broadcasted_iota(jnp.int32, (BLOCK, BLOCK), 0)
    k = lax.broadcasted_iota(jnp.int32, (BLOCK, BLOCK), 1)
    s1 = jnp.where(r == k, MASKED, s1)
    top = jnp.maximum(
        jnp.max(s1, axis=-1, keepdims=True), jnp.max(s2, axis=-1, keepdims=True)
    )
    e1 = jnp.exp(s1 - top)
    e2 = jnp.exp(s2 - top)
    total = jnp.sum(e1, axis=-1, keepdims=True) + jnp.sum(e2, axis=-1, keepdims=True)
    o = jnp.dot(e1.astype(BF), own[:, 128:], preferred_element_type=F32) + jnp.dot(
        e2.astype(BF), behind[:, 128:], preferred_element_type=F32
    )
    out_ref[:, :128] = (o / total).astype(BF)
    out_ref[:, 128:] = term_lanes(top + jnp.log(total), BLOCK)


def inner_kernel(dist_ref, qh_ref, qt_ref, kvh_ref, kvt_ref, out_ref, q_ref, kv_ref):
    head = kvh_ref.shape[0]

    @pl.when(pl.program_id(0) == 0)
    def _():
        q_ref[:head] = qh_ref[...]
        q_ref[head:] = qt_ref[...]
        kv_ref[:head] = kvh_ref[...]
        kv_ref[head:] = kvt_ref[...]

    def block(ref, c):
        return ref[pl.ds(pl.multiple_of(c * BLOCK, BLOCK), BLOCK), :]

    c = pl.program_id(0) + 2
    attend_block(block(q_ref, c), block(kv_ref, c), block(kv_ref, c - dist_ref[c]), out_ref)


def edge_kernel(dist_ref, q_ref, kv_ref, halo_ref, out_ref):
    c = pl.program_id(0)
    own = kv_ref[pl.ds(pl.multiple_of(c * BLOCK, BLOCK), BLOCK), :]
    at = c + 2 - dist_ref[c]
    before = halo_ref[pl.ds(pl.multiple_of(jnp.minimum(at, 1) * BLOCK, BLOCK), BLOCK), :]
    behind = jnp.where(at < 2, before, kv_ref[:BLOCK, :])
    attend_block(q_ref[...], own, behind, out_ref)


def attend_inner(dist, q_head, q_tail, kv_head, kv_tail):
    count = q_head.shape[0] + q_tail.shape[0]
    blocks = count // BLOCK - 2
    return pl.pallas_call(
        inner_kernel,
        grid_spec=pltpu.PrefetchScalarGridSpec(
            num_scalar_prefetch=1,
            grid=(blocks,),
            in_specs=[whole(v.shape) for v in (q_head, q_tail, kv_head, kv_tail)],
            out_specs=pl.BlockSpec((BLOCK, 256), lambda i, d: (i, 0)),
            scratch_shapes=[pltpu.VMEM((count, 128), BF), pltpu.VMEM((count, 256), BF)],
        ),
        out_shape=jax.ShapeDtypeStruct((blocks * BLOCK, 256), BF),
        compiler_params=params(),
        name="attend_inner",
    )(dist, q_head, q_tail, kv_head, kv_tail)


def attend_edge(dist, q, kv, halo):
    return pl.pallas_call(
        edge_kernel,
        grid_spec=pltpu.PrefetchScalarGridSpec(
            num_scalar_prefetch=1,
            grid=(2,),
            in_specs=[
                pl.BlockSpec((BLOCK, 128), lambda i, d: (i, 0)),
                whole((2 * BLOCK, 256)),
                whole(halo.shape),
            ],
            out_specs=pl.BlockSpec((BLOCK, 256), lambda i, d: (i, 0)),
        ),
        out_shape=jax.ShapeDtypeStruct((2 * BLOCK, 256), BF),
        compiler_params=params(),
        name="attend_edge",
    )(dist, q, kv, halo)


def back_kernel(width, idx_ref, edge_ref, inner_ref, *out_refs):
    n = 8 * width
    halves = []
    for half in range(2):
        idx = idx_ref[...] - (pl.program_id(0) * 2 + half) * n
        got = 0.0
        first = 0
        for ref in (edge_ref, inner_ref):
            count = ref.shape[0]
            place = lax.broadcasted_iota(jnp.int32, (n, count), 0)
            hot = one_hot(idx[:, first : first + count], place)
            got += jnp.dot(hot, ref[...], preferred_element_type=F32)
            first += count
        lines = terms_to_lines(got[:, 128:], n // 32).reshape(8, width // 32, 1, 128)
        row = lax.broadcasted_iota(jnp.int32, (8, 8, 128), 1)
        tail = jnp.zeros((8, 8, 128), F32)
        for part in range(width // 32):
            tail = jnp.where(row == part, lines[:, part], tail)
        halves.append((got[:, :128].astype(BF).reshape(8, width, 128), tail.astype(BF)))

    def store(ref, half):
        ref[:, :width, :] = halves[half][0]
        ref[:, width:, :] = halves[half][1]

    emit(out_refs, store)


def back_rows(idx, edge, inner, width, split):
    specs, shapes = emit_specs(split, width + 8, 128)
    return pl.pallas_call(
        functools.partial(back_kernel, width),
        grid=(4,),
        in_specs=[whole(idx.shape), whole(edge.shape), whole(inner.shape)],
        out_specs=specs,
        out_shape=shapes,
        compiler_params=params(),
        name="back_rows",
    )(idx, edge, inner)


ABSENT = -1e30


def fill_home(x_ref, width, home_refs):
    if len(home_refs) == 5:
        blocks = home_refs
    else:
        ref = home_refs[0]
        blocks = [ref.at[:, g] for g in range(3)] + [ref.at[:8, 3], ref.at[8:, 3]]
    row = 0
    for block in blocks:
        size = block.shape[0] * width
        x_ref[row : row + size, :128] = block[:, :width, :].reshape(size, 128)
        tail = block[:, width:, :].astype(F32)
        lines = jnp.concatenate(
            [tail[:, p : p + 1][:, None] for p in range(width // 32)], axis=1
        ).reshape(size // 32, 1, 128)
        x_ref[row : row + size, 128:] = lines_to_terms(lines).astype(BF)
        row += size


def gather_home(own_ref, cols, x_ref, width):
    near, far, row = 0.0, 0.0, 0
    for g in range(5):
        size = (16 if g < 3 else 8) * width
        first = 8 * width if g == 4 else 0
        place = lax.broadcasted_iota(jnp.int32, (cols.shape[0], size), 1) + first
        hot = one_hot(cols[:, g : g + 1], place)
        got = jnp.dot(hot, x_ref[row : row + size], preferred_element_type=F32)
        row += size
        if g == 0:
            near = got
        else:
            mine = own_ref[g] == 1
            near += jnp.where(mine, got, 0.0)
            far += jnp.where(mine, 0.0, got)
    return near, far


def home_kernel(width, own_ref, idx_ref, *refs):
    (*home_refs, out_ref, x_ref) = refs

    @pl.when(pl.program_id(0) == 0)
    def _():
        fill_home(x_ref, width, home_refs)

    near, far = gather_home(own_ref, jnp.transpose(idx_ref[0]), x_ref, width)
    out_ref[0] = near.astype(BF)
    out_ref[1] = far.astype(BF)


def last_kernel(width, own_ref, idx_ref, before_ref, *refs):
    (*home_refs, out_ref, x_ref) = refs

    @pl.when(pl.program_id(0) == 0)
    def _():
        fill_home(x_ref, width, home_refs)

    step = idx_ref.shape[2]
    states = list(gather_home(own_ref, jnp.transpose(idx_ref[0]), x_ref, width))
    states += [before_ref[i].astype(F32) for i in range(2)]
    here = [s[:, 131:132] > 0.5 for s in states]
    logs = [
        jnp.where(h, s[:, 128:129] + s[:, 129:130] + s[:, 130:131], ABSENT)
        for h, s in zip(here, states)
    ]
    top = functools.reduce(jnp.maximum, logs)
    scales = [jnp.where(h, jnp.exp(v - top), 0.0) for h, v in zip(here, logs)]
    total = sum(scales)
    some = total > 0.0
    summed = sum(s * p[:, :128] for s, p in zip(scales, states))
    safe = jnp.where(some, total, 1.0)
    log = jnp.where(some, top + jnp.log(safe), ABSENT)
    out_ref[0, :step, :] = (summed / safe).astype(BF)
    terms = term_lanes(log, step).astype(F32)
    out_ref[0, step:, :] = terms_to_lines(terms, step // 32).reshape(step // 32, 128).astype(BF)


def home_rows(own, idx, home, width, before=None):
    columns, count = idx.shape
    quarters = 4
    step = count // quarters
    args = [own, idx.reshape(columns, quarters, step).transpose(1, 0, 2)]
    specs = [pl.BlockSpec((1, columns, step), lambda i, o: (i, 0, 0))]
    if before is None:
        kernel = home_kernel
        out_spec = pl.BlockSpec((2, step, 256), lambda i, o: (0, i, 0))
        out_shape = jax.ShapeDtypeStruct((2, count, 256), BF)
    else:
        kernel = last_kernel
        args.append(before)
        specs.append(pl.BlockSpec((2, step, 256), lambda i, o: (0, i, 0)))
        out_spec = pl.BlockSpec((1, step + step // 32, 128), lambda i, o: (i, 0, 0))
        out_shape = jax.ShapeDtypeStruct((quarters, step + step // 32, 128), BF)
    return pl.pallas_call(
        functools.partial(kernel, width),
        grid_spec=pltpu.PrefetchScalarGridSpec(
            num_scalar_prefetch=1,
            grid=(quarters,),
            in_specs=specs + [whole(h.shape) for h in home],
            out_specs=out_spec,
            scratch_shapes=[pltpu.VMEM((64 * width, 256), BF)],
        ),
        out_shape=out_shape,
        compiler_params=params(),
        name="home_rows",
    )(*args, *home)


def finish_kernel(m_ref, w_ref, out_ref):
    rows = out_ref.shape[0]
    logs = []
    for i in range(4):
        line = m_ref[i, rows:, :].astype(F32).reshape(rows // 32, 1, 128)
        terms = lines_to_terms(line)
        logs.append(terms[:, 0:1] + terms[:, 1:2] + terms[:, 2:3])
    top = functools.reduce(jnp.maximum, logs)
    scales = [jnp.exp(v - top) for v in logs]
    total = sum(scales)
    summed = sum(s * m_ref[i, :rows, :].astype(F32) for i, s in enumerate(scales))
    blended = (summed / total).astype(BF)
    out_ref[...] = jnp.dot(blended, w_ref[...], preferred_element_type=F32).astype(BF)


def finish(merged, w_out):
    parts, rows, _ = merged.shape
    rows -= rows // 33
    return pl.pallas_call(
        finish_kernel,
        in_specs=[whole(merged.shape), whole(w_out.shape)],
        out_specs=whole((rows, w_out.shape[1])),
        grid=(1,),
        out_shape=jax.ShapeDtypeStruct((rows, w_out.shape[1]), BF),
        compiler_params=params(),
        name="finish",
    )(merged, w_out)


def send_places(own_slots, other_slots, low, width, by_target):
    zl, zh = lax.axis_index("zl"), lax.axis_index("zh")
    late = lax.axis_index(PLANE) >= 8
    places, mine = [], []
    for g, shift in enumerate(SHIFTS):
        if by_target or g < 3:
            k = shift
        else:
            k = jnp.where(late, -2, 2)
        own = ((zh * 4 + zl + k + 8) & 7) // 4 == zh
        slot = jnp.where(own, own_slots, other_slots)
        place = (slot >> 6) & 15
        at = slot & 63
        hit = ((slot >> 10) == ((zl + k + 8) & 3)) & (at >= low) & (at < low + width)
        if g == 3:
            hit &= place < 8
        if g == 4:
            hit &= place >= 8
        places.append(jnp.where(hit, place * width + at - low, -1))
        mine.append(own)
    return jnp.stack(places), jnp.stack(mine).astype(jnp.int32)


def take_places(taken, low, width):
    zl = lax.axis_index("zl")
    away = (zl - (taken >> 10)) & 3
    group = jnp.where(away < 2, away, 5 - away)
    source = (taken >> 6) & 15
    at = taken & 63
    hit = (at >= low) & (at < low + width)
    by_group = jnp.where(hit, (group * 16 + source) * width + at - low, -1)
    by_source = jnp.where(hit, (source * 4 + group) * width + at - low, -1)
    return by_group, by_source


def body(x, w_qk, w_v, w_out, slots, taken, looks):
    count = slots.shape[1]
    peers = lax.axis_size(SEQ)
    width = 2 * count // peers
    blocks = count // BLOCK
    tail = count - 2 * BLOCK
    others = lax.ppermute(slots, "zh", [(0, 1), (1, 0)])
    packed = project(x, w_qk, w_v)
    mine = lax.axis_index(SEQ) * blocks + jnp.arange(blocks, dtype=jnp.int32)
    dist = (mine[None, :] - looks) % (peers * blocks)
    next_device = [(i, (i + 1) % peers) for i in range(peers)]
    sent_0, own_0 = send_places(slots[0], others[0], 0, width, True)
    sent_1, own_1 = send_places(slots[1], others[1], 0, width, False)
    groups_0, _ = take_places(taken[0], 0, width)
    _, spots_0 = take_places(taken[0], 0, width)
    groups_1, _ = take_places(taken[1], 0, width)

    out_0 = scatter_rows(sent_0, packed, width, True)
    out_0, packed = together((out_0, packed))
    rung_0 = ring_all(out_0, 1)
    (out_1,) = scatter_rows(sent_1, packed, width, False)
    half_1 = plane(out_1)
    rung_0, half_1 = together((rung_0, half_1))
    arrived_0 = [plane(join(rung_0))]
    arrived_1 = ring_all(part(half_1), 1)

    def sort_round(spots, rows):
        q_tail, kv_tail = sort_rows(spots[tail:], rows, 2 * BLOCK)
        halo = lax.ppermute(kv_tail, SEQ, next_device)
        q_head, kv_head = sort_rows(spots[:tail], rows, 3 * BLOCK)
        return q_head, q_tail, kv_head, kv_tail, halo

    def attend_round(near, sorted_rows):
        q_head, q_tail, kv_head, kv_tail, halo = sorted_rows
        inner = attend_inner(near, q_head, q_tail, kv_head, kv_tail)
        return attend_edge(near, q_head, kv_head, halo), inner

    sorted_0 = sort_round(spots_0, arrived_0)
    edge, inner = attend_round(dist[0], sorted_0)
    (back_0,) = back_rows(groups_0[None], edge, inner, width, False)
    sorted_1 = sort_round(groups_1, arrived_1)
    edge, inner = attend_round(dist[1], sorted_1)
    back_1 = back_rows(groups_1[None], edge, inner, width, True)

    home_0 = ring_all(part(plane(back_0)), -1)
    home_1 = [plane(join(ring_all(back_1, -1)))]
    before = home_rows(own_0, sent_0, home_0, width)
    state = home_rows(own_1, sent_1, home_1, width, before)
    merged = lax.all_to_all(state, ROUND, 0, 0, tiled=True)
    return finish(merged, w_out)


def solution(mesh):
    fine = Mesh(mesh.devices.reshape(4, 4, 4, 2, 2), SEQ + ROUND)
    in_specs = (P(SEQ, None), P(), P(), P()) + (P(ROUND, SEQ),) * 3
    return jax.shard_map(
        body, mesh=fine, in_specs=in_specs, out_specs=P(SEQ + ROUND, None), check_vma=False
    )
```

```python
import functools

import jax
import jax.numpy as jnp
from jax import lax
from jax.experimental import pallas as pl
from jax.experimental.pallas import tpu as pltpu
from jax.sharding import Mesh
from jax.sharding import PartitionSpec as P

BLOCK = 256
SHIFTS = (0, 1, -1, 2, -2)
MASKED = -1000000000.0
SEQ = ("zl", "x", "y")
PLANE = ("x", "y")
ROUND = ("zh", "c")
BF = jnp.bfloat16
F32 = jnp.float32
VMEM_BYTES = 48 * 1024 * 1024


def params(n=1):
    return pltpu.CompilerParams(
        dimension_semantics=("arbitrary",) * n, vmem_limit_bytes=VMEM_BYTES
    )


def whole(shape):
    return pl.BlockSpec(shape, lambda *_: (0,) * len(shape))


def one_hot(a, b):
    return jnp.where(a == b, 1.0, 0.0).astype(BF)


def column(row):
    return jnp.transpose(jnp.broadcast_to(row, (8, row.shape[1])))[:, :1]


def in_hbm(v):
    return pltpu.with_memory_space_constraint(v, pltpu.HBM)


def project_kernel(x_ref, wqk_ref, wv_ref, out_ref, w_ref):
    @pl.when(pl.program_id(0) == 0)
    def _():
        w_ref[:, :128] = wqk_ref[...]
        w_ref[:, 128:] = wv_ref[...]

    out_ref[...] = jnp.dot(x_ref[...], w_ref[...], preferred_element_type=F32).astype(BF)


def project(x, w_qk, w_v):
    rows, model = x.shape
    step = 512
    return pl.pallas_call(
        project_kernel,
        grid=(rows // step,),
        in_specs=[
            pl.BlockSpec((step, model), lambda i: (i, 0)),
            whole(w_qk.shape),
            whole(w_v.shape),
        ],
        out_specs=pl.BlockSpec((step, 256), lambda i: (i, 0)),
        out_shape=jax.ShapeDtypeStruct((rows, 256), BF),
        scratch_shapes=[pltpu.VMEM((model, 256), BF)],
        compiler_params=params(),
        name="project",
    )(in_hbm(x), in_hbm(w_qk), in_hbm(w_v))


def ring(value, shift):
    def at(z):
        return (z % 4) * 2 + z // 4

    route = [(at(z), at((z + shift) % 8)) for z in range(8)]
    return lax.ppermute(value, ("zl", "zh"), route)


def ring_all(pieces, sign):
    return [pieces[0]] + [ring(p, sign * k) for p, k in zip(pieces[1:], SHIFTS[1:])]


def join(split):
    a, b, c, d, e = split
    return jnp.stack([a, b, c, jnp.concatenate([d, e])], axis=1)


def part(joint):
    return [joint[:, 0], joint[:, 1], joint[:, 2], joint[:8, 3], joint[8:, 3]]


def plane(joint):
    return lax.all_to_all(joint, PLANE, 0, 0, tiled=True)


together = lax.optimization_barrier


def emit_specs(split, width, lanes):
    if not split:
        return (
            [pl.BlockSpec((16, 1, width, lanes), lambda i: (0, i, 0, 0))],
            [jax.ShapeDtypeStruct((16, 4, width, lanes), BF)],
        )
    shapes = [(16, width, lanes)] * 3 + [(8, width, lanes)] * 2
    return [whole(v) for v in shapes], [jax.ShapeDtypeStruct(v, BF) for v in shapes]


def emit(refs, store):
    if len(refs) == 1:
        for half in range(2):
            store(refs[0].at[8 * half : 8 * half + 8, 0], half)
        return
    for group in range(4):

        @pl.when(pl.program_id(0) == group)
        def _(group=group):
            for half in range(2):
                if group < 3:
                    store(refs[group].at[8 * half : 8 * half + 8], half)
                else:
                    store(refs[3 + half], half)


def scatter_kernel(width, idx_ref, rows_ref, *out_refs):
    n = 8 * width
    group = pl.program_id(0)
    place = lax.broadcasted_iota(jnp.int32, (n, rows_ref.shape[0]), 0)
    halves = []
    for half in range(2):
        line = idx_ref[pl.ds(jnp.where(group == 3, 3 + half, group), 1), :]
        hot = one_hot(line - half * n, place)
        got = jnp.dot(hot, rows_ref[...], preferred_element_type=F32).astype(BF)
        halves.append(got.reshape(8, width, 256))

    def store(ref, half):
        ref[...] = halves[half]

    emit(out_refs, store)


def scatter_rows(idx, rows, width, split):
    specs, shapes = emit_specs(split, width, 256)
    return pl.pallas_call(
        functools.partial(scatter_kernel, width),
        grid=(4,),
        in_specs=[whole(idx.shape), whole(rows.shape)],
        out_specs=specs,
        out_shape=shapes,
        compiler_params=params(),
        name="scatter_rows",
    )(idx, rows)


def sort_kernel(idx_ref, *refs):
    (*row_refs, q_ref, kv_ref) = refs
    col = column(idx_ref[0])
    got, base = 0.0, 0
    for ref in row_refs:
        rows = ref[...].reshape(-1, 256)
        n = rows.shape[0]
        place = lax.broadcasted_iota(jnp.int32, (q_ref.shape[0], n), 1) + base
        got += jnp.dot(one_hot(col, place), rows, preferred_element_type=F32)
        base += n
    qk = got[:, :128]
    keys = qk * lax.rsqrt(jnp.sum(qk * qk, axis=-1, keepdims=True) + 1e-06)
    q_ref[...] = qk.astype(BF)
    kv_ref[:, :128] = keys.astype(BF)
    kv_ref[:, 128:] = got[:, 128:].astype(BF)


def sort_rows(idx, rows, step):
    count = idx.shape[-1]
    blocks = count // step
    return pl.pallas_call(
        sort_kernel,
        grid=(blocks,),
        in_specs=[pl.BlockSpec((1, 1, step), lambda i: (i, 0, 0))]
        + [whole(r.shape) for r in rows],
        out_specs=[
            pl.BlockSpec((step, 128), lambda i: (i, 0)),
            pl.BlockSpec((step, 256), lambda i: (i, 0)),
        ],
        out_shape=[
            jax.ShapeDtypeStruct((count, 128), BF),
            jax.ShapeDtypeStruct((count, 256), BF),
        ],
        compiler_params=params(),
        name="sort_rows",
    )(idx.reshape(blocks, 1, step), *rows)


def terms_to_lines(terms, groups):
    terms = terms.reshape(groups, 32, 128)
    slot = lax.broadcasted_iota(jnp.int32, terms.shape, 1)
    lane = lax.broadcasted_iota(jnp.int32, terms.shape, 2) % 32
    return jnp.sum(jnp.where(slot == lane, terms, 0.0), axis=1, keepdims=True)


def lines_to_terms(line):
    n = line.shape[0]
    shape = (n, 32, 128)
    slot = lax.broadcasted_iota(jnp.int32, shape, 1)
    lane = lax.broadcasted_iota(jnp.int32, shape, 2) % 32
    spread = jnp.where(slot == lane, line, 0.0).reshape(n * 32, 128).astype(BF)
    group = lax.broadcasted_iota(jnp.int32, (128, 128), 0) // 32
    pick = one_hot(group, lax.broadcasted_iota(jnp.int32, (128, 128), 1))
    return jnp.dot(spread, pick, preferred_element_type=F32)


def three_terms(v):
    hi = v.astype(BF).astype(F32)
    mid = (v - hi).astype(BF).astype(F32)
    lo = v - hi - mid
    return hi, mid, lo


def term_lanes(v, rows):
    hi, mid, lo = three_terms(v)
    group = lax.broadcasted_iota(jnp.int32, (rows, 128), 1) // 32
    return jnp.where(
        group == 0, hi, jnp.where(group == 1, mid, jnp.where(group == 2, lo, 1.0))
    ).astype(BF)


def attend_block(q, own, behind, out_ref):
    nt = (((1,), (1,)), ((), ()))
    s1 = lax.dot_general(q, own[:, :128], nt, preferred_element_type=F32)
    s2 = lax.dot_general(q, behind[:, :128], nt, preferred_element_type=F32)
    r = lax.broadcasted_iota(jnp.int32, (BLOCK, BLOCK), 0)
    k = lax.broadcasted_iota(jnp.int32, (BLOCK, BLOCK), 1)
    s1 = jnp.where(r == k, MASKED, s1)
    top = jnp.maximum(
        jnp.max(s1, axis=-1, keepdims=True), jnp.max(s2, axis=-1, keepdims=True)
    )
    e1 = jnp.exp(s1 - top)
    e2 = jnp.exp(s2 - top)
    total = jnp.sum(e1, axis=-1, keepdims=True) + jnp.sum(e2, axis=-1, keepdims=True)
    o = jnp.dot(e1.astype(BF), own[:, 128:], preferred_element_type=F32) + jnp.dot(
        e2.astype(BF), behind[:, 128:], preferred_element_type=F32
    )
    out_ref[:, :128] = (o / total).astype(BF)
    out_ref[:, 128:] = term_lanes(top + jnp.log(total), BLOCK)


def inner_kernel(dist_ref, qh_ref, qt_ref, kvh_ref, kvt_ref, out_ref, q_ref, kv_ref):
    head = kvh_ref.shape[0]

    @pl.when(pl.program_id(0) == 0)
    def _():
        q_ref[:head] = qh_ref[...]
        q_ref[head:] = qt_ref[...]
        kv_ref[:head] = kvh_ref[...]
        kv_ref[head:] = kvt_ref[...]

    def block(ref, c):
        return ref[pl.ds(pl.multiple_of(c * BLOCK, BLOCK), BLOCK), :]

    c = pl.program_id(0) + 2
    attend_block(block(q_ref, c), block(kv_ref, c), block(kv_ref, c - dist_ref[c]), out_ref)


def edge_kernel(dist_ref, q_ref, kv_ref, halo_ref, out_ref):
    c = pl.program_id(0)
    own = kv_ref[pl.ds(pl.multiple_of(c * BLOCK, BLOCK), BLOCK), :]
    at = c + 2 - dist_ref[c]
    before = halo_ref[pl.ds(pl.multiple_of(jnp.minimum(at, 1) * BLOCK, BLOCK), BLOCK), :]
    behind = jnp.where(at < 2, before, kv_ref[:BLOCK, :])
    attend_block(q_ref[...], own, behind, out_ref)


def attend_inner(dist, q_head, q_tail, kv_head, kv_tail):
    count = q_head.shape[0] + q_tail.shape[0]
    blocks = count // BLOCK - 2
    return pl.pallas_call(
        inner_kernel,
        grid_spec=pltpu.PrefetchScalarGridSpec(
            num_scalar_prefetch=1,
            grid=(blocks,),
            in_specs=[whole(v.shape) for v in (q_head, q_tail, kv_head, kv_tail)],
            out_specs=pl.BlockSpec((BLOCK, 256), lambda i, d: (i, 0)),
            scratch_shapes=[pltpu.VMEM((count, 128), BF), pltpu.VMEM((count, 256), BF)],
        ),
        out_shape=jax.ShapeDtypeStruct((blocks * BLOCK, 256), BF),
        compiler_params=params(),
        name="attend_inner",
    )(dist, q_head, q_tail, kv_head, kv_tail)


def attend_edge(dist, q, kv, halo):
    return pl.pallas_call(
        edge_kernel,
        grid_spec=pltpu.PrefetchScalarGridSpec(
            num_scalar_prefetch=1,
            grid=(2,),
            in_specs=[
                pl.BlockSpec((BLOCK, 128), lambda i, d: (i, 0)),
                whole((2 * BLOCK, 256)),
                whole(halo.shape),
            ],
            out_specs=pl.BlockSpec((BLOCK, 256), lambda i, d: (i, 0)),
        ),
        out_shape=jax.ShapeDtypeStruct((2 * BLOCK, 256), BF),
        compiler_params=params(),
        name="attend_edge",
    )(dist, q, kv, halo)


def back_kernel(width, idx_ref, edge_ref, inner_ref, *out_refs):
    n = 8 * width
    halves = []
    for half in range(2):
        idx = idx_ref[...] - (pl.program_id(0) * 2 + half) * n
        got = 0.0
        first = 0
        for ref in (edge_ref, inner_ref):
            count = ref.shape[0]
            place = lax.broadcasted_iota(jnp.int32, (n, count), 0)
            hot = one_hot(idx[:, first : first + count], place)
            got += jnp.dot(hot, ref[...], preferred_element_type=F32)
            first += count
        lines = terms_to_lines(got[:, 128:], n // 32).reshape(8, width // 32, 1, 128)
        row = lax.broadcasted_iota(jnp.int32, (8, 8, 128), 1)
        tail = jnp.zeros((8, 8, 128), F32)
        for part in range(width // 32):
            tail = jnp.where(row == part, lines[:, part], tail)
        halves.append((got[:, :128].astype(BF).reshape(8, width, 128), tail.astype(BF)))

    def store(ref, half):
        ref[:, :width, :] = halves[half][0]
        ref[:, width:, :] = halves[half][1]

    emit(out_refs, store)


def back_rows(idx, edge, inner, width, split):
    specs, shapes = emit_specs(split, width + 8, 128)
    return pl.pallas_call(
        functools.partial(back_kernel, width),
        grid=(4,),
        in_specs=[whole(idx.shape), whole(edge.shape), whole(inner.shape)],
        out_specs=specs,
        out_shape=shapes,
        compiler_params=params(),
        name="back_rows",
    )(idx, edge, inner)


ABSENT = -1e30


def fill_home(x_ref, width, home_refs):
    if len(home_refs) == 5:
        blocks = home_refs
    else:
        ref = home_refs[0]
        blocks = [ref.at[:, g] for g in range(3)] + [ref.at[:8, 3], ref.at[8:, 3]]
    row = 0
    for block in blocks:
        size = block.shape[0] * width
        x_ref[row : row + size, :128] = block[:, :width, :].reshape(size, 128)
        tail = block[:, width:, :].astype(F32)
        lines = jnp.concatenate(
            [tail[:, p : p + 1][:, None] for p in range(width // 32)], axis=1
        ).reshape(size // 32, 1, 128)
        x_ref[row : row + size, 128:] = lines_to_terms(lines).astype(BF)
        row += size


def gather_home(own_ref, cols, x_ref, width):
    near, far, row = 0.0, 0.0, 0
    for g in range(5):
        size = (16 if g < 3 else 8) * width
        first = 8 * width if g == 4 else 0
        place = lax.broadcasted_iota(jnp.int32, (cols.shape[0], size), 1) + first
        hot = one_hot(cols[:, g : g + 1], place)
        got = jnp.dot(hot, x_ref[row : row + size], preferred_element_type=F32)
        row += size
        if g == 0:
            near = got
        else:
            mine = own_ref[g] == 1
            near += jnp.where(mine, got, 0.0)
            far += jnp.where(mine, 0.0, got)
    return near, far


def home_kernel(width, own_ref, idx_ref, *refs):
    (*home_refs, out_ref, x_ref) = refs

    @pl.when(pl.program_id(0) == 0)
    def _():
        fill_home(x_ref, width, home_refs)

    near, far = gather_home(own_ref, jnp.transpose(idx_ref[0]), x_ref, width)
    out_ref[0] = near.astype(BF)
    out_ref[1] = far.astype(BF)


def last_kernel(width, own_ref, idx_ref, before_ref, *refs):
    (*home_refs, out_ref, x_ref) = refs

    @pl.when(pl.program_id(0) == 0)
    def _():
        fill_home(x_ref, width, home_refs)

    step = idx_ref.shape[2]
    states = list(gather_home(own_ref, jnp.transpose(idx_ref[0]), x_ref, width))
    states += [before_ref[i].astype(F32) for i in range(2)]
    here = [s[:, 131:132] > 0.5 for s in states]
    logs = [
        jnp.where(h, s[:, 128:129] + s[:, 129:130] + s[:, 130:131], ABSENT)
        for h, s in zip(here, states)
    ]
    top = functools.reduce(jnp.maximum, logs)
    scales = [jnp.where(h, jnp.exp(v - top), 0.0) for h, v in zip(here, logs)]
    total = sum(scales)
    some = total > 0.0
    summed = sum(s * p[:, :128] for s, p in zip(scales, states))
    safe = jnp.where(some, total, 1.0)
    log = jnp.where(some, top + jnp.log(safe), ABSENT)
    out_ref[0, :step, :] = (summed / safe).astype(BF)
    terms = term_lanes(log, step).astype(F32)
    out_ref[0, step:, :] = terms_to_lines(terms, step // 32).reshape(step // 32, 128).astype(BF)


def home_rows(own, idx, home, width, before=None):
    columns, count = idx.shape
    quarters = 4
    step = count // quarters
    args = [own, idx.reshape(columns, quarters, step).transpose(1, 0, 2)]
    specs = [pl.BlockSpec((1, columns, step), lambda i, o: (i, 0, 0))]
    if before is None:
        kernel = home_kernel
        out_spec = pl.BlockSpec((2, step, 256), lambda i, o: (0, i, 0))
        out_shape = jax.ShapeDtypeStruct((2, count, 256), BF)
    else:
        kernel = last_kernel
        args.append(before)
        specs.append(pl.BlockSpec((2, step, 256), lambda i, o: (0, i, 0)))
        out_spec = pl.BlockSpec((1, step + step // 32, 128), lambda i, o: (i, 0, 0))
        out_shape = jax.ShapeDtypeStruct((quarters, step + step // 32, 128), BF)
    return pl.pallas_call(
        functools.partial(kernel, width),
        grid_spec=pltpu.PrefetchScalarGridSpec(
            num_scalar_prefetch=1,
            grid=(quarters,),
            in_specs=specs + [whole(h.shape) for h in home],
            out_specs=out_spec,
            scratch_shapes=[pltpu.VMEM((64 * width, 256), BF)],
        ),
        out_shape=out_shape,
        compiler_params=params(),
        name="home_rows",
    )(*args, *[in_hbm(h) for h in home])


def finish_kernel(m_ref, w_ref, out_ref):
    rows = out_ref.shape[0]
    logs = []
    for i in range(4):
        line = m_ref[i, rows:, :].astype(F32).reshape(rows // 32, 1, 128)
        terms = lines_to_terms(line)
        logs.append(terms[:, 0:1] + terms[:, 1:2] + terms[:, 2:3])
    top = functools.reduce(jnp.maximum, logs)
    scales = [jnp.exp(v - top) for v in logs]
    total = sum(scales)
    summed = sum(s * m_ref[i, :rows, :].astype(F32) for i, s in enumerate(scales))
    blended = (summed / total).astype(BF)
    out_ref[...] = jnp.dot(blended, w_ref[...], preferred_element_type=F32).astype(BF)


def finish(merged, w_out):
    parts, rows, _ = merged.shape
    rows -= rows // 33
    return pl.pallas_call(
        finish_kernel,
        in_specs=[whole(merged.shape), whole(w_out.shape)],
        out_specs=whole((rows, w_out.shape[1])),
        grid=(1,),
        out_shape=jax.ShapeDtypeStruct((rows, w_out.shape[1]), BF),
        compiler_params=params(),
        name="finish",
    )(merged, w_out)


def send_places(own_slots, other_slots, low, width, by_target):
    zl, zh = lax.axis_index("zl"), lax.axis_index("zh")
    late = lax.axis_index(PLANE) >= 8
    places, mine = [], []
    for g, shift in enumerate(SHIFTS):
        if by_target or g < 3:
            k = shift
        else:
            k = jnp.where(late, -2, 2)
        own = ((zh * 4 + zl + k + 8) & 7) // 4 == zh
        slot = jnp.where(own, own_slots, other_slots)
        place = (slot >> 6) & 15
        at = slot & 63
        hit = ((slot >> 10) == ((zl + k + 8) & 3)) & (at >= low) & (at < low + width)
        if g == 3:
            hit &= place < 8
        if g == 4:
            hit &= place >= 8
        places.append(jnp.where(hit, place * width + at - low, -1))
        mine.append(own)
    return jnp.stack(places), jnp.stack(mine).astype(jnp.int32)


def take_places(taken, low, width):
    zl = lax.axis_index("zl")
    away = (zl - (taken >> 10)) & 3
    group = jnp.where(away < 2, away, 5 - away)
    source = (taken >> 6) & 15
    at = taken & 63
    hit = (at >= low) & (at < low + width)
    by_group = jnp.where(hit, (group * 16 + source) * width + at - low, -1)
    by_source = jnp.where(hit, (source * 4 + group) * width + at - low, -1)
    return by_group, by_source


def body(x, w_qk, w_v, w_out, slots, taken, looks):
    count = slots.shape[1]
    peers = lax.axis_size(SEQ)
    width = 2 * count // peers
    blocks = count // BLOCK
    tail = count - 2 * BLOCK
    others = lax.ppermute(slots, "zh", [(0, 1), (1, 0)])
    packed = project(x, w_qk, w_v)
    mine = lax.axis_index(SEQ) * blocks + jnp.arange(blocks, dtype=jnp.int32)
    dist = (mine[None, :] - looks) % (peers * blocks)
    next_device = [(i, (i + 1) % peers) for i in range(peers)]
    sent_0, own_0 = send_places(slots[0], others[0], 0, width, True)
    sent_1, own_1 = send_places(slots[1], others[1], 0, width, False)
    groups_0, _ = take_places(taken[0], 0, width)
    _, spots_0 = take_places(taken[0], 0, width)
    groups_1, _ = take_places(taken[1], 0, width)

    out_0 = scatter_rows(sent_0, packed, width, True)
    out_0, packed = together((out_0, packed))
    rung_0 = ring_all(out_0, 1)
    (out_1,) = scatter_rows(sent_1, packed, width, False)
    half_1 = plane(out_1)
    rung_0, half_1 = together((rung_0, half_1))
    arrived_0, arrived_1 = together(
        ([plane(join(rung_0))], ring_all(part(half_1), 1))
    )

    def sort_round(spots, rows):
        q_tail, kv_tail = sort_rows(spots[tail:], rows, 2 * BLOCK)
        halo = lax.ppermute(kv_tail, SEQ, next_device)
        q_head, kv_head = sort_rows(spots[:tail], rows, 3 * BLOCK)
        return q_head, q_tail, kv_head, kv_tail, halo

    def attend_round(near, sorted_rows):
        q_head, q_tail, kv_head, kv_tail, halo = sorted_rows
        inner = attend_inner(near, q_head, q_tail, kv_head, kv_tail)
        return attend_edge(near, q_head, kv_head, halo), inner

    sorted_0 = sort_round(spots_0, arrived_0)
    edge, inner = attend_round(dist[0], sorted_0)
    (back_0,) = back_rows(groups_0[None], edge, inner, width, False)
    sorted_1 = sort_round(groups_1, arrived_1)
    q_head, q_tail, kv_head, kv_tail, halo = sorted_1
    half_0, q_head, kv_head = together((plane(back_0), q_head, kv_head))
    edge, inner = attend_round(dist[1], (q_head, q_tail, kv_head, kv_tail, halo))
    back_1 = back_rows(groups_1[None], edge, inner, width, True)
    home_0, back_1 = together((ring_all(part(half_0), -1), back_1))
    home_1 = [plane(join(ring_all(back_1, -1)))]
    before = home_rows(own_0, sent_0, home_0, width)
    state = home_rows(own_1, sent_1, home_1, width, before)
    merged = lax.all_to_all(state, ROUND, 0, 0, tiled=True)
    return finish(merged, w_out)


def solution(mesh):
    fine = Mesh(mesh.devices.reshape(4, 4, 4, 2, 2), SEQ + ROUND)
    in_specs = (P(SEQ, None), P(), P(), P()) + (P(ROUND, SEQ),) * 3
    return jax.shard_map(
        body, mesh=fine, in_specs=in_specs, out_specs=P(SEQ + ROUND, None), check_vma=False
    )
```

```python
import functools

import jax
import jax.numpy as jnp
from jax import lax
from jax.experimental import pallas as pl
from jax.experimental.pallas import tpu as pltpu
from jax.sharding import Mesh
from jax.sharding import PartitionSpec as P

BLOCK = 256
MASKED = -1000000000.0
SEQ = ("zl", "x", "y")
PLANE = ("x", "y")
ROUND = ("zh", "c")
BF = jnp.bfloat16
F32 = jnp.float32
VMEM_BYTES = 48 * 1024 * 1024


def params(n=1):
    return pltpu.CompilerParams(
        dimension_semantics=("arbitrary",) * n, vmem_limit_bytes=VMEM_BYTES
    )


def whole(shape):
    return pl.BlockSpec(shape, lambda *_: (0,) * len(shape))


def one_hot(a, b):
    return jnp.where(a == b, 1.0, 0.0).astype(BF)


def column(row):
    return jnp.transpose(jnp.broadcast_to(row, (8, row.shape[1])))[:, :1]


def in_hbm(v):
    return pltpu.with_memory_space_constraint(v, pltpu.HBM)


def project_kernel(x_ref, wqk_ref, wv_ref, out_ref, w_ref):
    @pl.when(pl.program_id(0) == 0)
    def _():
        w_ref[:, :128] = wqk_ref[...]
        w_ref[:, 128:] = wv_ref[...]

    out_ref[...] = jnp.dot(x_ref[...], w_ref[...], preferred_element_type=F32).astype(BF)


def project(x, w_qk, w_v):
    rows, model = x.shape
    step = 512
    return pl.pallas_call(
        project_kernel,
        grid=(rows // step,),
        in_specs=[
            pl.BlockSpec((step, model), lambda i: (i, 0)),
            whole(w_qk.shape),
            whole(w_v.shape),
        ],
        out_specs=pl.BlockSpec((step, 256), lambda i: (i, 0)),
        out_shape=jax.ShapeDtypeStruct((rows, 256), BF),
        scratch_shapes=[pltpu.VMEM((model, 256), BF)],
        compiler_params=params(),
        name="project",
    )(in_hbm(x), in_hbm(w_qk), in_hbm(w_v))


def ring(value, shift):
    def at(z):
        return (z % 4) * 2 + z // 4

    route = [(at(z), at((z + shift) % 8)) for z in range(8)]
    return lax.ppermute(value, ("zl", "zh"), route)


def join(first, second):
    return jnp.stack([first, second], axis=1)


def plane(joint):
    return lax.all_to_all(joint, PLANE, 0, 0, tiled=True)


together = lax.optimization_barrier


def scatter_kernel(idx_ref, rows_ref, even_ref, up_ref, down_ref):
    peers, _, width, lanes = even_ref.shape
    group = pl.program_id(0)
    place = lax.broadcasted_iota(jnp.int32, (peers * width, rows_ref.shape[0]), 0)
    hot = one_hot(idx_ref[pl.ds(group, 1), :], place)
    got = jnp.dot(hot, rows_ref[...], preferred_element_type=F32)
    got = got.astype(BF).reshape(peers, width, lanes)
    places = (even_ref.at[:, 0], even_ref.at[:, 1], up_ref, down_ref)
    for g, ref in enumerate(places):

        @pl.when(group == g)
        def _(ref=ref):
            ref[...] = got


def scatter_rows(idx, rows, width):
    shapes = [(16, 2, width, 256)] + [(16, width, 256)] * 2
    return pl.pallas_call(
        scatter_kernel,
        grid=(4,),
        in_specs=[whole(idx.shape), whole(rows.shape)],
        out_specs=[whole(v) for v in shapes],
        out_shape=[pltpu.HBM(v, BF) for v in shapes],
        compiler_params=params(),
        name="scatter_rows",
    )(idx, rows)


def sort_kernel(idx_ref, *refs):
    (*row_refs, q_ref, kv_ref) = refs
    col = column(idx_ref[0])
    got, base = 0.0, 0
    for ref in row_refs:
        rows = ref[...].reshape(-1, 256)
        n = rows.shape[0]
        place = lax.broadcasted_iota(jnp.int32, (q_ref.shape[0], n), 1) + base
        got += jnp.dot(one_hot(col, place), rows, preferred_element_type=F32)
        base += n
    qk = got[:, :128]
    keys = qk * lax.rsqrt(jnp.sum(qk * qk, axis=-1, keepdims=True) + 1e-06)
    q_ref[...] = qk.astype(BF)
    kv_ref[:, :128] = keys.astype(BF)
    kv_ref[:, 128:] = got[:, 128:].astype(BF)


def sort_rows(idx, rows, step):
    count = idx.shape[-1]
    blocks = count // step
    peers, _, width, lanes = rows[0].shape
    near = pl.BlockSpec((peers, 1, width, lanes), lambda i: (0, 0, 0, 0))
    return pl.pallas_call(
        sort_kernel,
        grid=(blocks,),
        in_specs=[pl.BlockSpec((1, 1, step), lambda i: (i, 0, 0)), near]
        + [whole(r.shape) for r in rows[1:]],
        out_specs=[
            pl.BlockSpec((step, 128), lambda i: (i, 0)),
            pl.BlockSpec((step, 256), lambda i: (i, 0)),
        ],
        out_shape=[
            jax.ShapeDtypeStruct((count, 128), BF),
            jax.ShapeDtypeStruct((count, 256), BF),
        ],
        compiler_params=params(),
        name="sort_rows",
    )(idx.reshape(blocks, 1, step), *[in_hbm(r) for r in rows])


def terms_to_lines(terms, groups):
    terms = terms.reshape(groups, 32, 128)
    slot = lax.broadcasted_iota(jnp.int32, terms.shape, 1)
    lane = lax.broadcasted_iota(jnp.int32, terms.shape, 2) % 32
    return jnp.sum(jnp.where(slot == lane, terms, 0.0), axis=1, keepdims=True)


def lines_to_terms(line):
    n = line.shape[0]
    shape = (n, 32, 128)
    slot = lax.broadcasted_iota(jnp.int32, shape, 1)
    lane = lax.broadcasted_iota(jnp.int32, shape, 2) % 32
    spread = jnp.where(slot == lane, line, 0.0).reshape(n * 32, 128).astype(BF)
    group = lax.broadcasted_iota(jnp.int32, (128, 128), 0) // 32
    pick = one_hot(group, lax.broadcasted_iota(jnp.int32, (128, 128), 1))
    return jnp.dot(spread, pick, preferred_element_type=F32)


def three_terms(v):
    hi = v.astype(BF).astype(F32)
    mid = (v - hi).astype(BF).astype(F32)
    lo = v - hi - mid
    return hi, mid, lo


def term_lanes(v, rows):
    hi, mid, lo = three_terms(v)
    group = lax.broadcasted_iota(jnp.int32, (rows, 128), 1) // 32
    return jnp.where(
        group == 0, hi, jnp.where(group == 1, mid, jnp.where(group == 2, lo, 1.0))
    ).astype(BF)


def attend_block(q, own, behind, out_ref):
    nt = (((1,), (1,)), ((), ()))
    s1 = lax.dot_general(q, own[:, :128], nt, preferred_element_type=F32)
    s2 = lax.dot_general(q, behind[:, :128], nt, preferred_element_type=F32)
    r = lax.broadcasted_iota(jnp.int32, (BLOCK, BLOCK), 0)
    k = lax.broadcasted_iota(jnp.int32, (BLOCK, BLOCK), 1)
    s1 = jnp.where(r == k, MASKED, s1)
    top = jnp.maximum(
        jnp.max(s1, axis=-1, keepdims=True), jnp.max(s2, axis=-1, keepdims=True)
    )
    e1 = jnp.exp(s1 - top)
    e2 = jnp.exp(s2 - top)
    total = jnp.sum(e1, axis=-1, keepdims=True) + jnp.sum(e2, axis=-1, keepdims=True)
    o = jnp.dot(e1.astype(BF), own[:, 128:], preferred_element_type=F32) + jnp.dot(
        e2.astype(BF), behind[:, 128:], preferred_element_type=F32
    )
    out_ref[:, :128] = (o / total).astype(BF)
    out_ref[:, 128:] = term_lanes(top + jnp.log(total), BLOCK)


def inner_kernel(dist_ref, qh_ref, qt_ref, kvh_ref, kvt_ref, out_ref, q_ref, kv_ref):
    head = kvh_ref.shape[0]

    @pl.when(pl.program_id(0) == 0)
    def _():
        q_ref[:head] = qh_ref[...]
        q_ref[head:] = qt_ref[...]
        kv_ref[:head] = kvh_ref[...]
        kv_ref[head:] = kvt_ref[...]

    def block(ref, c):
        return ref[pl.ds(pl.multiple_of(c * BLOCK, BLOCK), BLOCK), :]

    c = pl.program_id(0) + 2
    attend_block(block(q_ref, c), block(kv_ref, c), block(kv_ref, c - dist_ref[c]), out_ref)


def edge_kernel(dist_ref, q_ref, kv_ref, halo_ref, out_ref):
    c = pl.program_id(0)
    own = kv_ref[pl.ds(pl.multiple_of(c * BLOCK, BLOCK), BLOCK), :]
    at = c + 2 - dist_ref[c]
    before = halo_ref[pl.ds(pl.multiple_of(jnp.minimum(at, 1) * BLOCK, BLOCK), BLOCK), :]
    behind = jnp.where(at < 2, before, kv_ref[:BLOCK, :])
    attend_block(q_ref[...], own, behind, out_ref)


def attend_inner(dist, q_head, q_tail, kv_head, kv_tail):
    count = q_head.shape[0] + q_tail.shape[0]
    blocks = count // BLOCK - 2
    return pl.pallas_call(
        inner_kernel,
        grid_spec=pltpu.PrefetchScalarGridSpec(
            num_scalar_prefetch=1,
            grid=(blocks,),
            in_specs=[whole(v.shape) for v in (q_head, q_tail, kv_head, kv_tail)],
            out_specs=pl.BlockSpec((BLOCK, 256), lambda i, d: (i, 0)),
            scratch_shapes=[pltpu.VMEM((count, 128), BF), pltpu.VMEM((count, 256), BF)],
        ),
        out_shape=jax.ShapeDtypeStruct((blocks * BLOCK, 256), BF),
        compiler_params=params(),
        name="attend_inner",
    )(dist, q_head, q_tail, kv_head, kv_tail)


def attend_edge(dist, q, kv, halo):
    return pl.pallas_call(
        edge_kernel,
        grid_spec=pltpu.PrefetchScalarGridSpec(
            num_scalar_prefetch=1,
            grid=(2,),
            in_specs=[
                pl.BlockSpec((BLOCK, 128), lambda i, d: (i, 0)),
                whole((2 * BLOCK, 256)),
                whole(halo.shape),
            ],
            out_specs=pl.BlockSpec((BLOCK, 256), lambda i, d: (i, 0)),
        ),
        out_shape=jax.ShapeDtypeStruct((2 * BLOCK, 256), BF),
        compiler_params=params(),
        name="attend_edge",
    )(dist, q, kv, halo)


def back_kernel(idx_ref, edge_ref, inner_ref, near_ref, low_ref, high_ref, odd_ref):
    peers, ext, _ = near_ref.shape
    width = ext - 8
    n = peers * width
    group = pl.program_id(0)
    idx = idx_ref[...] - group * n
    got = 0.0
    first = 0
    for ref in (edge_ref, inner_ref):
        count = ref.shape[0]
        place = lax.broadcasted_iota(jnp.int32, (n, count), 0)
        hot = one_hot(idx[:, first : first + count], place)
        got += jnp.dot(hot, ref[...], preferred_element_type=F32)
        first += count
    lines = terms_to_lines(got[:, 128:], n // 32).reshape(peers, width // 32, 1, 128)
    row = lax.broadcasted_iota(jnp.int32, (peers, 8, 128), 1)
    tail = jnp.zeros((peers, 8, 128), F32)
    for part in range(width // 32):
        tail = jnp.where(row == part, lines[:, part], tail)
    tail = tail.astype(BF)
    got = got[:, :128].astype(BF).reshape(peers, width, 128)

    def store(ref, at):
        ref[:, :width, :] = got[at]
        ref[:, width:, :] = tail[at]

    every, half = slice(None), peers // 2

    @pl.when(group == 0)
    def _():
        store(near_ref, every)

    @pl.when(group == 1)
    def _():
        store(low_ref, slice(0, half))
        store(high_ref, slice(half, peers))

    for g in range(2):

        @pl.when(group == 2 + g)
        def _(g=g):
            store(odd_ref.at[:, g], every)


def back_rows(idx, edge, inner, width):
    ext = width + 8
    shapes = [(16, ext, 128), (8, ext, 128), (8, ext, 128), (16, 2, ext, 128)]
    return pl.pallas_call(
        back_kernel,
        grid=(4,),
        in_specs=[whole(idx.shape), whole(edge.shape), whole(inner.shape)],
        out_specs=[whole(v) for v in shapes],
        out_shape=[pltpu.HBM(v, BF) for v in shapes],
        compiler_params=params(),
        name="back_rows",
    )(idx, edge, inner)


ABSENT = -1e30


def fill_home(x_ref, width, even_ref, up_ref, down_ref):
    row = 0
    for block in (even_ref.at[:, 0], even_ref.at[:, 1], up_ref, down_ref):
        size = block.shape[0] * width
        x_ref[row : row + size, :128] = block[:, :width, :].reshape(size, 128)
        tail = block[:, width:, :].astype(F32)
        lines = jnp.concatenate(
            [tail[:, p : p + 1][:, None] for p in range(width // 32)], axis=1
        ).reshape(size // 32, 1, 128)
        x_ref[row : row + size, 128:] = lines_to_terms(lines).astype(BF)
        row += size


def gather_home(own_ref, cols, x_ref, width):
    near, far = 0.0, 0.0
    size = 16 * width
    place = lax.broadcasted_iota(jnp.int32, (cols.shape[0], size), 1)
    for g in range(4):
        hot = one_hot(cols[:, g : g + 1], place)
        got = jnp.dot(hot, x_ref[g * size : (g + 1) * size], preferred_element_type=F32)
        if g == 0:
            near = got
        else:
            mine = own_ref[g] == 1
            near += jnp.where(mine, got, 0.0)
            far += jnp.where(mine, 0.0, got)
    return near, far


def home_kernel(width, own_ref, idx_ref, *refs):
    (*home_refs, out_ref, x_ref) = refs

    @pl.when(pl.program_id(0) == 0)
    def _():
        fill_home(x_ref, width, *home_refs)

    near, far = gather_home(own_ref, jnp.transpose(idx_ref[0]), x_ref, width)
    out_ref[0] = near.astype(BF)
    out_ref[1] = far.astype(BF)


def last_kernel(width, own_ref, idx_ref, before_ref, *refs):
    (*home_refs, out_ref, x_ref) = refs

    @pl.when(pl.program_id(0) == 0)
    def _():
        fill_home(x_ref, width, *home_refs)

    step = idx_ref.shape[2]
    states = list(gather_home(own_ref, jnp.transpose(idx_ref[0]), x_ref, width))
    states += [before_ref[i].astype(F32) for i in range(2)]
    here = [s[:, 131:132] > 0.5 for s in states]
    logs = [
        jnp.where(h, s[:, 128:129] + s[:, 129:130] + s[:, 130:131], ABSENT)
        for h, s in zip(here, states)
    ]
    top = functools.reduce(jnp.maximum, logs)
    scales = [jnp.where(h, jnp.exp(v - top), 0.0) for h, v in zip(here, logs)]
    total = sum(scales)
    some = total > 0.0
    summed = sum(s * p[:, :128] for s, p in zip(scales, states))
    safe = jnp.where(some, total, 1.0)
    log = jnp.where(some, top + jnp.log(safe), ABSENT)
    out_ref[0, :step, :] = (summed / safe).astype(BF)
    terms = term_lanes(log, step).astype(F32)
    out_ref[0, step:, :] = terms_to_lines(terms, step // 32).reshape(step // 32, 128).astype(BF)


def home_rows(own, idx, home, width, before=None):
    columns, count = idx.shape
    quarters = 4
    step = count // quarters
    args = [own, idx.reshape(columns, quarters, step).transpose(1, 0, 2)]
    specs = [pl.BlockSpec((1, columns, step), lambda i, o: (i, 0, 0))]
    if before is None:
        kernel = home_kernel
        out_spec = pl.BlockSpec((2, step, 256), lambda i, o: (0, i, 0))
        out_shape = jax.ShapeDtypeStruct((2, count, 256), BF)
    else:
        kernel = last_kernel
        args.append(before)
        specs.append(pl.BlockSpec((2, step, 256), lambda i, o: (0, i, 0)))
        out_spec = pl.BlockSpec((1, step + step // 32, 128), lambda i, o: (i, 0, 0))
        out_shape = jax.ShapeDtypeStruct((quarters, step + step // 32, 128), BF)
    return pl.pallas_call(
        functools.partial(kernel, width),
        grid_spec=pltpu.PrefetchScalarGridSpec(
            num_scalar_prefetch=1,
            grid=(quarters,),
            in_specs=specs + [whole(h.shape) for h in home],
            out_specs=out_spec,
            scratch_shapes=[pltpu.VMEM((64 * width, 256), BF)],
        ),
        out_shape=out_shape,
        compiler_params=params(),
        name="home_rows",
    )(*args, *[in_hbm(h) for h in home])


def finish_kernel(m_ref, w_ref, out_ref):
    rows = out_ref.shape[0]
    logs = []
    for i in range(4):
        line = m_ref[i, rows:, :].astype(F32).reshape(rows // 32, 1, 128)
        terms = lines_to_terms(line)
        logs.append(terms[:, 0:1] + terms[:, 1:2] + terms[:, 2:3])
    top = functools.reduce(jnp.maximum, logs)
    scales = [jnp.exp(v - top) for v in logs]
    total = sum(scales)
    summed = sum(s * m_ref[i, :rows, :].astype(F32) for i, s in enumerate(scales))
    blended = (summed / total).astype(BF)
    out_ref[...] = jnp.dot(blended, w_ref[...], preferred_element_type=F32).astype(BF)


def finish(merged, w_out):
    parts, rows, _ = merged.shape
    rows -= rows // 33
    return pl.pallas_call(
        finish_kernel,
        in_specs=[whole(merged.shape), whole(w_out.shape)],
        out_specs=whole((rows, w_out.shape[1])),
        grid=(1,),
        out_shape=jax.ShapeDtypeStruct((rows, w_out.shape[1]), BF),
        compiler_params=params(),
        name="finish",
    )(merged, w_out)


def send_places(own_slots, other_slots, width):
    zl, zh = lax.axis_index("zl"), lax.axis_index("zh")
    late = lax.axis_index(PLANE) >= 8
    places, mine = [], []
    for shift in (0, jnp.where(late, -2, 2), 1, -1):
        own = ((zh * 4 + zl + shift + 8) & 7) // 4 == zh
        slot = jnp.where(own, own_slots, other_slots)
        hit = (slot >> 10) == ((zl + shift + 8) & 3)
        places.append(jnp.where(hit, ((slot >> 6) & 15) * width + (slot & 63), -1))
        mine.append(own)
    return jnp.stack(places), jnp.stack(mine).astype(jnp.int32)


def take_places(taken, width):
    away = (lax.axis_index("zl") - (taken >> 10)) & 3
    group = jnp.where(away == 1, 2, jnp.where(away == 2, 1, away))
    source = (taken >> 6) & 15
    at = taken & 63
    by_group = (group * 16 + source) * width + at
    odd = (32 + source * 2 + group - 2) * width + at
    return jnp.where(group < 2, by_group, odd), by_group


def body(x, w_qk, w_v, w_out, slots, taken, looks):
    count = slots.shape[1]
    peers = lax.axis_size(SEQ)
    width = 2 * count // peers
    blocks = count // BLOCK
    tail = count - 2 * BLOCK
    others = lax.ppermute(slots, "zh", [(0, 1), (1, 0)])
    packed = project(x, w_qk, w_v)
    mine = lax.axis_index(SEQ) * blocks + jnp.arange(blocks, dtype=jnp.int32)
    dist = (mine[None, :] - looks) % (peers * blocks)
    next_device = [(i, (i + 1) % peers) for i in range(peers)]
    sent_0, own_0 = send_places(slots[0], others[0], width)
    sent_1, own_1 = send_places(slots[1], others[1], width)
    spots_0, groups_0 = take_places(taken[0], width)
    spots_1, groups_1 = take_places(taken[1], width)

    def leave(out):
        even, up, down = out
        return plane(even), [ring(up, 1), ring(down, -1)]

    def arrive(half, rung):
        return [ring(half[:8, 1], 2), ring(half[8:, 1], -2)], plane(join(*rung))

    def turn(back):
        _, low, high, odd = back
        return [ring(low, -2), ring(high, 2)], plane(odd)

    def land(back, rung, half):
        even = plane(join(back[0], jnp.concatenate(rung)))
        return [even, ring(half[:, 0], -1), ring(half[:, 1], 1)]

    def sort_round(spots, rows):
        q_tail, kv_tail = sort_rows(spots[tail:], rows, 2 * BLOCK)
        halo = lax.ppermute(kv_tail, SEQ, next_device)
        q_head, kv_head = sort_rows(spots[:tail], rows, 3 * BLOCK)
        return q_head, q_tail, kv_head, kv_tail, halo

    out_0 = scatter_rows(sent_0, packed, width)
    out_0, packed = together((out_0, packed))
    half_0, rung_0 = leave(out_0)
    out_1 = scatter_rows(sent_1, packed, width)
    half_0, rung_0, out_1 = together((half_0, rung_0, out_1))
    far_0, odd_0 = arrive(half_0, rung_0)
    far_0, odd_0, out_1 = together((far_0, odd_0, out_1))
    half_1, rung_1 = leave(out_1)

    q_head, q_tail, kv_head, kv_tail, halo = sort_round(spots_0, [half_0, *far_0, odd_0])
    inner = attend_inner(dist[0], q_head, q_tail, kv_head, kv_tail)
    inner, q_head, kv_head, halo, half_1, rung_1 = together(
        (inner, q_head, kv_head, halo, half_1, rung_1)
    )
    far_1, odd_1 = arrive(half_1, rung_1)
    edge = attend_edge(dist[0], q_head, kv_head, halo)
    back_0 = back_rows(groups_0[None], edge, inner, width)
    back_0, far_1, odd_1 = together((back_0, far_1, odd_1))
    rung_0, half_0 = turn(back_0)

    q_head, q_tail, kv_head, kv_tail, halo = sort_round(spots_1, [half_1, *far_1, odd_1])
    inner = attend_inner(dist[1], q_head, q_tail, kv_head, kv_tail)
    inner, q_head, kv_head, halo, half_0, rung_0 = together(
        (inner, q_head, kv_head, halo, half_0, rung_0)
    )
    home_0 = land(back_0, rung_0, half_0)
    edge = attend_edge(dist[1], q_head, kv_head, halo)
    back_1 = back_rows(groups_1[None], edge, inner, width)
    home_0, back_1 = together((home_0, back_1))
    rung_1, half_1 = together(turn(back_1))
    home_1 = land(back_1, rung_1, half_1)

    before = home_rows(own_0, sent_0, home_0, width)
    state = home_rows(own_1, sent_1, home_1, width, before)
    merged = lax.all_to_all(state, ROUND, 0, 0, tiled=True)
    return finish(merged, w_out)


def solution(mesh):
    fine = Mesh(mesh.devices.reshape(4, 4, 4, 2, 2), SEQ + ROUND)
    in_specs = (P(SEQ, None), P(), P(), P()) + (P(ROUND, SEQ),) * 3
    return jax.shard_map(
        body, mesh=fine, in_specs=in_specs, out_specs=P(SEQ + ROUND, None), check_vma=False
    )
```

```python
import functools

import jax
import jax.numpy as jnp
from jax import lax
from jax.experimental import pallas as pl
from jax.experimental.pallas import tpu as pltpu
from jax.sharding import Mesh
from jax.sharding import PartitionSpec as P

BLOCK = 256
MASKED = -1000000000.0
SEQ = ("zl", "x", "y")
PLANE = ("x", "y")
ROUND = ("zh", "c")
BF = jnp.bfloat16
F32 = jnp.float32
VMEM_BYTES = 48 * 1024 * 1024


def params(n=1):
    return pltpu.CompilerParams(
        dimension_semantics=("arbitrary",) * n, vmem_limit_bytes=VMEM_BYTES
    )


def whole(shape):
    return pl.BlockSpec(shape, lambda *_: (0,) * len(shape))


def one_hot(a, b):
    return jnp.where(a == b, 1.0, 0.0).astype(BF)


def column(row):
    return jnp.transpose(jnp.broadcast_to(row, (8, row.shape[1])))[:, :1]


def in_hbm(v):
    return pltpu.with_memory_space_constraint(v, pltpu.HBM)


def project_kernel(x_ref, wqk_ref, wv_ref, out_ref, w_ref):
    @pl.when(pl.program_id(0) == 0)
    def _():
        w_ref[:, :128] = wqk_ref[...]
        w_ref[:, 128:] = wv_ref[...]

    out_ref[...] = jnp.dot(x_ref[...], w_ref[...], preferred_element_type=F32).astype(BF)


def project(x, w_qk, w_v):
    rows, model = x.shape
    step = 512
    return pl.pallas_call(
        project_kernel,
        grid=(rows // step,),
        in_specs=[
            pl.BlockSpec((step, model), lambda i: (i, 0)),
            whole(w_qk.shape),
            whole(w_v.shape),
        ],
        out_specs=pl.BlockSpec((step, 256), lambda i: (i, 0)),
        out_shape=jax.ShapeDtypeStruct((rows, 256), BF),
        scratch_shapes=[pltpu.VMEM((model, 256), BF)],
        compiler_params=params(),
        name="project",
    )(in_hbm(x), in_hbm(w_qk), in_hbm(w_v))


def ring(value, shift):
    def at(z):
        return (z % 4) * 2 + z // 4

    route = [(at(z), at((z + shift) % 8)) for z in range(8)]
    return lax.ppermute(value, ("zl", "zh"), route)


def join(first, second):
    return jnp.stack([first, second], axis=1)


def plane(joint):
    return lax.all_to_all(joint, PLANE, 0, 0, tiled=True)


together = lax.optimization_barrier


def scatter_kernel(idx_ref, rows_ref, *out_refs):
    peers, _, width, lanes = out_refs[0].shape[:2] + out_refs[0].shape[-2:]
    group = pl.program_id(1)
    place = lax.broadcasted_iota(jnp.int32, (peers * width, rows_ref.shape[0]), 0)
    hot = one_hot(idx_ref[0, pl.ds(group, 1), :], place)
    got = jnp.dot(hot, rows_ref[...], preferred_element_type=F32)
    got = got.astype(BF).reshape(peers, width, lanes)
    if len(out_refs) == 1:
        out_refs[0][:, 0, 0] = got
        return
    for g, ref in enumerate(out_refs):

        @pl.when(group == g)
        def _(ref=ref):
            ref[:, 0] = got


def scatter_rows(idx, rows, width, even):
    rounds, groups, count = idx.shape
    if even:
        shapes = [(16, groups, rounds, width, 256)]
        specs = [pl.BlockSpec((16, 1, 1, width, 256), lambda r, g: (0, g, r, 0, 0))]
    else:
        shapes = [(16, rounds, width, 256)] * groups
        specs = [pl.BlockSpec((16, 1, width, 256), lambda r, g: (0, r, 0, 0))] * groups
    return pl.pallas_call(
        scatter_kernel,
        grid=(rounds, groups),
        in_specs=[pl.BlockSpec((1, groups, count), lambda r, g: (r, 0, 0)), whole(rows.shape)],
        out_specs=specs,
        out_shape=[pltpu.HBM(v, BF) for v in shapes],
        compiler_params=params(2),
        name="scatter_rows",
    )(idx, rows)


def sort_kernel(idx_ref, *refs):
    (*row_refs, q_ref, kv_ref) = refs
    col = column(idx_ref[0, 0])
    got, base = 0.0, 0
    for ref in row_refs:
        rows = ref[...].reshape(-1, 256)
        n = rows.shape[0]
        place = lax.broadcasted_iota(jnp.int32, (q_ref.shape[1], n), 1) + base
        got += jnp.dot(one_hot(col, place), rows, preferred_element_type=F32)
        base += n
    qk = got[:, :128]
    keys = qk * lax.rsqrt(jnp.sum(qk * qk, axis=-1, keepdims=True) + 1e-06)
    q_ref[0] = qk.astype(BF)
    kv_ref[0, :, :128] = keys.astype(BF)
    kv_ref[0, :, 128:] = got[:, 128:].astype(BF)


def sort_rows(idx, even, low, high, odd, step):
    rounds, count = idx.shape
    blocks = count // step
    peers, _, _, width, lanes = even.shape
    four = lambda r, b: (0, r, 0, 0)
    five = lambda r, b: (0, 0, r, 0, 0)
    return pl.pallas_call(
        sort_kernel,
        grid=(rounds, blocks),
        in_specs=[
            pl.BlockSpec((1, 1, 1, step), lambda r, b: (r, b, 0, 0)),
            pl.BlockSpec((peers, 1, 1, width, lanes), five),
            pl.BlockSpec((peers // 2, 1, width, lanes), four),
            pl.BlockSpec((peers // 2, 1, width, lanes), four),
            pl.BlockSpec((peers, 2, 1, width, lanes), five),
        ],
        out_specs=[
            pl.BlockSpec((1, step, 128), lambda r, b: (r, b, 0)),
            pl.BlockSpec((1, step, 256), lambda r, b: (r, b, 0)),
        ],
        out_shape=[
            jax.ShapeDtypeStruct((rounds, count, 128), BF),
            jax.ShapeDtypeStruct((rounds, count, 256), BF),
        ],
        compiler_params=params(2),
        name="sort_rows",
    )(idx.reshape(rounds, blocks, 1, step), even, low, high, odd)


def terms_to_lines(terms, groups):
    terms = terms.reshape(groups, 32, 128)
    slot = lax.broadcasted_iota(jnp.int32, terms.shape, 1)
    lane = lax.broadcasted_iota(jnp.int32, terms.shape, 2) % 32
    return jnp.sum(jnp.where(slot == lane, terms, 0.0), axis=1, keepdims=True)


def lines_to_terms(line):
    n = line.shape[0]
    shape = (n, 32, 128)
    slot = lax.broadcasted_iota(jnp.int32, shape, 1)
    lane = lax.broadcasted_iota(jnp.int32, shape, 2) % 32
    spread = jnp.where(slot == lane, line, 0.0).reshape(n * 32, 128).astype(BF)
    group = lax.broadcasted_iota(jnp.int32, (128, 128), 0) // 32
    pick = one_hot(group, lax.broadcasted_iota(jnp.int32, (128, 128), 1))
    return jnp.dot(spread, pick, preferred_element_type=F32)


def three_terms(v):
    hi = v.astype(BF).astype(F32)
    mid = (v - hi).astype(BF).astype(F32)
    lo = v - hi - mid
    return hi, mid, lo


def term_lanes(v, rows):
    hi, mid, lo = three_terms(v)
    group = lax.broadcasted_iota(jnp.int32, (rows, 128), 1) // 32
    return jnp.where(
        group == 0, hi, jnp.where(group == 1, mid, jnp.where(group == 2, lo, 1.0))
    ).astype(BF)


def attend_block(q, own, behind, out_ref):
    nt = (((1,), (1,)), ((), ()))
    s1 = lax.dot_general(q, own[:, :128], nt, preferred_element_type=F32)
    s2 = lax.dot_general(q, behind[:, :128], nt, preferred_element_type=F32)
    r = lax.broadcasted_iota(jnp.int32, (BLOCK, BLOCK), 0)
    k = lax.broadcasted_iota(jnp.int32, (BLOCK, BLOCK), 1)
    s1 = jnp.where(r == k, MASKED, s1)
    top = jnp.maximum(
        jnp.max(s1, axis=-1, keepdims=True), jnp.max(s2, axis=-1, keepdims=True)
    )
    e1 = jnp.exp(s1 - top)
    e2 = jnp.exp(s2 - top)
    total = jnp.sum(e1, axis=-1, keepdims=True) + jnp.sum(e2, axis=-1, keepdims=True)
    o = jnp.dot(e1.astype(BF), own[:, 128:], preferred_element_type=F32) + jnp.dot(
        e2.astype(BF), behind[:, 128:], preferred_element_type=F32
    )
    out_ref[0, :, :128] = (o / total).astype(BF)
    out_ref[0, :, 128:] = term_lanes(top + jnp.log(total), BLOCK)


def inner_kernel(dist_ref, qh_ref, qt_ref, kvh_ref, kvt_ref, out_ref, q_ref, kv_ref):
    head = kvh_ref.shape[1]

    @pl.when(pl.program_id(1) == 0)
    def _():
        q_ref[:head] = qh_ref[0]
        q_ref[head:] = qt_ref[0]
        kv_ref[:head] = kvh_ref[0]
        kv_ref[head:] = kvt_ref[0]

    def block(ref, c):
        return ref[pl.ds(pl.multiple_of(c * BLOCK, BLOCK), BLOCK), :]

    c = pl.program_id(1) + 2
    at = c - dist_ref[pl.program_id(0), c]
    attend_block(block(q_ref, c), block(kv_ref, c), block(kv_ref, at), out_ref)


def edge_kernel(dist_ref, q_ref, kv_ref, halo_ref, out_ref):
    c = pl.program_id(1)
    own = kv_ref[0, pl.ds(pl.multiple_of(c * BLOCK, BLOCK), BLOCK), :]
    at = c + 2 - dist_ref[pl.program_id(0), c]
    before = halo_ref[0, pl.ds(pl.multiple_of(jnp.minimum(at, 1) * BLOCK, BLOCK), BLOCK), :]
    behind = jnp.where(at < 2, before, kv_ref[0, :BLOCK, :])
    attend_block(q_ref[0], own, behind, out_ref)


def of_round(shape):
    return pl.BlockSpec((1,) + shape[1:], lambda r, b, d: (r, 0, 0))


def attend_inner(dist, q_head, q_tail, kv_head, kv_tail):
    rounds = q_head.shape[0]
    count = q_head.shape[1] + q_tail.shape[1]
    blocks = count // BLOCK - 2
    return pl.pallas_call(
        inner_kernel,
        grid_spec=pltpu.PrefetchScalarGridSpec(
            num_scalar_prefetch=1,
            grid=(rounds, blocks),
            in_specs=[of_round(v.shape) for v in (q_head, q_tail, kv_head, kv_tail)],
            out_specs=pl.BlockSpec((1, BLOCK, 256), lambda r, b, d: (r, b, 0)),
            scratch_shapes=[pltpu.VMEM((count, 128), BF), pltpu.VMEM((count, 256), BF)],
        ),
        out_shape=jax.ShapeDtypeStruct((rounds, blocks * BLOCK, 256), BF),
        compiler_params=params(2),
        name="attend_inner",
    )(dist, q_head, q_tail, kv_head, kv_tail)


def attend_edge(dist, q, kv, halo):
    rounds = q.shape[0]
    return pl.pallas_call(
        edge_kernel,
        grid_spec=pltpu.PrefetchScalarGridSpec(
            num_scalar_prefetch=1,
            grid=(rounds, 2),
            in_specs=[
                pl.BlockSpec((1, BLOCK, 128), lambda r, b, d: (r, b, 0)),
                of_round((rounds, 2 * BLOCK, 256)),
                of_round(halo.shape),
            ],
            out_specs=pl.BlockSpec((1, BLOCK, 256), lambda r, b, d: (r, b, 0)),
        ),
        out_shape=jax.ShapeDtypeStruct((rounds, 2 * BLOCK, 256), BF),
        compiler_params=params(2),
        name="attend_edge",
    )(dist, q, kv, halo)


def back_kernel(first_group, idx_ref, edge_ref, inner_ref, *out_refs):
    width, peers = out_refs[0].shape[-2] - 8, 16
    n = peers * width
    group = pl.program_id(1)
    idx = idx_ref[0] - (first_group + group) * n
    got = 0.0
    first = 0
    for ref in (edge_ref, inner_ref):
        count = ref.shape[1]
        place = lax.broadcasted_iota(jnp.int32, (n, count), 0)
        hot = one_hot(idx[:, first : first + count], place)
        got += jnp.dot(hot, ref[0], preferred_element_type=F32)
        first += count
    lines = terms_to_lines(got[:, 128:], n // 32).reshape(peers, width // 32, 1, 128)
    row = lax.broadcasted_iota(jnp.int32, (peers, 8, 128), 1)
    tail = jnp.zeros((peers, 8, 128), F32)
    for part in range(width // 32):
        tail = jnp.where(row == part, lines[:, part], tail)
    tail = tail.astype(BF)
    got = got[:, :128].astype(BF).reshape(peers, width, 128)

    def store(ref, at):
        ref[:, :width, :] = got[at]
        ref[:, width:, :] = tail[at]

    every, half = slice(None), peers // 2
    if len(out_refs) == 1:
        store(out_refs[0].at[:, 0, 0], every)
        return
    near_ref, low_ref, high_ref = out_refs

    @pl.when(group == 0)
    def _():
        store(near_ref.at[:, 0], every)

    @pl.when(group == 1)
    def _():
        store(low_ref.at[:, 0], slice(0, half))
        store(high_ref.at[:, 0], slice(half, peers))


def back_rows(idx, edge, inner, width, even):
    rounds = idx.shape[0]
    ext = width + 8
    if even:
        shapes = [(n, rounds, ext, 128) for n in (16, 8, 8)]
        specs = [pl.BlockSpec((v[0], 1, ext, 128), lambda r, g: (0, r, 0, 0)) for v in shapes]
    else:
        shapes = [(16, 2, rounds, ext, 128)]
        specs = [pl.BlockSpec((16, 1, 1, ext, 128), lambda r, g: (0, g, r, 0, 0))]
    one = lambda v: pl.BlockSpec((1,) + v.shape[1:], lambda r, g: (r, 0, 0))
    return pl.pallas_call(
        functools.partial(back_kernel, 0 if even else 2),
        grid=(rounds, 2),
        in_specs=[one(idx), one(edge), one(inner)],
        out_specs=specs,
        out_shape=[pltpu.HBM(v, BF) for v in shapes],
        compiler_params=params(2),
        name="back_rows",
    )(idx, edge, inner)


ABSENT = -1e30


def fill_home(x_ref, width, blocks):
    row = 0
    for block in blocks:
        size = block.shape[0] * width
        x_ref[row : row + size, :128] = block[:, :width, :].reshape(size, 128)
        tail = block[:, width:, :].astype(F32)
        lines = jnp.concatenate(
            [tail[:, p : p + 1][:, None] for p in range(width // 32)], axis=1
        ).reshape(size // 32, 1, 128)
        x_ref[row : row + size, 128:] = lines_to_terms(lines).astype(BF)
        row += size


def gather_home(own_ref, cols, x_ref, width):
    near, far = 0.0, 0.0
    size = 16 * width
    place = lax.broadcasted_iota(jnp.int32, (cols.shape[0], size), 1)
    for g in range(4):
        hot = one_hot(cols[:, g : g + 1], place)
        got = jnp.dot(hot, x_ref[g * size : (g + 1) * size], preferred_element_type=F32)
        if g == 0:
            near = got
        else:
            mine = own_ref[g] == 1
            near += jnp.where(mine, got, 0.0)
            far += jnp.where(mine, 0.0, got)
    return [near, far]


def home_kernel(width, own_ref, idx_ref, even_ref, up_ref, down_ref, out_ref, x_ref):
    rounds = even_ref.shape[2]

    @pl.when(pl.program_id(0) == 0)
    def _():
        for r in range(rounds):
            blocks = [even_ref.at[:, 0, r], even_ref.at[:, 1, r], up_ref.at[:, r], down_ref.at[:, r]]
            fill_home(x_ref.at[r], width, blocks)

    step = idx_ref.shape[2]
    cols = jnp.transpose(idx_ref[0])
    states = []
    for r in range(rounds):
        states += gather_home(own_ref, cols[:, 4 * r : 4 * r + 4], x_ref.at[r], width)
    here = [s[:, 131:132] > 0.5 for s in states]
    logs = [
        jnp.where(h, s[:, 128:129] + s[:, 129:130] + s[:, 130:131], ABSENT)
        for h, s in zip(here, states)
    ]
    top = functools.reduce(jnp.maximum, logs)
    scales = [jnp.where(h, jnp.exp(v - top), 0.0) for h, v in zip(here, logs)]
    total = sum(scales)
    some = total > 0.0
    summed = sum(s * p[:, :128] for s, p in zip(scales, states))
    safe = jnp.where(some, total, 1.0)
    log = jnp.where(some, top + jnp.log(safe), ABSENT)
    out_ref[0, :step, :] = (summed / safe).astype(BF)
    terms = term_lanes(log, step).astype(F32)
    out_ref[0, step:, :] = terms_to_lines(terms, step // 32).reshape(step // 32, 128).astype(BF)


def home_rows(own, idx, even, up, down, width):
    rounds, groups, count = idx.shape
    quarters = 4
    step = count // quarters
    columns = rounds * groups
    idx = idx.reshape(columns, quarters, step).transpose(1, 0, 2)
    return pl.pallas_call(
        functools.partial(home_kernel, width),
        grid_spec=pltpu.PrefetchScalarGridSpec(
            num_scalar_prefetch=1,
            grid=(quarters,),
            in_specs=[pl.BlockSpec((1, columns, step), lambda i, o: (i, 0, 0))]
            + [whole(v.shape) for v in (even, up, down)],
            out_specs=pl.BlockSpec((1, step + step // 32, 128), lambda i, o: (i, 0, 0)),
            scratch_shapes=[pltpu.VMEM((rounds, 64 * width, 256), BF)],
        ),
        out_shape=jax.ShapeDtypeStruct((quarters, step + step // 32, 128), BF),
        compiler_params=params(),
        name="home_rows",
    )(own, idx, even, up, down)


def finish_kernel(m_ref, w_ref, out_ref):
    rows = out_ref.shape[0]
    logs = []
    for i in range(4):
        line = m_ref[i, rows:, :].astype(F32).reshape(rows // 32, 1, 128)
        terms = lines_to_terms(line)
        logs.append(terms[:, 0:1] + terms[:, 1:2] + terms[:, 2:3])
    top = functools.reduce(jnp.maximum, logs)
    scales = [jnp.exp(v - top) for v in logs]
    total = sum(scales)
    summed = sum(s * m_ref[i, :rows, :].astype(F32) for i, s in enumerate(scales))
    blended = (summed / total).astype(BF)
    out_ref[...] = jnp.dot(blended, w_ref[...], preferred_element_type=F32).astype(BF)


def finish(merged, w_out):
    parts, rows, _ = merged.shape
    rows -= rows // 33
    return pl.pallas_call(
        finish_kernel,
        in_specs=[whole(merged.shape), whole(w_out.shape)],
        out_specs=whole((rows, w_out.shape[1])),
        grid=(1,),
        out_shape=jax.ShapeDtypeStruct((rows, w_out.shape[1]), BF),
        compiler_params=params(),
        name="finish",
    )(merged, w_out)


def send_places(own_slots, other_slots, width):
    zl, zh = lax.axis_index("zl"), lax.axis_index("zh")
    late = lax.axis_index(PLANE) >= 8
    group = jnp.arange(4, dtype=jnp.int32)
    shift = jnp.where(group == 0, 0, jnp.where(group == 1, jnp.where(late, -2, 2), 5 - 2 * group))
    own = ((zh * 4 + zl + shift + 8) & 7) // 4 == zh
    slot = jnp.where(own[:, None], own_slots[:, None], other_slots[:, None])
    hit = (slot >> 10) == ((zl + shift + 8) & 3)[:, None]
    return jnp.where(hit, ((slot >> 6) & 15) * width + (slot & 63), -1), own.astype(jnp.int32)


def take_places(taken, width):
    away = (lax.axis_index("zl") - (taken >> 10)) & 3
    group = jnp.where(away == 1, 2, jnp.where(away == 2, 1, away))
    source = (taken >> 6) & 15
    at = taken & 63
    by_group = (group * 16 + source) * width + at
    odd = (32 + source * 2 + group - 2) * width + at
    return jnp.where(group < 2, by_group, odd), by_group


def body(x, w_qk, w_v, w_out, slots, taken, looks):
    count = slots.shape[1]
    peers = lax.axis_size(SEQ)
    width = 2 * count // peers
    blocks = count // BLOCK
    tail = count - 2 * BLOCK
    others = lax.ppermute(slots, "zh", [(0, 1), (1, 0)])
    packed = project(x, w_qk, w_v)
    mine = lax.axis_index(SEQ) * blocks + jnp.arange(blocks, dtype=jnp.int32)
    dist = (mine[None, :] - looks) % (peers * blocks)
    next_device = [(i, (i + 1) % peers) for i in range(peers)]
    sent, own = send_places(slots, others, width)
    spots, groups = take_places(taken, width)

    (even,) = scatter_rows(sent[:, :2], packed, width, True)
    even, packed = together((even, packed))
    half = plane(even)
    up, down = scatter_rows(sent[:, 2:], packed, width, False)
    half, up, down = together((half, ring(up, 1), ring(down, -1)))
    rows = half, ring(half[:8, 1], 2), ring(half[8:, 1], -2), plane(join(up, down))
    rows = together(rows)

    q_tail, kv_tail = sort_rows(spots[:, tail:], *rows, 2 * BLOCK)
    halo = lax.ppermute(kv_tail, SEQ, next_device)
    q_head, kv_head = sort_rows(spots[:, :tail], *rows, 3 * BLOCK)
    inner = attend_inner(dist, q_head, q_tail, kv_head, kv_tail)
    edge = attend_edge(dist, q_head, kv_head, halo)

    (odd,) = back_rows(groups[:, None], edge, inner, width, False)
    odd, edge = together((odd, edge))
    half = plane(odd)
    near, low, high = back_rows(groups[:, None], edge, inner, width, True)
    half, low, high = together((half, ring(low, -2), ring(high, 2)))
    even = plane(join(near, jnp.concatenate([low, high])))
    state = home_rows(own, sent, even, ring(half[:, 0], -1), ring(half[:, 1], 1), width)
    merged = lax.all_to_all(state, ROUND, 0, 0, tiled=True)
    return finish(merged, w_out)


def solution(mesh):
    fine = Mesh(mesh.devices.reshape(4, 4, 4, 2, 2), SEQ + ROUND)
    in_specs = (P(SEQ, None), P(), P(), P()) + (P(ROUND, SEQ),) * 3
    return jax.shard_map(
        body, mesh=fine, in_specs=in_specs, out_specs=P(SEQ + ROUND, None), check_vma=False
    )
```

```python
import functools

import jax
import jax.numpy as jnp
from jax import lax
from jax.experimental import pallas as pl
from jax.experimental.pallas import tpu as pltpu
from jax.sharding import Mesh
from jax.sharding import PartitionSpec as P

BLOCK = 256
MASKED = -1000000000.0
SEQ = ("zl", "x", "y")
PLANE = ("x", "y")
ROUND = ("zh", "c")
BF = jnp.bfloat16
F32 = jnp.float32
VMEM_BYTES = 48 * 1024 * 1024


def params(n=1):
    return pltpu.CompilerParams(
        dimension_semantics=("arbitrary",) * n, vmem_limit_bytes=VMEM_BYTES
    )


def whole(shape):
    return pl.BlockSpec(shape, lambda *_: (0,) * len(shape))


def one_hot(a, b):
    return jnp.where(a == b, 1.0, 0.0).astype(BF)


def column(row):
    return jnp.transpose(jnp.broadcast_to(row, (8, row.shape[1])))[:, :1]


def in_hbm(v):
    return pltpu.with_memory_space_constraint(v, pltpu.HBM)


def project_kernel(x_ref, wqk_ref, wv_ref, out_ref, w_ref):
    @pl.when(pl.program_id(0) == 0)
    def _():
        w_ref[:, :128] = wqk_ref[...]
        w_ref[:, 128:] = wv_ref[...]

    out_ref[...] = jnp.dot(x_ref[...], w_ref[...], preferred_element_type=F32).astype(BF)


def project(x, w_qk, w_v):
    rows, model = x.shape
    step = 512
    return pl.pallas_call(
        project_kernel,
        grid=(rows // step,),
        in_specs=[
            pl.BlockSpec((step, model), lambda i: (i, 0)),
            whole(w_qk.shape),
            whole(w_v.shape),
        ],
        out_specs=pl.BlockSpec((step, 256), lambda i: (i, 0)),
        out_shape=jax.ShapeDtypeStruct((rows, 256), BF),
        scratch_shapes=[pltpu.VMEM((model, 256), BF)],
        compiler_params=params(),
        name="project",
    )(in_hbm(x), in_hbm(w_qk), in_hbm(w_v))


def ring(value, shift):
    def at(z):
        return (z % 4) * 2 + z // 4

    route = [(at(z), at((z + shift) % 8)) for z in range(8)]
    return lax.ppermute(value, ("zl", "zh"), route)


def join(first, second):
    return jnp.stack([first, second], axis=1)


def plane(joint):
    return lax.all_to_all(joint, PLANE, 0, 0, tiled=True)


together = lax.optimization_barrier


def scatter_kernel(idx_ref, rows_ref, *out_refs):
    peers, _, width, lanes = out_refs[0].shape[:2] + out_refs[0].shape[-2:]
    group = pl.program_id(1)
    place = lax.broadcasted_iota(jnp.int32, (peers * width, rows_ref.shape[0]), 0)
    hot = one_hot(idx_ref[0, pl.ds(group, 1), :], place)
    got = jnp.dot(hot, rows_ref[...], preferred_element_type=F32)
    got = got.astype(BF).reshape(peers, width, lanes)
    if len(out_refs) == 1:
        out_refs[0][:, 0, 0] = got
        return
    for g, ref in enumerate(out_refs):

        @pl.when(group == g)
        def _(ref=ref):
            ref[:, 0] = got


def scatter_rows(idx, rows, width, even):
    rounds, groups, count = idx.shape
    if even:
        shapes = [(16, groups, rounds, width, 256)]
        specs = [pl.BlockSpec((16, 1, 1, width, 256), lambda r, g: (0, g, r, 0, 0))]
    else:
        shapes = [(16, rounds, width, 256)] * groups
        specs = [pl.BlockSpec((16, 1, width, 256), lambda r, g: (0, r, 0, 0))] * groups
    return pl.pallas_call(
        scatter_kernel,
        grid=(rounds, groups),
        in_specs=[pl.BlockSpec((1, groups, count), lambda r, g: (r, 0, 0)), whole(rows.shape)],
        out_specs=specs,
        out_shape=[pltpu.HBM(v, BF) for v in shapes],
        compiler_params=params(2),
        name="scatter_rows",
    )(idx, rows)


def pick_rows(idx_ref, row_refs, base):
    col = column(idx_ref[0, 0])
    got = 0.0
    for ref in row_refs:
        rows = ref[...].reshape(-1, 256)
        n = rows.shape[0]
        place = lax.broadcasted_iota(jnp.int32, (col.shape[0], n), 1) + base
        got += jnp.dot(one_hot(col, place), rows, preferred_element_type=F32)
        base += n
    return got


def early_kernel(idx_ref, near_ref, low_ref, high_ref, out_ref):
    out_ref[0] = pick_rows(idx_ref, (near_ref, low_ref, high_ref), 0).astype(BF)


def early_rows(idx, even, low, high):
    rounds, count = idx.shape
    step = count // 2
    peers, _, _, width, lanes = even.shape
    four = lambda r, b: (0, r, 0, 0)
    return pl.pallas_call(
        early_kernel,
        grid=(rounds, 2),
        in_specs=[
            pl.BlockSpec((1, 1, 1, step), lambda r, b: (r, b, 0, 0)),
            pl.BlockSpec((peers, 1, 1, width, lanes), lambda r, b: (0, 0, r, 0, 0)),
            pl.BlockSpec((peers // 2, 1, width, lanes), four),
            pl.BlockSpec((peers // 2, 1, width, lanes), four),
        ],
        out_specs=pl.BlockSpec((1, step, 256), lambda r, b: (r, b, 0)),
        out_shape=pltpu.HBM((rounds, count, 256), BF),
        compiler_params=params(2),
        name="early_rows",
    )(idx.reshape(rounds, 2, 1, step), in_hbm(even), low, high)


def sort_kernel(idx_ref, early_ref, odd_ref, q_ref, kv_ref):
    n = odd_ref.shape[0] * odd_ref.shape[1] * odd_ref.shape[3]
    got = early_ref[0].astype(F32) + pick_rows(idx_ref, (odd_ref,), n)
    qk = got[:, :128]
    keys = qk * lax.rsqrt(jnp.sum(qk * qk, axis=-1, keepdims=True) + 1e-06)
    q_ref[0] = qk.astype(BF)
    kv_ref[0, :, :128] = keys.astype(BF)
    kv_ref[0, :, 128:] = got[:, 128:].astype(BF)


def sort_rows(idx, early, odd, first, step):
    rounds, count = idx.shape
    blocks = count // step
    peers, _, _, width, lanes = odd.shape
    return pl.pallas_call(
        sort_kernel,
        grid=(rounds, blocks),
        in_specs=[
            pl.BlockSpec((1, 1, 1, step), lambda r, b: (r, b, 0, 0)),
            pl.BlockSpec((1, step, 256), lambda r, b: (r, first // step + b, 0)),
            pl.BlockSpec((peers, 2, 1, width, lanes), lambda r, b: (0, 0, r, 0, 0)),
        ],
        out_specs=[
            pl.BlockSpec((1, step, 128), lambda r, b: (r, b, 0)),
            pl.BlockSpec((1, step, 256), lambda r, b: (r, b, 0)),
        ],
        out_shape=[
            jax.ShapeDtypeStruct((rounds, count, 128), BF),
            jax.ShapeDtypeStruct((rounds, count, 256), BF),
        ],
        compiler_params=params(2),
        name="sort_rows",
    )(idx.reshape(rounds, blocks, 1, step), in_hbm(early), in_hbm(odd))


def terms_to_lines(terms, groups):
    terms = terms.reshape(groups, 32, 128)
    slot = lax.broadcasted_iota(jnp.int32, terms.shape, 1)
    lane = lax.broadcasted_iota(jnp.int32, terms.shape, 2) % 32
    return jnp.sum(jnp.where(slot == lane, terms, 0.0), axis=1, keepdims=True)


def lines_to_terms(line):
    n = line.shape[0]
    shape = (n, 32, 128)
    slot = lax.broadcasted_iota(jnp.int32, shape, 1)
    lane = lax.broadcasted_iota(jnp.int32, shape, 2) % 32
    spread = jnp.where(slot == lane, line, 0.0).reshape(n * 32, 128).astype(BF)
    group = lax.broadcasted_iota(jnp.int32, (128, 128), 0) // 32
    pick = one_hot(group, lax.broadcasted_iota(jnp.int32, (128, 128), 1))
    return jnp.dot(spread, pick, preferred_element_type=F32)


def three_terms(v):
    hi = v.astype(BF).astype(F32)
    mid = (v - hi).astype(BF).astype(F32)
    lo = v - hi - mid
    return hi, mid, lo


def term_lanes(v, rows):
    hi, mid, lo = three_terms(v)
    group = lax.broadcasted_iota(jnp.int32, (rows, 128), 1) // 32
    return jnp.where(
        group == 0, hi, jnp.where(group == 1, mid, jnp.where(group == 2, lo, 1.0))
    ).astype(BF)


def attend_block(q, own, behind, out_ref):
    nt = (((1,), (1,)), ((), ()))
    s1 = lax.dot_general(q, own[:, :128], nt, preferred_element_type=F32)
    s2 = lax.dot_general(q, behind[:, :128], nt, preferred_element_type=F32)
    r = lax.broadcasted_iota(jnp.int32, (BLOCK, BLOCK), 0)
    k = lax.broadcasted_iota(jnp.int32, (BLOCK, BLOCK), 1)
    s1 = jnp.where(r == k, MASKED, s1)
    top = jnp.maximum(
        jnp.max(s1, axis=-1, keepdims=True), jnp.max(s2, axis=-1, keepdims=True)
    )
    e1 = jnp.exp(s1 - top)
    e2 = jnp.exp(s2 - top)
    total = jnp.sum(e1, axis=-1, keepdims=True) + jnp.sum(e2, axis=-1, keepdims=True)
    o = jnp.dot(e1.astype(BF), own[:, 128:], preferred_element_type=F32) + jnp.dot(
        e2.astype(BF), behind[:, 128:], preferred_element_type=F32
    )
    out_ref[0, :, :128] = (o / total).astype(BF)
    out_ref[0, :, 128:] = term_lanes(top + jnp.log(total), BLOCK)


def inner_kernel(dist_ref, qh_ref, qt_ref, kvh_ref, kvt_ref, out_ref, q_ref, kv_ref):
    head = kvh_ref.shape[1]

    @pl.when(pl.program_id(1) == 0)
    def _():
        q_ref[:head] = qh_ref[0]
        q_ref[head:] = qt_ref[0]
        kv_ref[:head] = kvh_ref[0]
        kv_ref[head:] = kvt_ref[0]

    def block(ref, c):
        return ref[pl.ds(pl.multiple_of(c * BLOCK, BLOCK), BLOCK), :]

    c = pl.program_id(1) + 2
    at = c - dist_ref[pl.program_id(0), c]
    attend_block(block(q_ref, c), block(kv_ref, c), block(kv_ref, at), out_ref)


def edge_kernel(dist_ref, q_ref, kv_ref, halo_ref, out_ref):
    c = pl.program_id(1)
    own = kv_ref[0, pl.ds(pl.multiple_of(c * BLOCK, BLOCK), BLOCK), :]
    at = c + 2 - dist_ref[pl.program_id(0), c]
    before = halo_ref[0, pl.ds(pl.multiple_of(jnp.minimum(at, 1) * BLOCK, BLOCK), BLOCK), :]
    behind = jnp.where(at < 2, before, kv_ref[0, :BLOCK, :])
    attend_block(q_ref[0], own, behind, out_ref)


def of_round(shape):
    return pl.BlockSpec((1,) + shape[1:], lambda r, b, d: (r, 0, 0))


def attend_inner(dist, q_head, q_tail, kv_head, kv_tail):
    rounds = q_head.shape[0]
    count = q_head.shape[1] + q_tail.shape[1]
    blocks = count // BLOCK - 2
    return pl.pallas_call(
        inner_kernel,
        grid_spec=pltpu.PrefetchScalarGridSpec(
            num_scalar_prefetch=1,
            grid=(rounds, blocks),
            in_specs=[of_round(v.shape) for v in (q_head, q_tail, kv_head, kv_tail)],
            out_specs=pl.BlockSpec((1, BLOCK, 256), lambda r, b, d: (r, b, 0)),
            scratch_shapes=[pltpu.VMEM((count, 128), BF), pltpu.VMEM((count, 256), BF)],
        ),
        out_shape=jax.ShapeDtypeStruct((rounds, blocks * BLOCK, 256), BF),
        compiler_params=params(2),
        name="attend_inner",
    )(dist, q_head, q_tail, kv_head, kv_tail)


def attend_edge(dist, q, kv, halo):
    rounds = q.shape[0]
    return pl.pallas_call(
        edge_kernel,
        grid_spec=pltpu.PrefetchScalarGridSpec(
            num_scalar_prefetch=1,
            grid=(rounds, 2),
            in_specs=[
                pl.BlockSpec((1, BLOCK, 128), lambda r, b, d: (r, b, 0)),
                of_round((rounds, 2 * BLOCK, 256)),
                of_round(halo.shape),
            ],
            out_specs=pl.BlockSpec((1, BLOCK, 256), lambda r, b, d: (r, b, 0)),
        ),
        out_shape=jax.ShapeDtypeStruct((rounds, 2 * BLOCK, 256), BF),
        compiler_params=params(2),
        name="attend_edge",
    )(dist, q, kv, halo)


def back_kernel(first_group, idx_ref, edge_ref, inner_ref, *out_refs):
    width, peers = out_refs[0].shape[-2] - 8, 16
    n = peers * width
    group = pl.program_id(1)
    idx = idx_ref[0] - (first_group + group) * n
    got = 0.0
    first = 0
    for ref in (edge_ref, inner_ref):
        count = ref.shape[1]
        place = lax.broadcasted_iota(jnp.int32, (n, count), 0)
        hot = one_hot(idx[:, first : first + count], place)
        got += jnp.dot(hot, ref[0], preferred_element_type=F32)
        first += count
    lines = terms_to_lines(got[:, 128:], n // 32).reshape(peers, width // 32, 1, 128)
    row = lax.broadcasted_iota(jnp.int32, (peers, 8, 128), 1)
    tail = jnp.zeros((peers, 8, 128), F32)
    for part in range(width // 32):
        tail = jnp.where(row == part, lines[:, part], tail)
    tail = tail.astype(BF)
    got = got[:, :128].astype(BF).reshape(peers, width, 128)

    def store(ref, at):
        ref[:, :width, :] = got[at]
        ref[:, width:, :] = tail[at]

    every, half = slice(None), peers // 2
    if len(out_refs) == 1:
        store(out_refs[0].at[:, 0, 0], every)
        return
    near_ref, low_ref, high_ref = out_refs

    @pl.when(group == 0)
    def _():
        store(near_ref.at[:, 0], every)

    @pl.when(group == 1)
    def _():
        store(low_ref.at[:, 0], slice(0, half))
        store(high_ref.at[:, 0], slice(half, peers))


def back_rows(idx, edge, inner, width, even):
    rounds = idx.shape[0]
    ext = width + 8
    if even:
        shapes = [(n, rounds, ext, 128) for n in (16, 8, 8)]
        specs = [pl.BlockSpec((v[0], 1, ext, 128), lambda r, g: (0, r, 0, 0)) for v in shapes]
    else:
        shapes = [(16, 2, rounds, ext, 128)]
        specs = [pl.BlockSpec((16, 1, 1, ext, 128), lambda r, g: (0, g, r, 0, 0))]
    one = lambda v: pl.BlockSpec((1,) + v.shape[1:], lambda r, g: (r, 0, 0))
    return pl.pallas_call(
        functools.partial(back_kernel, 0 if even else 2),
        grid=(rounds, 2),
        in_specs=[one(idx), one(edge), one(inner)],
        out_specs=specs,
        out_shape=[pltpu.HBM(v, BF) for v in shapes],
        compiler_params=params(2),
        name="back_rows",
    )(idx, edge, inner)


ABSENT = -1e30


def fill_home(x_ref, width, blocks):
    row = 0
    for block in blocks:
        size = block.shape[0] * width
        x_ref[row : row + size, :128] = block[:, :width, :].reshape(size, 128)
        tail = block[:, width:, :].astype(F32)
        lines = jnp.concatenate(
            [tail[:, p : p + 1][:, None] for p in range(width // 32)], axis=1
        ).reshape(size // 32, 1, 128)
        x_ref[row : row + size, 128:] = lines_to_terms(lines).astype(BF)
        row += size


def gather_home(own_ref, cols, x_ref, width, groups):
    near, far = 0.0, 0.0
    size = 16 * width
    place = lax.broadcasted_iota(jnp.int32, (cols.shape[0], size), 1)
    for at, g in enumerate(groups):
        hot = one_hot(cols[:, at : at + 1], place)
        got = jnp.dot(hot, x_ref[at * size : (at + 1) * size], preferred_element_type=F32)
        mine = own_ref[g] == 1
        near += jnp.where(mine, got, 0.0)
        far += jnp.where(mine, 0.0, got)
    return [near, far]


def odd_home_kernel(width, own_ref, idx_ref, up_ref, down_ref, out_ref, x_ref):
    rounds = up_ref.shape[1]

    @pl.when(pl.program_id(0) == 0)
    def _():
        for r in range(rounds):
            fill_home(x_ref.at[r], width, [up_ref.at[:, r], down_ref.at[:, r]])

    cols = jnp.transpose(idx_ref[0])
    for r in range(rounds):
        states = gather_home(own_ref, cols[:, 2 * r : 2 * r + 2], x_ref.at[r], width, (2, 3))
        for at, state in enumerate(states):
            out_ref[2 * r + at] = state.astype(BF)


def home_kernel(width, own_ref, idx_ref, odd_ref, even_ref, out_ref, x_ref):
    rounds = even_ref.shape[2]

    @pl.when(pl.program_id(0) == 0)
    def _():
        for r in range(rounds):
            fill_home(x_ref.at[r], width, [even_ref.at[:, 0, r], even_ref.at[:, 1, r]])

    step = idx_ref.shape[2]
    cols = jnp.transpose(idx_ref[0])
    states = []
    for r in range(rounds):
        states += gather_home(own_ref, cols[:, 2 * r : 2 * r + 2], x_ref.at[r], width, (0, 1))
    states = [s + odd_ref[at].astype(F32) for at, s in enumerate(states)]
    here = [s[:, 131:132] > 0.5 for s in states]
    logs = [
        jnp.where(h, s[:, 128:129] + s[:, 129:130] + s[:, 130:131], ABSENT)
        for h, s in zip(here, states)
    ]
    top = functools.reduce(jnp.maximum, logs)
    scales = [jnp.where(h, jnp.exp(v - top), 0.0) for h, v in zip(here, logs)]
    total = sum(scales)
    some = total > 0.0
    summed = sum(s * p[:, :128] for s, p in zip(scales, states))
    safe = jnp.where(some, total, 1.0)
    log = jnp.where(some, top + jnp.log(safe), ABSENT)
    out_ref[0, :step, :] = (summed / safe).astype(BF)
    terms = term_lanes(log, step).astype(F32)
    out_ref[0, step:, :] = terms_to_lines(terms, step // 32).reshape(step // 32, 128).astype(BF)


def home_rows(own, idx, width, homes, odd=None):
    rounds, groups, count = idx.shape
    quarters = 4
    step = count // quarters
    columns = rounds * groups
    idx = idx.reshape(columns, quarters, step).transpose(1, 0, 2)
    partial = pl.BlockSpec((2 * rounds, step, 256), lambda i, o: (0, i, 0))
    specs = [pl.BlockSpec((1, columns, step), lambda i, o: (i, 0, 0))]
    if odd is None:
        kernel, out_spec = odd_home_kernel, partial
        out_shape = pltpu.HBM((2 * rounds, count, 256), BF)
    else:
        kernel = home_kernel
        odd = in_hbm(odd)
        homes = (odd, *homes)
        out_spec = pl.BlockSpec((1, step + step // 32, 128), lambda i, o: (i, 0, 0))
        out_shape = jax.ShapeDtypeStruct((quarters, step + step // 32, 128), BF)
    for v in homes:
        specs.append(partial if v is odd else whole(v.shape))
    return pl.pallas_call(
        functools.partial(kernel, width),
        grid_spec=pltpu.PrefetchScalarGridSpec(
            num_scalar_prefetch=1,
            grid=(quarters,),
            in_specs=specs,
            out_specs=out_spec,
            scratch_shapes=[pltpu.VMEM((rounds, 32 * width, 256), BF)],
        ),
        out_shape=out_shape,
        compiler_params=params(),
        name="home_rows",
    )(own, idx, *homes)


def finish_kernel(m_ref, w_ref, out_ref):
    rows = out_ref.shape[0]
    logs = []
    for i in range(4):
        line = m_ref[i, rows:, :].astype(F32).reshape(rows // 32, 1, 128)
        terms = lines_to_terms(line)
        logs.append(terms[:, 0:1] + terms[:, 1:2] + terms[:, 2:3])
    top = functools.reduce(jnp.maximum, logs)
    scales = [jnp.exp(v - top) for v in logs]
    total = sum(scales)
    summed = sum(s * m_ref[i, :rows, :].astype(F32) for i, s in enumerate(scales))
    blended = (summed / total).astype(BF)
    out_ref[...] = jnp.dot(blended, w_ref[...], preferred_element_type=F32).astype(BF)


def finish(merged, w_out):
    parts, rows, _ = merged.shape
    rows -= rows // 33
    return pl.pallas_call(
        finish_kernel,
        in_specs=[whole(merged.shape), whole(w_out.shape)],
        out_specs=whole((rows, w_out.shape[1])),
        grid=(1,),
        out_shape=jax.ShapeDtypeStruct((rows, w_out.shape[1]), BF),
        compiler_params=params(),
        name="finish",
    )(merged, w_out)


def send_places(own_slots, other_slots, width):
    zl, zh = lax.axis_index("zl"), lax.axis_index("zh")
    late = lax.axis_index(PLANE) >= 8
    group = jnp.arange(4, dtype=jnp.int32)
    shift = jnp.where(group == 0, 0, jnp.where(group == 1, jnp.where(late, -2, 2), 5 - 2 * group))
    own = ((zh * 4 + zl + shift + 8) & 7) // 4 == zh
    slot = jnp.where(own[:, None], own_slots[:, None], other_slots[:, None])
    hit = (slot >> 10) == ((zl + shift + 8) & 3)[:, None]
    return jnp.where(hit, ((slot >> 6) & 15) * width + (slot & 63), -1), own.astype(jnp.int32)


def take_places(taken, width):
    away = (lax.axis_index("zl") - (taken >> 10)) & 3
    group = jnp.where(away == 1, 2, jnp.where(away == 2, 1, away))
    source = (taken >> 6) & 15
    at = taken & 63
    by_group = (group * 16 + source) * width + at
    odd = (32 + source * 2 + group - 2) * width + at
    return jnp.where(group < 2, by_group, odd), by_group


def body(x, w_qk, w_v, w_out, slots, taken, looks):
    count = slots.shape[1]
    peers = lax.axis_size(SEQ)
    width = 2 * count // peers
    blocks = count // BLOCK
    tail = count - 2 * BLOCK
    others = lax.ppermute(slots, "zh", [(0, 1), (1, 0)])
    packed = project(x, w_qk, w_v)
    mine = lax.axis_index(SEQ) * blocks + jnp.arange(blocks, dtype=jnp.int32)
    dist = (mine[None, :] - looks) % (peers * blocks)
    next_device = [(i, (i + 1) % peers) for i in range(peers)]
    sent, own = send_places(slots, others, width)
    spots, groups = take_places(taken, width)

    (even,) = scatter_rows(sent[:, :2], packed, width, True)
    even, packed = together((even, packed))
    half = plane(even)
    up, down = scatter_rows(sent[:, 2:], packed, width, False)
    up, down = ring(up, 1), ring(down, -1)
    low, high = ring(half[:8, 1], 2), ring(half[8:, 1], -2)
    odd = plane(join(up, down))
    early = early_rows(spots, half, low, high)
    early, odd = together((early, odd))

    q_tail, kv_tail = sort_rows(spots[:, tail:], early, odd, tail, 2 * BLOCK)
    halo = lax.ppermute(kv_tail, SEQ, next_device)
    q_head, kv_head = sort_rows(spots[:, :tail], early, odd, 0, 3 * BLOCK)
    inner = attend_inner(dist, q_head, q_tail, kv_head, kv_tail)
    edge = attend_edge(dist, q_head, kv_head, halo)

    (odd,) = back_rows(groups[:, None], edge, inner, width, False)
    odd, edge = together((odd, edge))
    half = plane(odd)
    near, low, high = back_rows(groups[:, None], edge, inner, width, True)
    low, high = ring(low, -2), ring(high, 2)
    up, down = ring(half[:, 0], -1), ring(half[:, 1], 1)
    even = plane(join(near, jnp.concatenate([low, high])))
    late = home_rows(own, sent[:, 2:], width, (up, down))
    late, even = together((late, even))
    state = home_rows(own, sent[:, :2], width, (even,), late)
    merged = lax.all_to_all(state, ROUND, 0, 0, tiled=True)
    return finish(merged, w_out)


def solution(mesh):
    fine = Mesh(mesh.devices.reshape(4, 4, 4, 2, 2), SEQ + ROUND)
    in_specs = (P(SEQ, None), P(), P(), P()) + (P(ROUND, SEQ),) * 3
    return jax.shard_map(
        body, mesh=fine, in_specs=in_specs, out_specs=P(SEQ + ROUND, None), check_vma=False
    )
```

```python
import functools

import jax
import jax.numpy as jnp
from jax import lax
from jax.experimental import pallas as pl
from jax.experimental.pallas import tpu as pltpu
from jax.sharding import Mesh
from jax.sharding import PartitionSpec as P

BLOCK = 256
MASKED = -1000000000.0
SEQ = ("zl", "x", "y")
PLANE = ("x", "y")
ROUND = ("zh", "c")
BF = jnp.bfloat16
F32 = jnp.float32
VMEM_BYTES = 48 * 1024 * 1024


def params(n=1):
    return pltpu.CompilerParams(
        dimension_semantics=("arbitrary",) * n, vmem_limit_bytes=VMEM_BYTES
    )


def whole(shape):
    return pl.BlockSpec(shape, lambda *_: (0,) * len(shape))


def one_hot(a, b):
    return jnp.where(a == b, 1.0, 0.0).astype(BF)


def column(row):
    return jnp.transpose(jnp.broadcast_to(row, (8, row.shape[1])))[:, :1]


def in_hbm(v):
    return pltpu.with_memory_space_constraint(v, pltpu.HBM)


def project_kernel(x_ref, wqk_ref, wv_ref, out_ref, w_ref):
    @pl.when(pl.program_id(0) == 0)
    def _():
        w_ref[:, :128] = wqk_ref[...]
        w_ref[:, 128:] = wv_ref[...]

    out_ref[...] = jnp.dot(x_ref[...], w_ref[...], preferred_element_type=F32).astype(BF)


def project(x, w_qk, w_v):
    rows, model = x.shape
    step = 512
    return pl.pallas_call(
        project_kernel,
        grid=(rows // step,),
        in_specs=[
            pl.BlockSpec((step, model), lambda i: (i, 0)),
            whole(w_qk.shape),
            whole(w_v.shape),
        ],
        out_specs=pl.BlockSpec((step, 256), lambda i: (i, 0)),
        out_shape=jax.ShapeDtypeStruct((rows, 256), BF),
        scratch_shapes=[pltpu.VMEM((model, 256), BF)],
        compiler_params=params(),
        name="project",
    )(in_hbm(x), in_hbm(w_qk), in_hbm(w_v))


def ring(value, shift):
    def at(z):
        return (z % 4) * 2 + z // 4

    route = [(at(z), at((z + shift) % 8)) for z in range(8)]
    return lax.ppermute(value, ("zl", "zh"), route)


def join(first, second):
    return jnp.stack([first, second], axis=1)


def plane(joint):
    return lax.all_to_all(joint, PLANE, 0, 0, tiled=True)


together = lax.optimization_barrier


def scatter_kernel(idx_ref, rows_ref, *out_refs):
    peers, _, width, lanes = out_refs[0].shape[:2] + out_refs[0].shape[-2:]
    group = pl.program_id(1)
    place = lax.broadcasted_iota(jnp.int32, (peers * width, rows_ref.shape[0]), 0)
    hot = one_hot(idx_ref[0, pl.ds(group, 1), :], place)
    got = jnp.dot(hot, rows_ref[...], preferred_element_type=F32)
    got = got.astype(BF).reshape(peers, width, lanes)
    if len(out_refs) == 1:
        out_refs[0][:, 0, 0] = got
        return
    for g, ref in enumerate(out_refs):

        @pl.when(group == g)
        def _(ref=ref):
            ref[:, 0] = got


def scatter_rows(idx, rows, width, even):
    rounds, groups, count = idx.shape
    if even:
        shapes = [(16, groups, rounds, width, 256)]
        specs = [pl.BlockSpec((16, 1, 1, width, 256), lambda r, g: (0, g, r, 0, 0))]
    else:
        shapes = [(16, rounds, width, 256)] * groups
        specs = [pl.BlockSpec((16, 1, width, 256), lambda r, g: (0, r, 0, 0))] * groups
    return pl.pallas_call(
        scatter_kernel,
        grid=(rounds, groups),
        in_specs=[pl.BlockSpec((1, groups, count), lambda r, g: (r, 0, 0)), whole(rows.shape)],
        out_specs=specs,
        out_shape=[pltpu.HBM(v, BF) for v in shapes],
        compiler_params=params(2),
        name="scatter_rows",
    )(idx, rows)


def pick_rows(idx_ref, row_refs, base):
    col = column(idx_ref[0, 0])
    got = 0.0
    for ref in row_refs:
        rows = ref[...].reshape(-1, 256)
        n = rows.shape[0]
        place = lax.broadcasted_iota(jnp.int32, (col.shape[0], n), 1) + base
        got += jnp.dot(one_hot(col, place), rows, preferred_element_type=F32)
        base += n
    return got


def near_kernel(idx_ref, near_ref, out_ref):
    out_ref[0] = pick_rows(idx_ref, (near_ref,), 0).astype(BF)


def odd_kernel(idx_ref, early_ref, odd_ref, out_ref):
    n = odd_ref.shape[0] * odd_ref.shape[1] * odd_ref.shape[3]
    out_ref[0] = (early_ref[0].astype(F32) + pick_rows(idx_ref, (odd_ref,), n)).astype(BF)


def early_rows(idx, rows, early=None):
    rounds, count = idx.shape
    step = count // 2
    peers, _, _, width, lanes = rows.shape
    wide = pl.BlockSpec((1, step, 256), lambda r, b: (r, b, 0))
    groups = 1 if early is None else 2
    specs = [pl.BlockSpec((1, 1, 1, step), lambda r, b: (r, b, 0, 0))]
    args = [idx.reshape(rounds, 2, 1, step)]
    if early is not None:
        specs.append(wide)
        args.append(in_hbm(early))
    specs.append(pl.BlockSpec((peers, groups, 1, width, lanes), lambda r, b: (0, 0, r, 0, 0)))
    return pl.pallas_call(
        near_kernel if early is None else odd_kernel,
        grid=(rounds, 2),
        in_specs=specs,
        out_specs=wide,
        out_shape=pltpu.HBM((rounds, count, 256), BF),
        compiler_params=params(2),
        name="early_rows",
    )(*args, in_hbm(rows))


def sort_kernel(idx_ref, early_ref, low_ref, high_ref, q_ref, kv_ref):
    n = 2 * low_ref.shape[0] * low_ref.shape[2]
    got = early_ref[0].astype(F32) + pick_rows(idx_ref, (low_ref, high_ref), n)
    qk = got[:, :128]
    keys = qk * lax.rsqrt(jnp.sum(qk * qk, axis=-1, keepdims=True) + 1e-06)
    q_ref[0] = qk.astype(BF)
    kv_ref[0, :, :128] = keys.astype(BF)
    kv_ref[0, :, 128:] = got[:, 128:].astype(BF)


def sort_rows(idx, early, low, high, first, step):
    rounds, count = idx.shape
    blocks = count // step
    peers, _, width, lanes = low.shape
    half = pl.BlockSpec((peers, 1, width, lanes), lambda r, b: (0, r, 0, 0))
    return pl.pallas_call(
        sort_kernel,
        grid=(rounds, blocks),
        in_specs=[
            pl.BlockSpec((1, 1, 1, step), lambda r, b: (r, b, 0, 0)),
            pl.BlockSpec((1, step, 256), lambda r, b: (r, first // step + b, 0)),
            half,
            half,
        ],
        out_specs=[
            pl.BlockSpec((1, step, 128), lambda r, b: (r, b, 0)),
            pl.BlockSpec((1, step, 256), lambda r, b: (r, b, 0)),
        ],
        out_shape=[
            jax.ShapeDtypeStruct((rounds, count, 128), BF),
            jax.ShapeDtypeStruct((rounds, count, 256), BF),
        ],
        compiler_params=params(2),
        name="sort_rows",
    )(idx.reshape(rounds, blocks, 1, step), in_hbm(early), low, high)


def terms_to_lines(terms, groups):
    terms = terms.reshape(groups, 32, 128)
    slot = lax.broadcasted_iota(jnp.int32, terms.shape, 1)
    lane = lax.broadcasted_iota(jnp.int32, terms.shape, 2) % 32
    return jnp.sum(jnp.where(slot == lane, terms, 0.0), axis=1, keepdims=True)


def lines_to_terms(line):
    n = line.shape[0]
    shape = (n, 32, 128)
    slot = lax.broadcasted_iota(jnp.int32, shape, 1)
    lane = lax.broadcasted_iota(jnp.int32, shape, 2) % 32
    spread = jnp.where(slot == lane, line, 0.0).reshape(n * 32, 128).astype(BF)
    group = lax.broadcasted_iota(jnp.int32, (128, 128), 0) // 32
    pick = one_hot(group, lax.broadcasted_iota(jnp.int32, (128, 128), 1))
    return jnp.dot(spread, pick, preferred_element_type=F32)


def three_terms(v):
    hi = v.astype(BF).astype(F32)
    mid = (v - hi).astype(BF).astype(F32)
    lo = v - hi - mid
    return hi, mid, lo


def term_lanes(v, rows):
    hi, mid, lo = three_terms(v)
    group = lax.broadcasted_iota(jnp.int32, (rows, 128), 1) // 32
    return jnp.where(
        group == 0, hi, jnp.where(group == 1, mid, jnp.where(group == 2, lo, 1.0))
    ).astype(BF)


def attend_block(q, own, behind, out_ref):
    nt = (((1,), (1,)), ((), ()))
    s1 = lax.dot_general(q, own[:, :128], nt, preferred_element_type=F32)
    s2 = lax.dot_general(q, behind[:, :128], nt, preferred_element_type=F32)
    r = lax.broadcasted_iota(jnp.int32, (BLOCK, BLOCK), 0)
    k = lax.broadcasted_iota(jnp.int32, (BLOCK, BLOCK), 1)
    s1 = jnp.where(r == k, MASKED, s1)
    top = jnp.maximum(
        jnp.max(s1, axis=-1, keepdims=True), jnp.max(s2, axis=-1, keepdims=True)
    )
    e1 = jnp.exp(s1 - top)
    e2 = jnp.exp(s2 - top)
    total = jnp.sum(e1, axis=-1, keepdims=True) + jnp.sum(e2, axis=-1, keepdims=True)
    o = jnp.dot(e1.astype(BF), own[:, 128:], preferred_element_type=F32) + jnp.dot(
        e2.astype(BF), behind[:, 128:], preferred_element_type=F32
    )
    out_ref[0, :, :128] = (o / total).astype(BF)
    out_ref[0, :, 128:] = term_lanes(top + jnp.log(total), BLOCK)


def inner_kernel(dist_ref, qh_ref, qt_ref, kvh_ref, kvt_ref, out_ref, q_ref, kv_ref):
    head = kvh_ref.shape[1]

    @pl.when(pl.program_id(1) == 0)
    def _():
        q_ref[:head] = qh_ref[0]
        q_ref[head:] = qt_ref[0]
        kv_ref[:head] = kvh_ref[0]
        kv_ref[head:] = kvt_ref[0]

    def block(ref, c):
        return ref[pl.ds(pl.multiple_of(c * BLOCK, BLOCK), BLOCK), :]

    c = pl.program_id(1) + 2
    at = c - dist_ref[pl.program_id(0), c]
    attend_block(block(q_ref, c), block(kv_ref, c), block(kv_ref, at), out_ref)


def edge_kernel(dist_ref, q_ref, kv_ref, halo_ref, out_ref):
    c = pl.program_id(1)
    own = kv_ref[0, pl.ds(pl.multiple_of(c * BLOCK, BLOCK), BLOCK), :]
    at = c + 2 - dist_ref[pl.program_id(0), c]
    before = halo_ref[0, pl.ds(pl.multiple_of(jnp.minimum(at, 1) * BLOCK, BLOCK), BLOCK), :]
    behind = jnp.where(at < 2, before, kv_ref[0, :BLOCK, :])
    attend_block(q_ref[0], own, behind, out_ref)


def of_round(shape):
    return pl.BlockSpec((1,) + shape[1:], lambda r, b, d: (r, 0, 0))


def attend_inner(dist, q_head, q_tail, kv_head, kv_tail):
    rounds = q_head.shape[0]
    count = q_head.shape[1] + q_tail.shape[1]
    blocks = count // BLOCK - 2
    return pl.pallas_call(
        inner_kernel,
        grid_spec=pltpu.PrefetchScalarGridSpec(
            num_scalar_prefetch=1,
            grid=(rounds, blocks),
            in_specs=[of_round(v.shape) for v in (q_head, q_tail, kv_head, kv_tail)],
            out_specs=pl.BlockSpec((1, BLOCK, 256), lambda r, b, d: (r, b, 0)),
            scratch_shapes=[pltpu.VMEM((count, 128), BF), pltpu.VMEM((count, 256), BF)],
        ),
        out_shape=jax.ShapeDtypeStruct((rounds, blocks * BLOCK, 256), BF),
        compiler_params=params(2),
        name="attend_inner",
    )(dist, q_head, q_tail, kv_head, kv_tail)


def attend_edge(dist, q, kv, halo):
    rounds = q.shape[0]
    return pl.pallas_call(
        edge_kernel,
        grid_spec=pltpu.PrefetchScalarGridSpec(
            num_scalar_prefetch=1,
            grid=(rounds, 2),
            in_specs=[
                pl.BlockSpec((1, BLOCK, 128), lambda r, b, d: (r, b, 0)),
                of_round((rounds, 2 * BLOCK, 256)),
                of_round(halo.shape),
            ],
            out_specs=pl.BlockSpec((1, BLOCK, 256), lambda r, b, d: (r, b, 0)),
        ),
        out_shape=jax.ShapeDtypeStruct((rounds, 2 * BLOCK, 256), BF),
        compiler_params=params(2),
        name="attend_edge",
    )(dist, q, kv, halo)


def back_kernel(first_group, idx_ref, edge_ref, inner_ref, *out_refs):
    width, peers = out_refs[0].shape[-2] - 8, 16
    n = peers * width
    group = pl.program_id(1)
    idx = idx_ref[0] - (first_group + group) * n
    got = 0.0
    first = 0
    for ref in (edge_ref, inner_ref):
        count = ref.shape[1]
        place = lax.broadcasted_iota(jnp.int32, (n, count), 0)
        hot = one_hot(idx[:, first : first + count], place)
        got += jnp.dot(hot, ref[0], preferred_element_type=F32)
        first += count
    lines = terms_to_lines(got[:, 128:], n // 32).reshape(peers, width // 32, 1, 128)
    row = lax.broadcasted_iota(jnp.int32, (peers, 8, 128), 1)
    tail = jnp.zeros((peers, 8, 128), F32)
    for part in range(width // 32):
        tail = jnp.where(row == part, lines[:, part], tail)
    tail = tail.astype(BF)
    got = got[:, :128].astype(BF).reshape(peers, width, 128)

    def store(ref, at):
        ref[:, :width, :] = got[at]
        ref[:, width:, :] = tail[at]

    every, half = slice(None), peers // 2
    if len(out_refs) == 1:
        store(out_refs[0].at[:, 0, 0], every)
        return
    near_ref, low_ref, high_ref = out_refs

    @pl.when(group == 0)
    def _():
        store(near_ref.at[:, 0], every)

    @pl.when(group == 1)
    def _():
        store(low_ref.at[:, 0], slice(0, half))
        store(high_ref.at[:, 0], slice(half, peers))


def back_rows(idx, edge, inner, width, even):
    rounds = idx.shape[0]
    ext = width + 8
    if even:
        shapes = [(n, rounds, ext, 128) for n in (16, 8, 8)]
        specs = [pl.BlockSpec((v[0], 1, ext, 128), lambda r, g: (0, r, 0, 0)) for v in shapes]
    else:
        shapes = [(16, 2, rounds, ext, 128)]
        specs = [pl.BlockSpec((16, 1, 1, ext, 128), lambda r, g: (0, g, r, 0, 0))]
    one = lambda v: pl.BlockSpec((1,) + v.shape[1:], lambda r, g: (r, 0, 0))
    return pl.pallas_call(
        functools.partial(back_kernel, 0 if even else 2),
        grid=(rounds, 2),
        in_specs=[one(idx), one(edge), one(inner)],
        out_specs=specs,
        out_shape=[pltpu.HBM(v, BF) for v in shapes],
        compiler_params=params(2),
        name="back_rows",
    )(idx, edge, inner)


ABSENT = -1e30


def fill_home(x_ref, width, blocks):
    row = 0
    for block in blocks:
        size = block.shape[0] * width
        x_ref[row : row + size, :128] = block[:, :width, :].reshape(size, 128)
        tail = block[:, width:, :].astype(F32)
        lines = jnp.concatenate(
            [tail[:, p : p + 1][:, None] for p in range(width // 32)], axis=1
        ).reshape(size // 32, 1, 128)
        x_ref[row : row + size, 128:] = lines_to_terms(lines).astype(BF)
        row += size


def gather_home(own_ref, cols, x_ref, width):
    near, far = 0.0, 0.0
    size = 16 * width
    place = lax.broadcasted_iota(jnp.int32, (cols.shape[0], size), 1)
    for g in range(4):
        hot = one_hot(cols[:, g : g + 1], place)
        got = jnp.dot(hot, x_ref[g * size : (g + 1) * size], preferred_element_type=F32)
        if g == 0:
            near = got
        else:
            mine = own_ref[g] == 1
            near += jnp.where(mine, got, 0.0)
            far += jnp.where(mine, 0.0, got)
    return [near, far]


def home_kernel(width, own_ref, idx_ref, even_ref, up_ref, down_ref, out_ref, x_ref):
    rounds = even_ref.shape[2]

    @pl.when(pl.program_id(0) == 0)
    def _():
        for r in range(rounds):
            blocks = [even_ref.at[:, 0, r], even_ref.at[:, 1, r], up_ref.at[:, r], down_ref.at[:, r]]
            fill_home(x_ref.at[r], width, blocks)

    step = idx_ref.shape[2]
    cols = jnp.transpose(idx_ref[0])
    states = []
    for r in range(rounds):
        states += gather_home(own_ref, cols[:, 4 * r : 4 * r + 4], x_ref.at[r], width)
    here = [s[:, 131:132] > 0.5 for s in states]
    logs = [
        jnp.where(h, s[:, 128:129] + s[:, 129:130] + s[:, 130:131], ABSENT)
        for h, s in zip(here, states)
    ]
    top = functools.reduce(jnp.maximum, logs)
    scales = [jnp.where(h, jnp.exp(v - top), 0.0) for h, v in zip(here, logs)]
    total = sum(scales)
    some = total > 0.0
    summed = sum(s * p[:, :128] for s, p in zip(scales, states))
    safe = jnp.where(some, total, 1.0)
    log = jnp.where(some, top + jnp.log(safe), ABSENT)
    out_ref[0, :step, :] = (summed / safe).astype(BF)
    terms = term_lanes(log, step).astype(F32)
    out_ref[0, step:, :] = terms_to_lines(terms, step // 32).reshape(step // 32, 128).astype(BF)


def home_rows(own, idx, even, up, down, width):
    rounds, groups, count = idx.shape
    quarters = 4
    step = count // quarters
    columns = rounds * groups
    idx = idx.reshape(columns, quarters, step).transpose(1, 0, 2)
    return pl.pallas_call(
        functools.partial(home_kernel, width),
        grid_spec=pltpu.PrefetchScalarGridSpec(
            num_scalar_prefetch=1,
            grid=(quarters,),
            in_specs=[pl.BlockSpec((1, columns, step), lambda i, o: (i, 0, 0))]
            + [whole(v.shape) for v in (even, up, down)],
            out_specs=pl.BlockSpec((1, step + step // 32, 128), lambda i, o: (i, 0, 0)),
            scratch_shapes=[pltpu.VMEM((rounds, 64 * width, 256), BF)],
        ),
        out_shape=jax.ShapeDtypeStruct((quarters, step + step // 32, 128), BF),
        compiler_params=params(),
        name="home_rows",
    )(own, idx, even, up, down)


def finish_kernel(m_ref, w_ref, out_ref):
    rows = out_ref.shape[0]
    logs = []
    for i in range(4):
        line = m_ref[i, rows:, :].astype(F32).reshape(rows // 32, 1, 128)
        terms = lines_to_terms(line)
        logs.append(terms[:, 0:1] + terms[:, 1:2] + terms[:, 2:3])
    top = functools.reduce(jnp.maximum, logs)
    scales = [jnp.exp(v - top) for v in logs]
    total = sum(scales)
    summed = sum(s * m_ref[i, :rows, :].astype(F32) for i, s in enumerate(scales))
    blended = (summed / total).astype(BF)
    out_ref[...] = jnp.dot(blended, w_ref[...], preferred_element_type=F32).astype(BF)


def finish(merged, w_out):
    parts, rows, _ = merged.shape
    rows -= rows // 33
    return pl.pallas_call(
        finish_kernel,
        in_specs=[whole(merged.shape), whole(w_out.shape)],
        out_specs=whole((rows, w_out.shape[1])),
        grid=(1,),
        out_shape=jax.ShapeDtypeStruct((rows, w_out.shape[1]), BF),
        compiler_params=params(),
        name="finish",
    )(merged, w_out)


def send_places(own_slots, other_slots, width):
    zl, zh = lax.axis_index("zl"), lax.axis_index("zh")
    late = lax.axis_index(PLANE) >= 8
    group = jnp.arange(4, dtype=jnp.int32)
    shift = jnp.where(group == 0, 0, jnp.where(group == 1, jnp.where(late, -2, 2), 5 - 2 * group))
    own = ((zh * 4 + zl + shift + 8) & 7) // 4 == zh
    slot = jnp.where(own[:, None], own_slots[:, None], other_slots[:, None])
    hit = (slot >> 10) == ((zl + shift + 8) & 3)[:, None]
    return jnp.where(hit, ((slot >> 6) & 15) * width + (slot & 63), -1), own.astype(jnp.int32)


def take_places(taken, width):
    away = (lax.axis_index("zl") - (taken >> 10)) & 3
    group = jnp.where(away == 1, 2, jnp.where(away == 2, 1, away))
    source = (taken >> 6) & 15
    at = taken & 63
    by_group = (group * 16 + source) * width + at
    odd = (32 + source * 2 + group - 2) * width + at
    return jnp.where(group < 2, by_group, odd), by_group


def body(x, w_qk, w_v, w_out, slots, taken, looks):
    count = slots.shape[1]
    peers = lax.axis_size(SEQ)
    width = 2 * count // peers
    blocks = count // BLOCK
    tail = count - 2 * BLOCK
    others = lax.ppermute(slots, "zh", [(0, 1), (1, 0)])
    packed = project(x, w_qk, w_v)
    mine = lax.axis_index(SEQ) * blocks + jnp.arange(blocks, dtype=jnp.int32)
    dist = (mine[None, :] - looks) % (peers * blocks)
    next_device = [(i, (i + 1) % peers) for i in range(peers)]
    sent, own = send_places(slots, others, width)
    spots, groups = take_places(taken, width)

    (even,) = scatter_rows(sent[:, :2], packed, width, True)
    even, packed = together((even, packed))
    half = plane(even)
    up, down = scatter_rows(sent[:, 2:], packed, width, False)
    up, down = ring(up, 1), ring(down, -1)
    low, high = ring(half[:8, 1], 2), ring(half[8:, 1], -2)
    odd = plane(join(up, down))
    early = early_rows(spots, odd, early_rows(spots, half))
    early, low, high = together((early, low, high))

    q_tail, kv_tail = sort_rows(spots[:, tail:], early, low, high, tail, 2 * BLOCK)
    halo = lax.ppermute(kv_tail, SEQ, next_device)
    q_head, kv_head = sort_rows(spots[:, :tail], early, low, high, 0, 3 * BLOCK)
    inner = attend_inner(dist, q_head, q_tail, kv_head, kv_tail)
    edge = attend_edge(dist, q_head, kv_head, halo)

    (odd,) = back_rows(groups[:, None], edge, inner, width, False)
    odd, edge = together((odd, edge))
    half = plane(odd)
    near, low, high = back_rows(groups[:, None], edge, inner, width, True)
    low, high = ring(low, -2), ring(high, 2)
    up, down = ring(half[:, 0], -1), ring(half[:, 1], 1)
    even = plane(join(near, jnp.concatenate([low, high])))
    state = home_rows(own, sent, even, up, down, width)
    merged = lax.all_to_all(state, ROUND, 0, 0, tiled=True)
    return finish(merged, w_out)


def solution(mesh):
    fine = Mesh(mesh.devices.reshape(4, 4, 4, 2, 2), SEQ + ROUND)
    in_specs = (P(SEQ, None), P(), P(), P()) + (P(ROUND, SEQ),) * 3
    return jax.shard_map(
        body, mesh=fine, in_specs=in_specs, out_specs=P(SEQ + ROUND, None), check_vma=False
    )
```

```python
import functools

import jax
import jax.numpy as jnp
from jax import lax
from jax.experimental import pallas as pl
from jax.experimental.pallas import tpu as pltpu
from jax.sharding import Mesh
from jax.sharding import PartitionSpec as P

BLOCK = 256
MASKED = -1000000000.0
SEQ = ("zl", "x", "y")
PLANE = ("x", "y")
ROUND = ("zh", "c")
BF = jnp.bfloat16
F32 = jnp.float32
VMEM_BYTES = 48 * 1024 * 1024


def params(n=1):
    return pltpu.CompilerParams(
        dimension_semantics=("arbitrary",) * n, vmem_limit_bytes=VMEM_BYTES
    )


def whole(shape):
    return pl.BlockSpec(shape, lambda *_: (0,) * len(shape))


def one_hot(a, b):
    return jnp.where(a == b, 1.0, 0.0).astype(BF)


def column(row):
    return jnp.transpose(jnp.broadcast_to(row, (8, row.shape[1])))[:, :1]


def in_hbm(v):
    return pltpu.with_memory_space_constraint(v, pltpu.HBM)


def project_kernel(left_ref, right_ref, wqk_ref, wv_ref, out_ref, w_ref):
    @pl.when(pl.program_id(0) == 0)
    def _():
        w_ref[:, :128] = wqk_ref[...]
        w_ref[:, 128:] = wv_ref[...]

    half = left_ref.shape[1]
    got = jnp.dot(left_ref[...], w_ref[:half], preferred_element_type=F32)
    got += jnp.dot(right_ref[...], w_ref[half:], preferred_element_type=F32)
    out_ref[...] = got.astype(BF)


def project(x, w_qk, w_v):
    rows, model = x.shape
    step = 512
    return pl.pallas_call(
        project_kernel,
        grid=(rows // step,),
        in_specs=[
            pl.BlockSpec((step, model // 2), lambda i: (i, 0)),
            pl.BlockSpec((step, model // 2), lambda i: (i, 1)),
            whole(w_qk.shape),
            whole(w_v.shape),
        ],
        out_specs=pl.BlockSpec((step, 256), lambda i: (i, 0)),
        out_shape=jax.ShapeDtypeStruct((rows, 256), BF),
        scratch_shapes=[pltpu.VMEM((model, 256), BF)],
        compiler_params=params(),
        name="project",
    )(in_hbm(x), in_hbm(x), in_hbm(w_qk), in_hbm(w_v))


def ring(value, shift):
    def at(z):
        return (z % 4) * 2 + z // 4

    route = [(at(z), at((z + shift) % 8)) for z in range(8)]
    return lax.ppermute(value, ("zl", "zh"), route)


def join(first, second):
    return jnp.stack([first, second], axis=1)


def plane(joint):
    return lax.all_to_all(joint, PLANE, 0, 0, tiled=True)


together = lax.optimization_barrier


def scatter_kernel(idx_ref, rows_ref, *out_refs):
    peers, _, width, lanes = out_refs[0].shape[:2] + out_refs[0].shape[-2:]
    group = pl.program_id(1)
    place = lax.broadcasted_iota(jnp.int32, (peers * width, rows_ref.shape[0]), 0)
    hot = one_hot(idx_ref[0, pl.ds(group, 1), :], place)
    got = jnp.dot(hot, rows_ref[...], preferred_element_type=F32)
    got = got.astype(BF).reshape(peers, width, lanes)
    if len(out_refs) == 1:
        out_refs[0][:, 0, 0] = got
        return
    for g, ref in enumerate(out_refs):

        @pl.when(group == g)
        def _(ref=ref):
            ref[:, 0] = got


def scatter_rows(idx, rows, width, even):
    rounds, groups, count = idx.shape
    if even:
        shapes = [(16, groups, rounds, width, 256)]
        specs = [pl.BlockSpec((16, 1, 1, width, 256), lambda r, g: (0, g, r, 0, 0))]
    else:
        shapes = [(16, rounds, width, 256)] * groups
        specs = [pl.BlockSpec((16, 1, width, 256), lambda r, g: (0, r, 0, 0))] * groups
    return pl.pallas_call(
        scatter_kernel,
        grid=(rounds, groups),
        in_specs=[pl.BlockSpec((1, groups, count), lambda r, g: (r, 0, 0)), whole(rows.shape)],
        out_specs=specs,
        out_shape=[pltpu.HBM(v, BF) for v in shapes],
        compiler_params=params(2),
        name="scatter_rows",
    )(idx, rows)


def pick_rows(idx_ref, row_refs, base):
    col = column(idx_ref[0, 0])
    got = 0.0
    for ref in row_refs:
        rows = ref[...].reshape(-1, 256)
        n = rows.shape[0]
        place = lax.broadcasted_iota(jnp.int32, (col.shape[0], n), 1) + base
        got += jnp.dot(one_hot(col, place), rows, preferred_element_type=F32)
        base += n
    return got


def near_kernel(idx_ref, near_ref, out_ref):
    out_ref[0] = pick_rows(idx_ref, (near_ref,), 0).astype(BF)


def odd_kernel(idx_ref, early_ref, odd_ref, out_ref):
    n = odd_ref.shape[0] * odd_ref.shape[1] * odd_ref.shape[3]
    out_ref[0] = (early_ref[0].astype(F32) + pick_rows(idx_ref, (odd_ref,), n)).astype(BF)


def early_rows(idx, rows, early=None):
    rounds, count = idx.shape
    step = count // 2
    peers, _, _, width, lanes = rows.shape
    wide = pl.BlockSpec((1, step, 256), lambda r, b: (r, b, 0))
    groups = 1 if early is None else 2
    specs = [pl.BlockSpec((1, 1, 1, step), lambda r, b: (r, b, 0, 0))]
    args = [idx.reshape(rounds, 2, 1, step)]
    if early is not None:
        specs.append(wide)
        args.append(in_hbm(early))
    specs.append(pl.BlockSpec((peers, groups, 1, width, lanes), lambda r, b: (0, 0, r, 0, 0)))
    return pl.pallas_call(
        near_kernel if early is None else odd_kernel,
        grid=(rounds, 2),
        in_specs=specs,
        out_specs=wide,
        out_shape=pltpu.HBM((rounds, count, 256), BF),
        compiler_params=params(2),
        name="early_rows",
    )(*args, in_hbm(rows))


def sort_kernel(idx_ref, early_ref, low_ref, high_ref, q_ref, kv_ref):
    n = 2 * low_ref.shape[0] * low_ref.shape[2]
    got = early_ref[0].astype(F32) + pick_rows(idx_ref, (low_ref, high_ref), n)
    qk = got[:, :128]
    keys = qk * lax.rsqrt(jnp.sum(qk * qk, axis=-1, keepdims=True) + 1e-06)
    q_ref[0] = qk.astype(BF)
    kv_ref[0, :, :128] = keys.astype(BF)
    kv_ref[0, :, 128:] = got[:, 128:].astype(BF)


def sort_rows(idx, early, low, high, first, step):
    rounds, count = idx.shape
    blocks = count // step
    peers, _, width, lanes = low.shape
    half = pl.BlockSpec((peers, 1, width, lanes), lambda r, b: (0, r, 0, 0))
    return pl.pallas_call(
        sort_kernel,
        grid=(rounds, blocks),
        in_specs=[
            pl.BlockSpec((1, 1, 1, step), lambda r, b: (r, b, 0, 0)),
            pl.BlockSpec((1, step, 256), lambda r, b: (r, first // step + b, 0)),
            half,
            half,
        ],
        out_specs=[
            pl.BlockSpec((1, step, 128), lambda r, b: (r, b, 0)),
            pl.BlockSpec((1, step, 256), lambda r, b: (r, b, 0)),
        ],
        out_shape=[
            jax.ShapeDtypeStruct((rounds, count, 128), BF),
            jax.ShapeDtypeStruct((rounds, count, 256), BF),
        ],
        compiler_params=params(2),
        name="sort_rows",
    )(idx.reshape(rounds, blocks, 1, step), in_hbm(early), low, high)


def terms_to_lines(terms, groups):
    terms = terms.reshape(groups, 32, 128)
    slot = lax.broadcasted_iota(jnp.int32, terms.shape, 1)
    lane = lax.broadcasted_iota(jnp.int32, terms.shape, 2) % 32
    return jnp.sum(jnp.where(slot == lane, terms, 0.0), axis=1, keepdims=True)


def lines_to_terms(line):
    n = line.shape[0]
    shape = (n, 32, 128)
    slot = lax.broadcasted_iota(jnp.int32, shape, 1)
    lane = lax.broadcasted_iota(jnp.int32, shape, 2) % 32
    spread = jnp.where(slot == lane, line, 0.0).reshape(n * 32, 128).astype(BF)
    group = lax.broadcasted_iota(jnp.int32, (128, 128), 0) // 32
    pick = one_hot(group, lax.broadcasted_iota(jnp.int32, (128, 128), 1))
    return jnp.dot(spread, pick, preferred_element_type=F32)


def three_terms(v):
    hi = v.astype(BF).astype(F32)
    mid = (v - hi).astype(BF).astype(F32)
    lo = v - hi - mid
    return hi, mid, lo


def term_lanes(v, rows):
    hi, mid, lo = three_terms(v)
    group = lax.broadcasted_iota(jnp.int32, (rows, 128), 1) // 32
    return jnp.where(
        group == 0, hi, jnp.where(group == 1, mid, jnp.where(group == 2, lo, 1.0))
    ).astype(BF)


def attend_block(q, own, behind, out_ref):
    nt = (((1,), (1,)), ((), ()))
    s1 = lax.dot_general(q, own[:, :128], nt, preferred_element_type=F32)
    s2 = lax.dot_general(q, behind[:, :128], nt, preferred_element_type=F32)
    r = lax.broadcasted_iota(jnp.int32, (BLOCK, BLOCK), 0)
    k = lax.broadcasted_iota(jnp.int32, (BLOCK, BLOCK), 1)
    s1 = jnp.where(r == k, MASKED, s1)
    top = jnp.maximum(
        jnp.max(s1, axis=-1, keepdims=True), jnp.max(s2, axis=-1, keepdims=True)
    )
    e1 = jnp.exp(s1 - top)
    e2 = jnp.exp(s2 - top)
    total = jnp.sum(e1, axis=-1, keepdims=True) + jnp.sum(e2, axis=-1, keepdims=True)
    o = jnp.dot(e1.astype(BF), own[:, 128:], preferred_element_type=F32) + jnp.dot(
        e2.astype(BF), behind[:, 128:], preferred_element_type=F32
    )
    out_ref[0, :, :128] = (o / total).astype(BF)
    out_ref[0, :, 128:] = term_lanes(top + jnp.log(total), BLOCK)


def inner_kernel(dist_ref, qh_ref, qt_ref, kvh_ref, kvt_ref, out_ref, q_ref, kv_ref):
    head = kvh_ref.shape[1]

    @pl.when(pl.program_id(1) == 0)
    def _():
        q_ref[:head] = qh_ref[0]
        q_ref[head:] = qt_ref[0]
        kv_ref[:head] = kvh_ref[0]
        kv_ref[head:] = kvt_ref[0]

    def block(ref, c):
        return ref[pl.ds(pl.multiple_of(c * BLOCK, BLOCK), BLOCK), :]

    c = pl.program_id(1) + 2
    at = c - dist_ref[pl.program_id(0), c]
    attend_block(block(q_ref, c), block(kv_ref, c), block(kv_ref, at), out_ref)


def edge_kernel(dist_ref, q_ref, kv_ref, halo_ref, out_ref):
    c = pl.program_id(1)
    own = kv_ref[0, pl.ds(pl.multiple_of(c * BLOCK, BLOCK), BLOCK), :]
    at = c + 2 - dist_ref[pl.program_id(0), c]
    before = halo_ref[0, pl.ds(pl.multiple_of(jnp.minimum(at, 1) * BLOCK, BLOCK), BLOCK), :]
    behind = jnp.where(at < 2, before, kv_ref[0, :BLOCK, :])
    attend_block(q_ref[0], own, behind, out_ref)


def of_round(shape):
    return pl.BlockSpec((1,) + shape[1:], lambda r, b, d: (r, 0, 0))


def attend_inner(dist, q_head, q_tail, kv_head, kv_tail):
    rounds = q_head.shape[0]
    count = q_head.shape[1] + q_tail.shape[1]
    blocks = count // BLOCK - 2
    return pl.pallas_call(
        inner_kernel,
        grid_spec=pltpu.PrefetchScalarGridSpec(
            num_scalar_prefetch=1,
            grid=(rounds, blocks),
            in_specs=[of_round(v.shape) for v in (q_head, q_tail, kv_head, kv_tail)],
            out_specs=pl.BlockSpec((1, BLOCK, 256), lambda r, b, d: (r, b, 0)),
            scratch_shapes=[pltpu.VMEM((count, 128), BF), pltpu.VMEM((count, 256), BF)],
        ),
        out_shape=jax.ShapeDtypeStruct((rounds, blocks * BLOCK, 256), BF),
        compiler_params=params(2),
        name="attend_inner",
    )(dist, q_head, q_tail, kv_head, kv_tail)


def attend_edge(dist, q, kv, halo):
    rounds = q.shape[0]
    return pl.pallas_call(
        edge_kernel,
        grid_spec=pltpu.PrefetchScalarGridSpec(
            num_scalar_prefetch=1,
            grid=(rounds, 2),
            in_specs=[
                pl.BlockSpec((1, BLOCK, 128), lambda r, b, d: (r, b, 0)),
                of_round((rounds, 2 * BLOCK, 256)),
                of_round(halo.shape),
            ],
            out_specs=pl.BlockSpec((1, BLOCK, 256), lambda r, b, d: (r, b, 0)),
        ),
        out_shape=jax.ShapeDtypeStruct((rounds, 2 * BLOCK, 256), BF),
        compiler_params=params(2),
        name="attend_edge",
    )(dist, q, kv, halo)


def back_kernel(first_group, idx_ref, edge_ref, inner_ref, *out_refs):
    width, peers = out_refs[0].shape[-2] - 8, 16
    n = peers * width
    group = pl.program_id(1)
    idx = idx_ref[0] - (first_group + group) * n
    got = 0.0
    first = 0
    for ref in (edge_ref, inner_ref):
        count = ref.shape[1]
        place = lax.broadcasted_iota(jnp.int32, (n, count), 0)
        hot = one_hot(idx[:, first : first + count], place)
        got += jnp.dot(hot, ref[0], preferred_element_type=F32)
        first += count
    lines = terms_to_lines(got[:, 128:], n // 32).reshape(peers, width // 32, 1, 128)
    row = lax.broadcasted_iota(jnp.int32, (peers, 8, 128), 1)
    tail = jnp.zeros((peers, 8, 128), F32)
    for part in range(width // 32):
        tail = jnp.where(row == part, lines[:, part], tail)
    tail = tail.astype(BF)
    got = got[:, :128].astype(BF).reshape(peers, width, 128)

    def store(ref, at):
        ref[:, :width, :] = got[at]
        ref[:, width:, :] = tail[at]

    every, half = slice(None), peers // 2
    if len(out_refs) == 1:
        store(out_refs[0].at[:, 0, 0], every)
        return
    near_ref, low_ref, high_ref = out_refs

    @pl.when(group == 0)
    def _():
        store(near_ref.at[:, 0], every)

    @pl.when(group == 1)
    def _():
        store(low_ref.at[:, 0], slice(0, half))
        store(high_ref.at[:, 0], slice(half, peers))


def back_rows(idx, edge, inner, width, even):
    rounds = idx.shape[0]
    ext = width + 8
    if even:
        shapes = [(n, rounds, ext, 128) for n in (16, 8, 8)]
        specs = [pl.BlockSpec((v[0], 1, ext, 128), lambda r, g: (0, r, 0, 0)) for v in shapes]
    else:
        shapes = [(16, 2, rounds, ext, 128)]
        specs = [pl.BlockSpec((16, 1, 1, ext, 128), lambda r, g: (0, g, r, 0, 0))]
    one = lambda v: pl.BlockSpec((1,) + v.shape[1:], lambda r, g: (r, 0, 0))
    return pl.pallas_call(
        functools.partial(back_kernel, 0 if even else 2),
        grid=(rounds, 2),
        in_specs=[one(idx), one(edge), one(inner)],
        out_specs=specs,
        out_shape=[pltpu.HBM(v, BF) for v in shapes],
        compiler_params=params(2),
        name="back_rows",
    )(idx, edge, inner)


ABSENT = -1e30


def fill_home(x_ref, width, blocks):
    row = 0
    for block in blocks:
        size = block.shape[0] * width
        x_ref[row : row + size, :128] = block[:, :width, :].reshape(size, 128)
        tail = block[:, width:, :].astype(F32)
        lines = jnp.concatenate(
            [tail[:, p : p + 1][:, None] for p in range(width // 32)], axis=1
        ).reshape(size // 32, 1, 128)
        x_ref[row : row + size, 128:] = lines_to_terms(lines).astype(BF)
        row += size


def gather_home(own_ref, cols, x_ref, width):
    near, far = 0.0, 0.0
    size = 16 * width
    place = lax.broadcasted_iota(jnp.int32, (cols.shape[0], size), 1)
    for g in range(4):
        hot = one_hot(cols[:, g : g + 1], place)
        got = jnp.dot(hot, x_ref[g * size : (g + 1) * size], preferred_element_type=F32)
        if g == 0:
            near = got
        else:
            mine = own_ref[g] == 1
            near += jnp.where(mine, got, 0.0)
            far += jnp.where(mine, 0.0, got)
    return [near, far]


def home_kernel(width, own_ref, idx_ref, even_ref, up_ref, down_ref, out_ref, x_ref):
    rounds = even_ref.shape[2]

    @pl.when(pl.program_id(0) == 0)
    def _():
        for r in range(rounds):
            blocks = [even_ref.at[:, 0, r], even_ref.at[:, 1, r], up_ref.at[:, r], down_ref.at[:, r]]
            fill_home(x_ref.at[r], width, blocks)

    step = idx_ref.shape[2]
    cols = jnp.transpose(idx_ref[0])
    states = []
    for r in range(rounds):
        states += gather_home(own_ref, cols[:, 4 * r : 4 * r + 4], x_ref.at[r], width)
    here = [s[:, 131:132] > 0.5 for s in states]
    logs = [
        jnp.where(h, s[:, 128:129] + s[:, 129:130] + s[:, 130:131], ABSENT)
        for h, s in zip(here, states)
    ]
    top = functools.reduce(jnp.maximum, logs)
    scales = [jnp.where(h, jnp.exp(v - top), 0.0) for h, v in zip(here, logs)]
    total = sum(scales)
    some = total > 0.0
    summed = sum(s * p[:, :128] for s, p in zip(scales, states))
    safe = jnp.where(some, total, 1.0)
    log = jnp.where(some, top + jnp.log(safe), ABSENT)
    mean = (summed / safe).astype(BF)
    terms = term_lanes(log, step).astype(F32)
    lines = terms_to_lines(terms, step // 32).reshape(step // 32, 128).astype(BF)
    part = step // out_ref.shape[0]
    for q in range(out_ref.shape[0]):
        out_ref[q, :part, :] = mean[q * part : (q + 1) * part]
        out_ref[q, part:, :] = lines[q * part // 32 : (q + 1) * part // 32]


def home_rows(own, idx, even, up, down, width):
    rounds, groups, count = idx.shape
    quarters, steps = 4, 2
    step = count // steps
    part = count // quarters
    columns = rounds * groups
    idx = idx.reshape(columns, steps, step).transpose(1, 0, 2)
    return pl.pallas_call(
        functools.partial(home_kernel, width),
        grid_spec=pltpu.PrefetchScalarGridSpec(
            num_scalar_prefetch=1,
            grid=(steps,),
            in_specs=[pl.BlockSpec((1, columns, step), lambda i, o: (i, 0, 0))]
            + [whole(v.shape) for v in (even, up, down)],
            out_specs=pl.BlockSpec((quarters // steps, part + part // 32, 128), lambda i, o: (i, 0, 0)),
            scratch_shapes=[pltpu.VMEM((rounds, 64 * width, 256), BF)],
        ),
        out_shape=jax.ShapeDtypeStruct((quarters, part + part // 32, 128), BF),
        compiler_params=params(),
        name="home_rows",
    )(own, idx, even, up, down)


def finish_kernel(m_ref, w_ref, out_ref):
    rows = out_ref.shape[0]
    logs = []
    for i in range(4):
        line = m_ref[i, rows:, :].astype(F32).reshape(rows // 32, 1, 128)
        terms = lines_to_terms(line)
        logs.append(terms[:, 0:1] + terms[:, 1:2] + terms[:, 2:3])
    top = functools.reduce(jnp.maximum, logs)
    scales = [jnp.exp(v - top) for v in logs]
    total = sum(scales)
    summed = sum(s * m_ref[i, :rows, :].astype(F32) for i, s in enumerate(scales))
    blended = (summed / total).astype(BF)
    out_ref[...] = jnp.dot(blended, w_ref[...], preferred_element_type=F32).astype(BF)


def finish(merged, w_out):
    parts, rows, _ = merged.shape
    rows -= rows // 33
    return pl.pallas_call(
        finish_kernel,
        in_specs=[whole(merged.shape), whole(w_out.shape)],
        out_specs=whole((rows, w_out.shape[1])),
        grid=(1,),
        out_shape=jax.ShapeDtypeStruct((rows, w_out.shape[1]), BF),
        compiler_params=params(),
        name="finish",
    )(merged, w_out)


def send_places(own_slots, other_slots, width):
    zl, zh = lax.axis_index("zl"), lax.axis_index("zh")
    late = lax.axis_index(PLANE) >= 8
    group = jnp.arange(4, dtype=jnp.int32)
    shift = jnp.where(group == 0, 0, jnp.where(group == 1, jnp.where(late, -2, 2), 5 - 2 * group))
    own = ((zh * 4 + zl + shift + 8) & 7) // 4 == zh
    slot = jnp.where(own[:, None], own_slots[:, None], other_slots[:, None])
    hit = (slot >> 10) == ((zl + shift + 8) & 3)[:, None]
    return jnp.where(hit, ((slot >> 6) & 15) * width + (slot & 63), -1), own.astype(jnp.int32)


def take_places(taken, width):
    away = (lax.axis_index("zl") - (taken >> 10)) & 3
    group = jnp.where(away == 1, 2, jnp.where(away == 2, 1, away))
    source = (taken >> 6) & 15
    at = taken & 63
    by_group = (group * 16 + source) * width + at
    odd = (32 + source * 2 + group - 2) * width + at
    return jnp.where(group < 2, by_group, odd), by_group


def body(x, w_qk, w_v, w_out, slots, taken, looks):
    count = slots.shape[1]
    peers = lax.axis_size(SEQ)
    width = 2 * count // peers
    blocks = count // BLOCK
    tail = count - 2 * BLOCK
    others = lax.ppermute(slots, "zh", [(0, 1), (1, 0)])
    packed = project(x, w_qk, w_v)
    mine = lax.axis_index(SEQ) * blocks + jnp.arange(blocks, dtype=jnp.int32)
    dist = (mine[None, :] - looks) % (peers * blocks)
    next_device = [(i, (i + 1) % peers) for i in range(peers)]
    sent, own = send_places(slots, others, width)
    spots, groups = take_places(taken, width)

    (even,) = scatter_rows(sent[:, :2], packed, width, True)
    even, packed = together((even, packed))
    half = plane(even)
    up, down = scatter_rows(sent[:, 2:], packed, width, False)
    up, down = ring(up, 1), ring(down, -1)
    low, high, up, down = together((half[:8, 1], half[8:, 1], up, down))
    low, high = ring(low, 2), ring(high, -2)
    odd = plane(join(up, down))
    early = early_rows(spots, odd, early_rows(spots, half))
    early, low, high = together((early, low, high))

    q_tail, kv_tail = sort_rows(spots[:, tail:], early, low, high, tail, 2 * BLOCK)
    halo = lax.ppermute(kv_tail, SEQ, next_device)
    q_head, kv_head = sort_rows(spots[:, :tail], early, low, high, 0, 3 * BLOCK)
    inner = attend_inner(dist, q_head, q_tail, kv_head, kv_tail)
    edge = attend_edge(dist, q_head, kv_head, halo)

    (odd,) = back_rows(groups[:, None], edge, inner, width, False)
    odd, edge = together((odd, edge))
    half = plane(odd)
    near, low, high = back_rows(groups[:, None], edge, inner, width, True)
    low, high = ring(low, -2), ring(high, 2)
    up, down, low, high = together((half[:, 0], half[:, 1], low, high))
    up, down = ring(up, -1), ring(down, 1)
    even = plane(join(near, jnp.concatenate([low, high])))
    state = home_rows(own, sent, even, up, down, width)
    merged = lax.all_to_all(state, ROUND, 0, 0, tiled=True)
    return finish(merged, w_out)


def solution(mesh):
    fine = Mesh(mesh.devices.reshape(4, 4, 4, 2, 2), SEQ + ROUND)
    in_specs = (P(SEQ, None), P(), P(), P()) + (P(ROUND, SEQ),) * 3
    return jax.shard_map(
        body, mesh=fine, in_specs=in_specs, out_specs=P(SEQ + ROUND, None), check_vma=False
    )
```

```python
import functools

import jax
import jax.numpy as jnp
from jax import lax
from jax.experimental import pallas as pl
from jax.experimental.pallas import tpu as pltpu
from jax.sharding import Mesh
from jax.sharding import PartitionSpec as P

BLOCK = 256
MASKED = -1000000000.0
SEQ = ("zl", "x", "y")
PLANE = ("x", "y")
ROUND = ("zh", "c")
BF = jnp.bfloat16
F32 = jnp.float32
VMEM_BYTES = 48 * 1024 * 1024


def params(n=1):
    return pltpu.CompilerParams(
        dimension_semantics=("arbitrary",) * n, vmem_limit_bytes=VMEM_BYTES
    )


def whole(shape):
    return pl.BlockSpec(shape, lambda *_: (0,) * len(shape))


def one_hot(a, b):
    return jnp.where(a == b, 1.0, 0.0).astype(BF)


def column(row):
    return jnp.transpose(jnp.broadcast_to(row, (8, row.shape[1])))[:, :1]


def in_hbm(v):
    return pltpu.with_memory_space_constraint(v, pltpu.HBM)


def project_kernel(left_ref, right_ref, wqk_ref, wv_ref, out_ref, w_ref):
    @pl.when(pl.program_id(0) == 0)
    def _():
        w_ref[:, :128] = wqk_ref[...]
        w_ref[:, 128:] = wv_ref[...]

    half = left_ref.shape[1]
    got = jnp.dot(left_ref[...], w_ref[:half], preferred_element_type=F32)
    got += jnp.dot(right_ref[...], w_ref[half:], preferred_element_type=F32)
    out_ref[...] = got.astype(BF)


def project(x, w_qk, w_v):
    rows, model = x.shape
    step = 512
    return pl.pallas_call(
        project_kernel,
        grid=(rows // step,),
        in_specs=[
            pl.BlockSpec((step, model // 2), lambda i: (i, 0)),
            pl.BlockSpec((step, model // 2), lambda i: (i, 1)),
            whole(w_qk.shape),
            whole(w_v.shape),
        ],
        out_specs=pl.BlockSpec((step, 256), lambda i: (i, 0)),
        out_shape=jax.ShapeDtypeStruct((rows, 256), BF),
        scratch_shapes=[pltpu.VMEM((model, 256), BF)],
        compiler_params=params(),
        name="project",
    )(in_hbm(x), in_hbm(x), in_hbm(w_qk), in_hbm(w_v))


def ring(value, shift):
    def at(z):
        return (z % 4) * 2 + z // 4

    route = [(at(z), at((z + shift) % 8)) for z in range(8)]
    return lax.ppermute(value, ("zl", "zh"), route)


def join(first, second):
    return jnp.stack([first, second], axis=1)


def plane(joint):
    return lax.all_to_all(joint, PLANE, 0, 0, tiled=True)


together = lax.optimization_barrier


def scatter_kernel(idx_ref, rows_ref, *out_refs):
    peers, _, width, lanes = out_refs[0].shape[:2] + out_refs[0].shape[-2:]
    group = pl.program_id(1)
    place = lax.broadcasted_iota(jnp.int32, (peers * width, rows_ref.shape[0]), 0)
    hot = one_hot(idx_ref[0, pl.ds(group, 1), :], place)
    got = jnp.dot(hot, rows_ref[...], preferred_element_type=F32)
    got = got.astype(BF).reshape(peers, width, lanes)
    if len(out_refs) == 1:
        out_refs[0][:, 0, 0] = got
        return
    for g, ref in enumerate(out_refs):

        @pl.when(group == g)
        def _(ref=ref):
            ref[:, 0] = got


def scatter_rows(idx, rows, width, even):
    rounds, groups, count = idx.shape
    if even:
        shapes = [(16, groups, rounds, width, 256)]
        specs = [pl.BlockSpec((16, 1, 1, width, 256), lambda r, g: (0, g, r, 0, 0))]
    else:
        shapes = [(16, rounds, width, 256)] * groups
        specs = [pl.BlockSpec((16, 1, width, 256), lambda r, g: (0, r, 0, 0))] * groups
    return pl.pallas_call(
        scatter_kernel,
        grid=(rounds, groups),
        in_specs=[pl.BlockSpec((1, groups, count), lambda r, g: (r, 0, 0)), whole(rows.shape)],
        out_specs=specs,
        out_shape=[pltpu.HBM(v, BF) for v in shapes],
        compiler_params=params(2),
        name="scatter_rows",
    )(idx, rows)


def pick_rows(idx_ref, row_refs, base):
    col = column(idx_ref[0, 0])
    got = 0.0
    for ref in row_refs:
        rows = ref[...].reshape(-1, 256)
        n = rows.shape[0]
        place = lax.broadcasted_iota(jnp.int32, (col.shape[0], n), 1) + base
        got += jnp.dot(one_hot(col, place), rows, preferred_element_type=F32)
        base += n
    return got


def near_kernel(idx_ref, near_ref, out_ref):
    out_ref[0] = pick_rows(idx_ref, (near_ref,), 0).astype(BF)


def near_rows(idx, rows):
    rounds, count = idx.shape
    step = count // 2
    peers, _, _, width, lanes = rows.shape
    return pl.pallas_call(
        near_kernel,
        grid=(rounds, 2),
        in_specs=[
            pl.BlockSpec((1, 1, 1, step), lambda r, b: (r, b, 0, 0)),
            pl.BlockSpec((peers, 1, 1, width, lanes), lambda r, b: (0, 0, r, 0, 0)),
        ],
        out_specs=pl.BlockSpec((1, step, 256), lambda r, b: (r, b, 0)),
        out_shape=pltpu.HBM((rounds, count, 256), BF),
        compiler_params=params(2),
        name="near_rows",
    )(idx.reshape(rounds, 2, 1, step), in_hbm(rows))


def sort_kernel(idx_ref, early_ref, low_ref, high_ref, odd_ref, q_ref, kv_ref):
    n = 2 * low_ref.shape[0] * low_ref.shape[2]
    got = early_ref[0].astype(F32) + pick_rows(idx_ref, (low_ref, high_ref, odd_ref), n)
    qk = got[:, :128]
    keys = qk * lax.rsqrt(jnp.sum(qk * qk, axis=-1, keepdims=True) + 1e-06)
    q_ref[0] = qk.astype(BF)
    kv_ref[0, :, :128] = keys.astype(BF)
    kv_ref[0, :, 128:] = got[:, 128:].astype(BF)


def sort_rows(idx, early, low, high, odd, first, step):
    rounds, count = idx.shape
    blocks = count // step
    peers, _, width, lanes = low.shape
    half = pl.BlockSpec((peers, 1, width, lanes), lambda r, b: (0, r, 0, 0))
    return pl.pallas_call(
        sort_kernel,
        grid=(rounds, blocks),
        in_specs=[
            pl.BlockSpec((1, 1, 1, step), lambda r, b: (r, b, 0, 0)),
            pl.BlockSpec((1, step, 256), lambda r, b: (r, first // step + b, 0)),
            half,
            half,
            pl.BlockSpec((2 * peers, 2, 1, width, lanes), lambda r, b: (0, 0, r, 0, 0)),
        ],
        out_specs=[
            pl.BlockSpec((1, step, 128), lambda r, b: (r, b, 0)),
            pl.BlockSpec((1, step, 256), lambda r, b: (r, b, 0)),
        ],
        out_shape=[
            jax.ShapeDtypeStruct((rounds, count, 128), BF),
            jax.ShapeDtypeStruct((rounds, count, 256), BF),
        ],
        compiler_params=params(2),
        name="sort_rows",
    )(idx.reshape(rounds, blocks, 1, step), in_hbm(early), low, high, in_hbm(odd))


def terms_to_lines(terms, groups):
    terms = terms.reshape(groups, 32, 128)
    slot = lax.broadcasted_iota(jnp.int32, terms.shape, 1)
    lane = lax.broadcasted_iota(jnp.int32, terms.shape, 2) % 32
    return jnp.sum(jnp.where(slot == lane, terms, 0.0), axis=1, keepdims=True)


def lines_to_terms(line):
    n = line.shape[0]
    shape = (n, 32, 128)
    slot = lax.broadcasted_iota(jnp.int32, shape, 1)
    lane = lax.broadcasted_iota(jnp.int32, shape, 2) % 32
    spread = jnp.where(slot == lane, line, 0.0).reshape(n * 32, 128).astype(BF)
    group = lax.broadcasted_iota(jnp.int32, (128, 128), 0) // 32
    pick = one_hot(group, lax.broadcasted_iota(jnp.int32, (128, 128), 1))
    return jnp.dot(spread, pick, preferred_element_type=F32)


def three_terms(v):
    hi = v.astype(BF).astype(F32)
    mid = (v - hi).astype(BF).astype(F32)
    lo = v - hi - mid
    return hi, mid, lo


def term_lanes(v, rows):
    hi, mid, lo = three_terms(v)
    group = lax.broadcasted_iota(jnp.int32, (rows, 128), 1) // 32
    return jnp.where(
        group == 0, hi, jnp.where(group == 1, mid, jnp.where(group == 2, lo, 1.0))
    ).astype(BF)


def attend_block(q, own, behind, out_ref):
    nt = (((1,), (1,)), ((), ()))
    s1 = lax.dot_general(q, own[:, :128], nt, preferred_element_type=F32)
    s2 = lax.dot_general(q, behind[:, :128], nt, preferred_element_type=F32)
    r = lax.broadcasted_iota(jnp.int32, (BLOCK, BLOCK), 0)
    k = lax.broadcasted_iota(jnp.int32, (BLOCK, BLOCK), 1)
    s1 = jnp.where(r == k, MASKED, s1)
    top = jnp.maximum(
        jnp.max(s1, axis=-1, keepdims=True), jnp.max(s2, axis=-1, keepdims=True)
    )
    e1 = jnp.exp(s1 - top)
    e2 = jnp.exp(s2 - top)
    total = jnp.sum(e1, axis=-1, keepdims=True) + jnp.sum(e2, axis=-1, keepdims=True)
    o = jnp.dot(e1.astype(BF), own[:, 128:], preferred_element_type=F32) + jnp.dot(
        e2.astype(BF), behind[:, 128:], preferred_element_type=F32
    )
    out_ref[0, :, :128] = (o / total).astype(BF)
    out_ref[0, :, 128:] = term_lanes(top + jnp.log(total), BLOCK)


def inner_kernel(dist_ref, qh_ref, qt_ref, kvh_ref, kvt_ref, out_ref, q_ref, kv_ref):
    head = kvh_ref.shape[1]

    @pl.when(pl.program_id(1) == 0)
    def _():
        q_ref[:head] = qh_ref[0]
        q_ref[head:] = qt_ref[0]
        kv_ref[:head] = kvh_ref[0]
        kv_ref[head:] = kvt_ref[0]

    def block(ref, c):
        return ref[pl.ds(pl.multiple_of(c * BLOCK, BLOCK), BLOCK), :]

    c = pl.program_id(1) + 2
    at = c - dist_ref[pl.program_id(0), c]
    attend_block(block(q_ref, c), block(kv_ref, c), block(kv_ref, at), out_ref)


def edge_kernel(dist_ref, q_ref, kv_ref, halo_ref, out_ref):
    c = pl.program_id(1)
    own = kv_ref[0, pl.ds(pl.multiple_of(c * BLOCK, BLOCK), BLOCK), :]
    at = c + 2 - dist_ref[pl.program_id(0), c]
    before = halo_ref[0, pl.ds(pl.multiple_of(jnp.minimum(at, 1) * BLOCK, BLOCK), BLOCK), :]
    behind = jnp.where(at < 2, before, kv_ref[0, :BLOCK, :])
    attend_block(q_ref[0], own, behind, out_ref)


def of_round(shape):
    return pl.BlockSpec((1,) + shape[1:], lambda r, b, d: (r, 0, 0))


def attend_inner(dist, q_head, q_tail, kv_head, kv_tail):
    rounds = q_head.shape[0]
    count = q_head.shape[1] + q_tail.shape[1]
    blocks = count // BLOCK - 2
    return pl.pallas_call(
        inner_kernel,
        grid_spec=pltpu.PrefetchScalarGridSpec(
            num_scalar_prefetch=1,
            grid=(rounds, blocks),
            in_specs=[of_round(v.shape) for v in (q_head, q_tail, kv_head, kv_tail)],
            out_specs=pl.BlockSpec((1, BLOCK, 256), lambda r, b, d: (r, b, 0)),
            scratch_shapes=[pltpu.VMEM((count, 128), BF), pltpu.VMEM((count, 256), BF)],
        ),
        out_shape=jax.ShapeDtypeStruct((rounds, blocks * BLOCK, 256), BF),
        compiler_params=params(2),
        name="attend_inner",
    )(dist, q_head, q_tail, kv_head, kv_tail)


def attend_edge(dist, q, kv, halo):
    rounds = q.shape[0]
    return pl.pallas_call(
        edge_kernel,
        grid_spec=pltpu.PrefetchScalarGridSpec(
            num_scalar_prefetch=1,
            grid=(rounds, 2),
            in_specs=[
                pl.BlockSpec((1, BLOCK, 128), lambda r, b, d: (r, b, 0)),
                of_round((rounds, 2 * BLOCK, 256)),
                of_round(halo.shape),
            ],
            out_specs=pl.BlockSpec((1, BLOCK, 256), lambda r, b, d: (r, b, 0)),
        ),
        out_shape=jax.ShapeDtypeStruct((rounds, 2 * BLOCK, 256), BF),
        compiler_params=params(2),
        name="attend_edge",
    )(dist, q, kv, halo)


def back_kernel(first_group, idx_ref, edge_ref, inner_ref, *out_refs):
    width, peers = out_refs[0].shape[-2] - 8, 16
    n = peers * width
    group = pl.program_id(1)
    idx = idx_ref[0] - (first_group + group) * n
    got = 0.0
    first = 0
    for ref in (edge_ref, inner_ref):
        count = ref.shape[1]
        place = lax.broadcasted_iota(jnp.int32, (n, count), 0)
        hot = one_hot(idx[:, first : first + count], place)
        got += jnp.dot(hot, ref[0], preferred_element_type=F32)
        first += count
    lines = terms_to_lines(got[:, 128:], n // 32).reshape(peers, width // 32, 1, 128)
    row = lax.broadcasted_iota(jnp.int32, (peers, 8, 128), 1)
    tail = jnp.zeros((peers, 8, 128), F32)
    for part in range(width // 32):
        tail = jnp.where(row == part, lines[:, part], tail)
    tail = tail.astype(BF)
    got = got[:, :128].astype(BF).reshape(peers, width, 128)

    def store(ref, at):
        ref[:, :width, :] = got[at]
        ref[:, width:, :] = tail[at]

    every, half = slice(None), peers // 2
    if len(out_refs) == 1:
        store(out_refs[0].at[:, 0, 0], every)
        return
    near_ref, low_ref, high_ref = out_refs

    @pl.when(group == 0)
    def _():
        store(near_ref.at[:, 0], every)

    @pl.when(group == 1)
    def _():
        store(low_ref.at[:, 0], slice(0, half))
        store(high_ref.at[:, 0], slice(half, peers))


def back_rows(idx, edge, inner, width, even):
    rounds = idx.shape[0]
    ext = width + 8
    if even:
        shapes = [(n, rounds, ext, 128) for n in (16, 8, 8)]
        specs = [pl.BlockSpec((v[0], 1, ext, 128), lambda r, g: (0, r, 0, 0)) for v in shapes]
    else:
        shapes = [(16, 2, rounds, ext, 128)]
        specs = [pl.BlockSpec((16, 1, 1, ext, 128), lambda r, g: (0, g, r, 0, 0))]
    one = lambda v: pl.BlockSpec((1,) + v.shape[1:], lambda r, g: (r, 0, 0))
    return pl.pallas_call(
        functools.partial(back_kernel, 0 if even else 2),
        grid=(rounds, 2),
        in_specs=[one(idx), one(edge), one(inner)],
        out_specs=specs,
        out_shape=[pltpu.HBM(v, BF) for v in shapes],
        compiler_params=params(2),
        name="back_rows",
    )(idx, edge, inner)


ABSENT = -1e30


def fill_home(x_ref, width, blocks):
    row = 0
    for block in blocks:
        size = block.shape[0] * width
        x_ref[row : row + size, :128] = block[:, :width, :].reshape(size, 128)
        tail = block[:, width:, :].astype(F32)
        lines = jnp.concatenate(
            [tail[:, p : p + 1][:, None] for p in range(width // 32)], axis=1
        ).reshape(size // 32, 1, 128)
        x_ref[row : row + size, 128:] = lines_to_terms(lines).astype(BF)
        row += size


def gather_home(own_ref, cols, x_ref, width):
    near, far = 0.0, 0.0
    size = 16 * width
    place = lax.broadcasted_iota(jnp.int32, (cols.shape[0], size), 1)
    for g in range(4):
        hot = one_hot(cols[:, g : g + 1], place)
        got = jnp.dot(hot, x_ref[g * size : (g + 1) * size], preferred_element_type=F32)
        if g == 0:
            near = got
        else:
            mine = own_ref[g] == 1
            near += jnp.where(mine, got, 0.0)
            far += jnp.where(mine, 0.0, got)
    return [near, far]


def home_kernel(width, own_ref, idx_ref, even_ref, up_ref, down_ref, out_ref, x_ref):
    rounds = even_ref.shape[2]

    @pl.when(pl.program_id(0) == 0)
    def _():
        for r in range(rounds):
            blocks = [even_ref.at[:, 0, r], even_ref.at[:, 1, r], up_ref.at[:, r], down_ref.at[:, r]]
            fill_home(x_ref.at[r], width, blocks)

    step = idx_ref.shape[2]
    cols = jnp.transpose(idx_ref[0])
    states = []
    for r in range(rounds):
        states += gather_home(own_ref, cols[:, 4 * r : 4 * r + 4], x_ref.at[r], width)
    here = [s[:, 131:132] > 0.5 for s in states]
    logs = [
        jnp.where(h, s[:, 128:129] + s[:, 129:130] + s[:, 130:131], ABSENT)
        for h, s in zip(here, states)
    ]
    top = functools.reduce(jnp.maximum, logs)
    scales = [jnp.where(h, jnp.exp(v - top), 0.0) for h, v in zip(here, logs)]
    total = sum(scales)
    some = total > 0.0
    summed = sum(s * p[:, :128] for s, p in zip(scales, states))
    safe = jnp.where(some, total, 1.0)
    log = jnp.where(some, top + jnp.log(safe), ABSENT)
    mean = (summed / safe).astype(BF)
    terms = term_lanes(log, step).astype(F32)
    lines = terms_to_lines(terms, step // 32).reshape(step // 32, 128).astype(BF)
    part = step // out_ref.shape[0]
    for q in range(out_ref.shape[0]):
        out_ref[q, :part, :] = mean[q * part : (q + 1) * part]
        out_ref[q, part:, :] = lines[q * part // 32 : (q + 1) * part // 32]


def home_rows(own, idx, even, up, down, width):
    rounds, groups, count = idx.shape
    quarters, steps = 4, 2
    step = count // steps
    part = count // quarters
    columns = rounds * groups
    idx = idx.reshape(columns, steps, step).transpose(1, 0, 2)
    return pl.pallas_call(
        functools.partial(home_kernel, width),
        grid_spec=pltpu.PrefetchScalarGridSpec(
            num_scalar_prefetch=1,
            grid=(steps,),
            in_specs=[pl.BlockSpec((1, columns, step), lambda i, o: (i, 0, 0))]
            + [whole(v.shape) for v in (even, up, down)],
            out_specs=pl.BlockSpec((quarters // steps, part + part // 32, 128), lambda i, o: (i, 0, 0)),
            scratch_shapes=[pltpu.VMEM((rounds, 64 * width, 256), BF)],
        ),
        out_shape=jax.ShapeDtypeStruct((quarters, part + part // 32, 128), BF),
        compiler_params=params(),
        name="home_rows",
    )(own, idx, even, up, down)


def finish_kernel(m_ref, w_ref, out_ref):
    rows = out_ref.shape[0]
    logs = []
    for i in range(4):
        line = m_ref[i, rows:, :].astype(F32).reshape(rows // 32, 1, 128)
        terms = lines_to_terms(line)
        logs.append(terms[:, 0:1] + terms[:, 1:2] + terms[:, 2:3])
    top = functools.reduce(jnp.maximum, logs)
    scales = [jnp.exp(v - top) for v in logs]
    total = sum(scales)
    summed = sum(s * m_ref[i, :rows, :].astype(F32) for i, s in enumerate(scales))
    blended = (summed / total).astype(BF)
    out_ref[...] = jnp.dot(blended, w_ref[...], preferred_element_type=F32).astype(BF)


def finish(merged, w_out):
    parts, rows, _ = merged.shape
    rows -= rows // 33
    return pl.pallas_call(
        finish_kernel,
        in_specs=[whole(merged.shape), whole(w_out.shape)],
        out_specs=whole((rows, w_out.shape[1])),
        grid=(1,),
        out_shape=jax.ShapeDtypeStruct((rows, w_out.shape[1]), BF),
        compiler_params=params(),
        name="finish",
    )(merged, w_out)


def send_places(own_slots, other_slots, width):
    zl, zh = lax.axis_index("zl"), lax.axis_index("zh")
    late = lax.axis_index(PLANE) >= 8
    group = jnp.arange(4, dtype=jnp.int32)
    shift = jnp.where(group == 0, 0, jnp.where(group == 1, jnp.where(late, -2, 2), 5 - 2 * group))
    own = ((zh * 4 + zl + shift + 8) & 7) // 4 == zh
    slot = jnp.where(own[:, None], own_slots[:, None], other_slots[:, None])
    hit = (slot >> 10) == ((zl + shift + 8) & 3)[:, None]
    return jnp.where(hit, ((slot >> 6) & 15) * width + (slot & 63), -1), own.astype(jnp.int32)


def take_places(taken, width):
    away = (lax.axis_index("zl") - (taken >> 10)) & 3
    group = jnp.where(away == 1, 2, jnp.where(away == 2, 1, away))
    source = (taken >> 6) & 15
    at = taken & 63
    by_group = (group * 16 + source) * width + at
    odd = (32 + source * 2 + group - 2) * width + at
    return jnp.where(group < 2, by_group, odd), by_group


def body(x, w_qk, w_v, w_out, slots, taken, looks):
    count = slots.shape[1]
    peers = lax.axis_size(SEQ)
    width = 2 * count // peers
    blocks = count // BLOCK
    tail = count - 2 * BLOCK
    others = lax.ppermute(slots, "zh", [(0, 1), (1, 0)])
    packed = project(x, w_qk, w_v)
    mine = lax.axis_index(SEQ) * blocks + jnp.arange(blocks, dtype=jnp.int32)
    dist = (mine[None, :] - looks) % (peers * blocks)
    next_device = [(i, (i + 1) % peers) for i in range(peers)]
    sent, own = send_places(slots, others, width)
    spots, groups = take_places(taken, width)

    (even,) = scatter_rows(sent[:, :2], packed, width, True)
    even, packed = together((even, packed))
    half = plane(even)
    up, down = scatter_rows(sent[:, 2:], packed, width, False)
    up, down = ring(up, 1), ring(down, -1)
    low, high, up, down = together((half[:8, 1], half[8:, 1], up, down))
    low, high = ring(low, 2), ring(high, -2)
    odd = plane(join(up, down))
    early = near_rows(spots, half)
    early, low, high, odd = together((early, low, high, odd))

    q_tail, kv_tail = sort_rows(spots[:, tail:], early, low, high, odd, tail, 2 * BLOCK)
    halo = lax.ppermute(kv_tail, SEQ, next_device)
    q_head, kv_head = sort_rows(spots[:, :tail], early, low, high, odd, 0, 3 * BLOCK)
    inner = attend_inner(dist, q_head, q_tail, kv_head, kv_tail)
    edge = attend_edge(dist, q_head, kv_head, halo)

    (odd,) = back_rows(groups[:, None], edge, inner, width, False)
    odd, edge = together((odd, edge))
    half = plane(odd)
    near, low, high = back_rows(groups[:, None], edge, inner, width, True)
    low, high = ring(low, -2), ring(high, 2)
    up, down, low, high = together((half[:, 0], half[:, 1], low, high))
    up, down = ring(up, -1), ring(down, 1)
    even = plane(join(near, jnp.concatenate([low, high])))
    state = home_rows(own, sent, even, up, down, width)
    merged = lax.all_to_all(state, ROUND, 0, 0, tiled=True)
    return finish(merged, w_out)


def solution(mesh):
    fine = Mesh(mesh.devices.reshape(4, 4, 4, 2, 2), SEQ + ROUND)
    in_specs = (P(SEQ, None), P(), P(), P()) + (P(ROUND, SEQ),) * 3
    return jax.shard_map(
        body, mesh=fine, in_specs=in_specs, out_specs=P(SEQ + ROUND, None), check_vma=False
    )
```
